32 devices in a mesh: dp: 8 (over z, y), chan: 4 (over x, core).
Axes of the slice: x: 2, y: 2, z: 4, core: 2. Of those that a mesh axis runs over, the one named last changes fastest.
Arguments:
- tokens: bfloat16 [640, 65536], P('chan', 'dp'), may hold values from -6 to 6
- weights: bfloat16 [3, 640, 1280], P(None, 'chan', 'dp'), may hold values from -0.15625 to 0.15625
- bias: float32 [3, 640], P(None, 'chan'), may hold values from -3 to 8
- segment_ids: int32 [65536], P('dp'), may hold values from 0 to 191, never falling along the last dimension, each value on 1 to 1024 neighbouring positions
- cotangent: bfloat16 [640, 65536], P('chan', 'dp'), may hold values from -6 to 6
Outputs:
- hidden: bfloat16 [640, 65536], P('chan', 'dp')
- input_grad: bfloat16 [640, 65536], P('chan', 'dp')
- weight_grad: float32 [3, 640, 1280], P(None, 'chan', 'dp')
- bias_grad: float32 [3, 640], P(None, 'chan')
The draws below stay inside these ranges and needn't reach their ends.
All inputs are finite; a program needn't handle non-finite values.
Results may differ from the reference program's by a relative error of at most 0.0051.
Values may be sent and summed in bfloat16 or wider, within the bound.
No kernel may reach another device: no remote copies, remote signals or barrier semaphores. Data moves between devices by JAX's collectives and lax.ppermute only.
A program may use at most 320 MiB of HBM per device.

```python
import math
import jax
import jax.numpy as jnp
import numpy as np
from jax import lax

D = 640
LEN = 1024
TOKENS = 65536


def draw_bias(key, part):
    first = jax.random.fold_in(key, 11)
    third = jax.random.fold_in(key, 37)
    outer = jnp.clip(0.7 * jax.random.normal(first, (2, D), jnp.float32), -3.0, 3.0)
    middle = jax.random.uniform(third, (D,), jnp.float32, 2.0, 7.5)
    return jnp.stack([outer[0], middle, outer[1]], 0).astype(jnp.float32)


def block_scale(key, extent, cuts, least, largest):
    def one(dim, parts):
        steps = jax.random.uniform(jax.random.fold_in(jax.random.fold_in(key, 6), dim), (parts,), jnp.float32, least / len(cuts), largest / len(cuts))
        return jnp.repeat(jnp.exp(steps), extent[dim] // parts).reshape((-1,) + (1,) * (len(extent) - dim - 1))

    gain = one(*cuts[0])
    for cut in cuts[1:]:
        gain = gain * one(*cut)
    return gain


def length_profile(count, total, bound, lean):
    loads = [(1 << 20) // math.isqrt(grade ** lean) + 1 for grade in range(2, count + 1)]
    rest, holding = total - bound - (count - 1), [1] * (count - 1)
    while rest > 0:
        movable = [i for i in range(count - 1) if holding[i] < bound]
        pool, budget = sum([loads[i] for i in movable]), rest
        for i in movable:
            more = min(bound - holding[i], max(1, budget * loads[i] // pool), rest)
            holding[i] = holding[i] + more
            rest = rest - more
    return np.array([bound] + holding)


def ragged_sizes(own_key, count, total, limit, skew):
    if count == 2:
        one = jax.random.randint(own_key, (), max(1, total - limit), min(limit, total - 1) + 1)
        return jnp.stack([one, total - one])
    tallies = jnp.asarray(length_profile(count, total, limit, skew), jnp.int32)
    pairs = (count - 1) // 2
    giver, receiver = tallies[1:1 + 2 * pairs:2], tallies[2:2 + 2 * pairs:2]
    room = jnp.minimum(giver - 1, limit - receiver)
    moved = jax.random.randint(jax.random.fold_in(own_key, 1), (pairs,), 0, 1 << 20) % (room + 1)
    tallies = tallies.at[1:1 + 2 * pairs:2].set(giver - moved).at[2:2 + 2 * pairs:2].set(receiver + moved)
    return tallies[jax.random.permutation(jax.random.fold_in(own_key, 2), count)]


def scatter_about(stream_key, dims, spread, limit, cuts=(), dtype=jnp.bfloat16):
    array = spread * jax.random.normal(stream_key, dims, jnp.float32)
    if cuts:
        array = array * block_scale(stream_key, dims, cuts, -0.22, 0.18)
    return jnp.clip(array, -limit, limit).astype(dtype)


def setup_inputs(seed: int = 0) -> dict:
    key_list = jax.random.split(jax.random.key(seed), 6)
    tokens = scatter_about(key_list[0], (D, TOKENS), 1.0, 6.0, ((0, 4), (1, 8)))
    weights = scatter_about(key_list[1], (3, D, 2 * D), (2 * D) ** -0.5, 0.15625, ((1, 4), (2, 8)))
    bias = draw_bias(jax.random.fold_in(key_list[5], 71), 0)
    segment_ids = jnp.searchsorted(jnp.cumsum(ragged_sizes(key_list[3], TOKENS * 3 // LEN, TOKENS, LEN, 2)), jnp.arange(TOKENS), side="right").astype(jnp.int32)
    cotangent = scatter_about(key_list[4], (D, TOKENS), 1.0, 6.0, ((0, 4), (1, 8)))
    return dict(tokens=tokens, weights=weights, bias=bias, segment_ids=segment_ids, cotangent=cotangent)


@jax.custom_vjp
def low(v):
    return lax.optimization_barrier(v.astype(jnp.bfloat16)).astype(jnp.float32)

@jax.custom_vjp
def low_back(v):
    return v

def low_keep(v):
    return (low(v), None)

def low_pass(kept, grad):
    return (grad,)

def back_keep(v):
    return (v, None)

def back_low(kept, grad):
    return (low(grad),)
low.defvjp(low_keep, low_pass)
low_back.defvjp(back_keep, back_low)

def layer_forward(inputs, stacked_weight, stacked_bias, carry_on):
    shifted = jnp.concatenate([jnp.zeros((1, inputs.shape[1]), jnp.float32), inputs[:-1]], 0)
    previous = shifted * carry_on[:, None]
    joined_inputs = jnp.concatenate([inputs, previous], 1)
    preactivation = jnp.einsum('kj,aej->ake', joined_inputs, stacked_weight, precision=lax.Precision.HIGHEST) + stacked_bias[:, None, :]
    preactivation = low_back(preactivation)
    gate_z = jnp.tanh(preactivation[0])
    forget = jax.nn.sigmoid(preactivation[1])
    output_gate = jax.nn.sigmoid(preactivation[2])
    decay = forget * carry_on[:, None]
    source = (1.0 - forget) * gate_z

    def advance(cell, item):
        cell = item[0] * cell + item[1]
        return (cell, cell)
    start = jnp.zeros((inputs.shape[1],), jnp.float32)
    final, cells = lax.scan(advance, start, (decay, source))
    return output_gate * cells

def reference(tokens, weights, bias, segment_ids, cotangent):
    count = TOKENS // LEN
    stacked_weight = weights.astype(jnp.float32)
    sequence_tokens = tokens.T.reshape(count, LEN, D)
    seq_ids = segment_ids.reshape(count, LEN)
    seq_cot = cotangent.T.reshape(count, LEN, D)
    position = jnp.arange(LEN)

    def one_row(totals, item):
        inputs, ids, cot = item
        before = jnp.concatenate([ids[:1], ids[:-1]], 0)
        carry_on = jnp.where((position > 0) & (ids == before), 1.0, 0.0).astype(jnp.float32)
        func = jax.checkpoint(lambda xx, ww, bb: layer_forward(xx, ww, bb, carry_on))
        layer_output, pull = jax.vjp(func, inputs.astype(jnp.float32), stacked_weight, bias)
        incoming_gradient, grad_w, grad_b = pull(cot.astype(jnp.float32))
        return ((totals[0] + grad_w, totals[1] + grad_b), (layer_output.astype(jnp.bfloat16), incoming_gradient.astype(jnp.bfloat16)))
    init = (jnp.zeros((3, D, 2 * D), jnp.float32), jnp.zeros((3, D), jnp.float32))
    totals, outputs = lax.scan(one_row, init, (sequence_tokens, seq_ids, seq_cot))
    hidden = outputs[0].reshape(TOKENS, D).T
    input_grad = outputs[1].reshape(TOKENS, D).T
    return (hidden, input_grad, totals[0], totals[1])
```

```python
import functools

import jax
import jax.numpy as jnp
from jax import lax
from jax.experimental import pallas as pl
from jax.experimental.pallas import tpu as pltpu
from jax.sharding import PartitionSpec as P

LEN = 1024
MICRO = 4
LANES = 128
SEGS = 8
PAD = 8
TILE = 256
UNROLL = 16
f32 = jnp.float32
bf16 = jnp.bfloat16
ANY = pl.BlockSpec(memory_space=pl.ANY)
VMEM = pl.BlockSpec(memory_space=pltpu.VMEM)
SMEM = pl.BlockSpec(memory_space=pltpu.SMEM)


def dot(a, b, ca, cb):
    return lax.dot_general(a, b, (((ca,), (cb,)), ((), ())), preferred_element_type=f32)


def sigmoid(v):
    return 0.5 * jnp.tanh(0.5 * v) + 0.5


def layer_kernel(k, first, last, parts, C, n, *refs):
    refs = list(refs)
    me_ref, tok, sib, px, pd, cot, scot, carry_l, carry_t, bias = refs[:10]
    refs = refs[10:]
    if first:
        w_in, refs = refs[: 2 * parts], refs[2 * parts :]
    else:
        w_in, acc_in, refs = refs[0], refs[1], refs[3:]
    hid, hid_sib, dx_own, dx_sib, dx_px, dx_pd, bsum = refs[:7]
    refs = refs[7:]
    if last:
        acc_own, acc_sib, refs = refs[0], refs[1], refs[2:]
    else:
        acc_out, refs = refs[0], refs[1:]
    if first:
        w_out, refs = refs[0], refs[1:]
    (xb, wb, cb, pre, zs, fs, os_, cbs, ct, hs, hb, dp, dxb, accb, ab, small, nxt, cl, ca_t, sem) = refs
    D = 4 * C
    tl = C - LANES
    steps = n // SEGS
    sp = steps + PAD
    me, row, place = me_ref[0], me_ref[1], me_ref[2]
    col = pl.multiple_of(row * n, n)
    half = 4 * LANES

    def go(src, dst, i):
        copy = pltpu.make_async_copy(src, dst, sem.at[i])
        copy.start()
        return copy

    def block(j):
        return pl.ds(pl.multiple_of((me ^ j) * C, 32), C)

    def nat(o, h):
        return pl.ds(pl.multiple_of((o // steps + h) * sp, 8), steps)

    here = pl.ds(col, n)
    x_copies = [
        go(px, xb.at[block(2), :], 2),
        go(pd, xb.at[block(3), :], 3),
        go(tok.at[:, here], xb.at[block(0), :], 0),
        go(sib.at[:, here], xb.at[block(1), :], 1),
        go(carry_l.at[k], cl, 10),
    ]
    if first:
        w_copies = []
        for j in range(parts):
            at = pl.ds(pl.multiple_of((place ^ j) * C, 32), C)
            w_copies.append(go(w_in[j], wb.at[at, 0:half], 12 + j))
            w_copies.append(go(w_in[parts + j], wb.at[at, half : 2 * half], 12 + parts + j))
    else:
        w_copies = [go(w_in, wb, 4)]
    c_copies = [
        go(cot.at[0:LANES, here], cb.at[0:LANES], 5),
        go(scot.at[0:LANES, here], cb.at[LANES : 2 * LANES], 6),
        go(cot.at[LANES:C, here], cb.at[2 * LANES : 2 * LANES + tl], 7),
        go(scot.at[LANES:C, here], cb.at[2 * LANES + tl : 2 * LANES + 2 * tl], 8),
        go(carry_t.at[k], ca_t, 11),
    ]
    for copy in x_copies:
        copy.wait()
    mask = cl[0:1, :]
    rb = 32

    def prev_step(i, _):
        o = pl.multiple_of(i * rb, rb)
        v = xb[pl.ds(o, rb), :].astype(f32)
        xb[pl.ds(D + o, rb), :] = (pltpu.roll(v, 1, 1) * mask).astype(bf16)
        return 0

    lax.fori_loop(0, D // rb, prev_step, 0, unroll=2)
    for copy in w_copies:
        copy.wait()
    if first:
        w_save = go(wb, w_out, 4)
    else:
        acc_copy = go(acc_in, accb, 9)

    def forward_step(i, _):
        o = pl.multiple_of(i * TILE, TILE)
        v = dot(xb[:, pl.ds(o, TILE)], wb[...], 0, 0)
        for q in range(8):
            for h in range(TILE // steps):
                pre[q, nat(o, h), :] = v[h * steps : (h + 1) * steps, q * LANES : (q + 1) * LANES]
        return 0

    lax.fori_loop(0, n // TILE, forward_step, 0)
    for copy in c_copies:
        copy.wait()

    def cot_step(i, _):
        o = pl.multiple_of(i * TILE, TILE)
        v = cb[:, pl.ds(o, TILE)].astype(f32).T
        for q in range(3):
            for h in range(TILE // steps):
                ct[q, nat(o, h), :] = v[h * steps : (h + 1) * steps, q * LANES : (q + 1) * LANES]
        return 0

    lax.fori_loop(0, n // TILE, cot_step, 0)
    lane = lax.broadcasted_iota(jnp.int32, (SEGS, LANES), 1)
    b_all = bias[...]
    b = [jnp.broadcast_to(b_all[:, q * LANES : (q + 1) * LANES], (SEGS, LANES)) for q in range(8)]
    cols = [slice(q * LANES, (q + 1) * LANES) for q in range(3)]
    one = jnp.ones((SEGS, LANES), f32)
    zero = jnp.zeros((SEGS, LANES), f32)

    def strided(ref, t, q):
        return ref[q, pl.ds(t, SEGS, stride=sp), :]

    def now(t):
        return pl.ds(pl.multiple_of(t * SEGS, SEGS), SEGS)

    def gates_step(t, state):
        gain, total = state
        v = [strided(pre, t, q) + b[q] for q in range(8)]
        u, w = v[3], v[7]
        tz = jnp.where(lane < tl, u, pltpu.roll(w, tl, 1))
        tf = jnp.where(lane < tl, pltpu.roll(u, LANES - tl, 1), w)
        to = jnp.where(lane < tl, pltpu.roll(u, LANES - 2 * tl, 1), pltpu.roll(w, LANES - tl, 1))
        z = [jnp.tanh(g) for g in (v[0], v[4], tz)]
        f = [sigmoid(g) for g in (v[1], v[5], tf)]
        o = [sigmoid(g) for g in (v[2], v[6], to)]
        r = now(t)
        ca = ca_t[r, :]
        gains, totals = [], []
        for q in range(3):
            zs[r, cols[q]] = z[q]
            fs[r, cols[q]] = f[q]
            os_[r, cols[q]] = o[q]
            gains.append(gain[q] * (f[q] * ca))
            totals.append(z[q] + f[q] * (ca * total[q] - z[q]))
        return tuple(gains), tuple(totals)

    gain, total = lax.fori_loop(0, steps, gates_step, ((one,) * 3, (zero,) * 3), unroll=UNROLL)
    for q in range(3):
        small[0, :, cols[q]] = gain[q]
        small[1, :, cols[q]] = total[q]
    run = jnp.zeros((1, 3 * LANES), f32)
    for s in range(SEGS):
        small[2, s : s + 1, :] = run
        run = small[0, s : s + 1, :] * run + small[1, s : s + 1, :]
    cell = tuple(small[2, :, cols[q]] for q in range(3))

    def cell_step(t, state):
        cell, back, gain = state
        r = now(t)
        ca = ca_t[r, :]
        cells, backs, gains = [], [], []
        for q in range(3):
            z, f, o = zs[r, cols[q]], fs[r, cols[q]], os_[r, cols[q]]
            prev = ca * cell[q]
            cbs[r, cols[q]] = prev
            new = z + f * (prev - z)
            hs[q, pl.ds(t, SEGS, stride=sp), :] = o * new
            g = jnp.where(t == 0, one, gain[q] * (f * ca))
            cells.append(new)
            gains.append(g)
            backs.append(back[q] + g * (strided(ct, t, q) * o))
        return tuple(cells), tuple(backs), tuple(gains)

    cell, back, gain = lax.fori_loop(0, steps, cell_step, (cell, (zero,) * 3, (one,) * 3), unroll=UNROLL)
    for q in range(3):
        small[0, :, cols[q]] = back[q]
        small[1, :, cols[q]] = gain[q]
        small[3, :, cols[q]] = fs[0:SEGS, cols[q]] * ca_t[0:SEGS, :]
    run = jnp.zeros((1, 3 * LANES), f32)
    for s in range(SEGS - 1, -1, -1):
        small[2, s : s + 1, :] = run
        run = small[3, s : s + 1, :] * (small[0, s : s + 1, :] + small[1, s : s + 1, :] * run)
    later = tuple(small[2, :, cols[q]] for q in range(3))

    def hidden_step(i, _):
        o = pl.multiple_of(i * TILE, TILE)
        for q in range(3):
            e = LANES if q < 2 else 2 * tl
            for h in range(TILE // steps):
                v = hs[q, nat(o, h), :].T.astype(bf16)
                hb[q * LANES : q * LANES + e, pl.ds(pl.multiple_of(o + h * steps, LANES), steps)] = v[0:e]
        return 0

    lax.fori_loop(0, n // TILE, hidden_step, 0)
    out_copies = [
        go(hb.at[0:LANES], hid.at[0:LANES, here], 5),
        go(hb.at[LANES : 2 * LANES], hid_sib.at[0:LANES], 6),
        go(hb.at[2 * LANES : 2 * LANES + tl], hid.at[LANES:C, here], 7),
        go(hb.at[2 * LANES + tl : 2 * LANES + 2 * tl], hid_sib.at[LANES:C], 8),
    ]

    def grad_step(i, later):
        t = steps - 1 - i
        r = now(t)
        ca = ca_t[r, :]
        gz, gf, go_, laters = [], [], [], []
        for q in range(3):
            z, f, o, prev = zs[r, cols[q]], fs[r, cols[q]], os_[r, cols[q]], cbs[r, cols[q]]
            c = strided(ct, t, q)
            dc = c * o + later[q]
            laters.append((f * ca) * dc)
            d = prev - z
            u = dc * (1.0 - f)
            gz.append(u * (1.0 - z * z))
            gf.append(u * (f * d))
            go_.append(c * (z + f * d) * (o * (1.0 - o)))
        z, f, o = gz[2], gf[2], go_[2]
        u = jnp.where(
            lane < tl,
            z,
            jnp.where(
                lane < 2 * tl,
                pltpu.roll(f, tl, 1),
                jnp.where(lane < 3 * tl, pltpu.roll(o, 2 * tl, 1), 0.0),
            ),
        )
        w = jnp.where(
            lane < tl,
            pltpu.roll(z, LANES - tl, 1),
            jnp.where(lane < 2 * tl, f, jnp.where(lane < 3 * tl, pltpu.roll(o, tl, 1), 0.0)),
        )
        for q, v in enumerate((gz[0], gf[0], go_[0], u, gz[1], gf[1], go_[1], w)):
            pre[q, pl.ds(t, SEGS, stride=sp), :] = v
        return tuple(laters)

    lax.fori_loop(0, steps, grad_step, later, unroll=UNROLL)
    ck = 64

    def cast_step(i, sums):
        o = pl.multiple_of(i * ck, ck)
        at = pl.ds(pl.multiple_of(o // steps * sp + o % steps, 8), ck)
        out = []
        for q in range(8):
            v = pre[q, at, :].astype(bf16)
            dp[pl.ds(o, ck), q * LANES : (q + 1) * LANES] = v
            w = v.astype(f32)
            a = sums[q]
            for h in range(ck // SEGS):
                a = a + w[h * SEGS : (h + 1) * SEGS]
            out.append(a)
        return tuple(out)

    sums = lax.fori_loop(0, n // ck, cast_step, (zero,) * 8)
    for q in range(8):
        bsum[:, q * LANES : (q + 1) * LANES] = sums[q]
    if not first:
        acc_copy.wait()

    def weight_step(j, _):
        o = pl.multiple_of(j * TILE, TILE)
        v = dot(xb[...], dp[:, pl.ds(o, TILE)], 1, 0)
        if not first:
            v = v + accb[:, pl.ds(o, TILE)]
        accb[:, pl.ds(o, TILE)] = v
        return 0

    def weight_sib_step(j, _):
        o = pl.multiple_of(j * TILE, TILE)
        v = dot(xb[...], dp[:, pl.ds(half + o, TILE)], 1, 0)
        if not first:
            v = v + accb[:, pl.ds(half + o, TILE)]
        ab[:, pl.ds(o, TILE)] = v.astype(bf16)
        return 0

    if last:
        lax.fori_loop(0, half // TILE, weight_sib_step, 0)
        out_copies.append(go(ab, acc_sib, 10))
        lax.fori_loop(0, half // TILE, weight_step, 0)
        out_copies.append(go(accb.at[:, 0:half], acc_own, 9))
    else:
        lax.fori_loop(0, 2 * half // TILE, weight_step, 0)
        out_copies.append(go(accb, acc_out, 9))
    nxt[...] = jnp.zeros_like(nxt)
    lane2 = lax.broadcasted_iota(jnp.int32, (D, LANES), 1)

    def input_step(i, _):
        o = pl.multiple_of((n // TILE - 1 - i) * TILE, TILE)
        dj = dot(wb[...], dp[pl.ds(o, TILE), :], 1, 1)
        rolled = [
            pltpu.roll(
                dj[D:, h * LANES : (h + 1) * LANES] * cl[0:1, pl.ds(o + h * LANES, LANES)], LANES - 1, 1
            )
            for h in range(2)
        ]
        after = nxt[...]
        nxt[...] = rolled[0]
        edge = lane2 == LANES - 1
        dxb[:, pl.ds(o, LANES)] = (dj[:D, 0:LANES] + jnp.where(edge, rolled[1], rolled[0])).astype(bf16)
        dxb[:, pl.ds(o + LANES, LANES)] = (
            dj[:D, LANES : 2 * LANES] + jnp.where(edge, after, rolled[1])
        ).astype(bf16)
        return 0

    lax.fori_loop(0, n // TILE, input_step, 0)
    for j, out in enumerate((dx_own, dx_sib, dx_px, dx_pd)):
        out_copies.append(go(dxb.at[block(j), :], out, j))
    if first:
        out_copies.append(w_save)
    for copy in out_copies:
        copy.wait()


def layer(k, first, last, parts, C, n, total, scal, tok, sib, px, pd, cot, scot, carry_l, carry_t, bias, w, acc, hid):
    D = 4 * C
    N = 8 * LANES
    shape = jax.ShapeDtypeStruct
    ins = [scal, tok, sib, px, pd, cot, scot, carry_l, carry_t, bias]
    specs = [SMEM] + [ANY] * 8 + [VMEM]
    alias = {}
    piece = shape((C, n), bf16)
    outs = [shape((C, total), bf16)] + [piece] * 5 + [shape((SEGS, N), f32)]
    out_specs = [ANY] * 6 + [VMEM]
    if first:
        ins += list(w)
        specs += [ANY] * len(w)
    else:
        ins += [w, acc, hid]
        specs += [ANY] * 3
        alias = {12: 0}
        if not last:
            alias[11] = 7
    if last:
        outs += [shape((2 * D, N // 2), f32), shape((2 * D, N // 2), bf16)]
        out_specs += [ANY] * 2
    else:
        outs += [shape((2 * D, N), f32)]
        out_specs += [ANY]
    if first:
        outs += [shape((2 * D, N), bf16)]
        out_specs += [ANY]
    w3 = 3 * LANES
    tall = n + SEGS * PAD
    scratch = (
        [
            pltpu.VMEM((2 * D, n), bf16),
            pltpu.VMEM((2 * D, N), bf16),
            pltpu.VMEM((w3, n), bf16),
            pltpu.VMEM((8, tall, LANES), f32),
        ]
        + [pltpu.VMEM((n, w3), f32)] * 4
        + [pltpu.VMEM((3, tall, LANES), f32)] * 2
        + [
            pltpu.VMEM((2 * C, n), bf16),
            pltpu.VMEM((n, N), bf16),
            pltpu.VMEM((D, n), bf16),
            pltpu.VMEM((2 * D, N), f32),
            pltpu.VMEM((2 * D, N // 2), bf16),
            pltpu.VMEM((4, SEGS, w3), f32),
            pltpu.VMEM((D, LANES), f32),
            pltpu.VMEM((SEGS, n), f32),
            pltpu.VMEM((n, LANES), f32),
            pltpu.SemaphoreType.DMA((12 + 2 * parts,)),
        ]
    )
    return pl.pallas_call(
        functools.partial(layer_kernel, k, first, last, parts, C, n),
        out_shape=outs,
        in_specs=specs,
        out_specs=out_specs,
        scratch_shapes=scratch,
        input_output_aliases=alias,
        compiler_params=pltpu.CompilerParams(vmem_limit_bytes=58 << 20),
        cost_estimate=pl.CostEstimate(
            flops=12 * D * N * n, bytes_accessed=24 << 20, transcendentals=9 * n * LANES
        ),
        name="layer",
    )(*ins)


def finish_kernel(n, me_ref, own, px, sib, pd, *refs):
    out, a, b, sem = refs[-4:]
    here = pl.ds(pl.multiple_of(me_ref[1] * n, n), n)
    there = pl.ds(pl.multiple_of(me_ref[3] * n, n), n)
    a[...] = (own[...].astype(f32) + px[...].astype(f32)).astype(bf16)
    first = pltpu.make_async_copy(a, out.at[:, here], sem.at[0])
    first.start()
    b[...] = (sib[...].astype(f32) + pd[...].astype(f32)).astype(bf16)
    second = pltpu.make_async_copy(b, out.at[:, there], sem.at[1])
    second.start()
    first.wait()
    second.wait()


def finish(C, n, total, scal, own, px, sib, pd, grad):
    ins = [scal, own, px, sib, pd]
    specs = [SMEM] + [VMEM] * 4
    alias = {}
    if grad is not None:
        ins.append(grad)
        specs.append(ANY)
        alias = {5: 0}
    return pl.pallas_call(
        functools.partial(finish_kernel, n),
        out_shape=jax.ShapeDtypeStruct((C, total), bf16),
        in_specs=specs,
        out_specs=ANY,
        scratch_shapes=[pltpu.VMEM((C, n), bf16)] * 2 + [pltpu.SemaphoreType.DMA((2,))],
        input_output_aliases=alias,
        cost_estimate=pl.CostEstimate(flops=4 * C * n, bytes_accessed=12 * C * n, transcendentals=0),
        name="finish",
    )(*ins)


def place_kernel(n, rows_ref, *refs):
    out, sem = refs[-2:]
    pieces = refs[:-3]
    copies = []
    for k, piece in enumerate(pieces):
        there = pl.ds(pl.multiple_of(rows_ref[k] * n, n), n)
        copies.append(pltpu.make_async_copy(piece, out.at[:, there], sem.at[k]))
        copies[-1].start()
    for copy in copies:
        copy.wait()


def place(n, rows, pieces, hid):
    return pl.pallas_call(
        functools.partial(place_kernel, n),
        out_shape=jax.ShapeDtypeStruct(hid.shape, hid.dtype),
        in_specs=[SMEM] + [ANY] * (len(pieces) + 1),
        out_specs=ANY,
        scratch_shapes=[pltpu.SemaphoreType.DMA((len(pieces),))],
        input_output_aliases={1 + len(pieces): 0},
        cost_estimate=pl.CostEstimate(flops=0, bytes_accessed=4 * hid.size, transcendentals=0),
        name="place",
    )(rows, *pieces, hid)


def pack(w):
    tail = w.shape[1] - LANES
    rest = w.shape[2:]
    return jnp.concatenate(
        [
            w[:, :LANES].reshape((3 * LANES,) + rest),
            w[:, LANES:].reshape((3 * tail,) + rest),
            jnp.zeros((LANES - 3 * tail,) + rest, w.dtype),
        ],
        0,
    )


def unpack(w, C):
    tail = C - LANES
    rest = w.shape[1:]
    return jnp.concatenate(
        [
            w[: 3 * LANES].reshape((3, LANES) + rest),
            w[3 * LANES : 3 * LANES + 3 * tail].reshape((3, tail) + rest),
        ],
        1,
    )


def local(chan, parts, tokens, weights, bias, segment_ids, cotangent):
    C, total = tokens.shape
    n = LEN
    rows = total // n
    micros = rows // 2
    me = lax.axis_index("chan")
    place_dp = lax.axis_index("dp")
    core = me & 1

    def chan_move(v, j):
        return lax.ppermute(v, "chan", [(i, i ^ j) for i in range(chan)])

    def dp_move(v, j):
        return lax.ppermute(v, "dp", [(i, i ^ j) for i in range(parts)])

    px, pd = [], []
    for k in range(micros):
        mine = lax.dynamic_slice(tokens, (0, (2 * k + core) * n), (C, n))
        other = lax.dynamic_slice(tokens, (0, (2 * k + 1 - core) * n), (C, n))
        px.append(chan_move(mine, 2))
        pd.append(chan_move(other, 3))
    shard = pack(weights).T
    g = {0: shard}
    g[4] = dp_move(shard, 4)
    g[1] = dp_move(shard, 1)
    g[2] = dp_move(shard, 2)
    g[5] = dp_move(g[4], 1)
    g[6] = dp_move(g[4], 2)
    g[3] = dp_move(g[1], 2)
    g[7] = dp_move(g[6], 1)
    w = [g[j] for j in range(parts)] + [chan_move(g[j], 1) for j in range(parts)]
    b_own = pack(bias)[None, :]
    b_all = jnp.concatenate([b_own, chan_move(b_own, 1)], 1)
    sib = chan_move(tokens, 1)
    scot = chan_move(cotangent, 1)

    ids = segment_ids.reshape(rows, n)
    same = jnp.concatenate([jnp.zeros((rows, 1), jnp.bool_), ids[:, 1:] == ids[:, :-1]], 1)
    carry = jnp.where(same, 1.0, 0.0).astype(f32).reshape(micros, 2, n)
    carry = jnp.where(core == 0, carry[:, 0], carry[:, 1])
    carry_l = jnp.broadcast_to(carry[:, None, :], (micros, SEGS, n))
    carry_t = carry.reshape(micros, SEGS, n // SEGS).swapaxes(1, 2).reshape(micros, n, 1)
    carry_t = jnp.broadcast_to(carry_t, (micros, n, LANES))

    acc = hid = grad = None
    bias_sum = 0.0
    hid_parts, pending = [], []
    for k in range(micros):
        scal = jnp.stack([me, 2 * k + core, place_dp, 2 * k + 1 - core]).astype(jnp.int32)
        first, last = k == 0, k == micros - 1
        out = layer(
            k, first, last, parts, C, n, total, scal, tokens, sib, px[k], pd[k], cotangent, scot,
            carry_l, carry_t, b_all, w, acc, hid,
        )
        hid, hid_sib, own, d_sib, d_px, d_pd, bsum, acc = out[:8]
        if first:
            w = out[8]
        pending.append((scal, own, chan_move(d_px, 2), chan_move(d_sib, 1), chan_move(d_pd, 3)))
        hid_parts.append(chan_move(hid_sib, 1))
        bias_sum = bias_sum + bsum
        if last:
            acc_sib = out[8]
    for scal, own, r_px, r_sib, r_pd in pending:
        grad = finish(C, n, total, scal, own, r_px, r_sib, r_pd, grad)
    others = jnp.stack([2 * k + 1 - core for k in range(micros)]).astype(jnp.int32)
    hid = place(n, others, hid_parts, hid)

    half = 4 * LANES
    partial = (acc + chan_move(acc_sib, 1).astype(f32)).reshape(parts, C, half)

    def rows_of(j):
        return lax.dynamic_index_in_dim(partial, place_dp ^ j, 0, keepdims=False)

    def send(v, j):
        return dp_move(v.astype(bf16), j).astype(f32)

    r7 = send(rows_of(7), 1)
    r3 = send(rows_of(3), 2)
    r5 = send(rows_of(5), 1)
    r2 = send(rows_of(2), 2)
    r6 = send(rows_of(6) + r7, 2)
    r1 = send(rows_of(1) + r3, 1)
    r4 = send(rows_of(4) + r5 + r6, 4)
    shard_grad = rows_of(0) + r2 + r1 + r4
    weight_grad = unpack(shard_grad.T, C)

    bias_sum = jnp.sum(bias_sum, 0)
    b = bias_sum[:half] + chan_move(bias_sum[half:], 1)
    for j in (1, 2, 4):
        b = b + dp_move(b, j)
    bias_grad = unpack(b, C)
    return (hid, grad, weight_grad, bias_grad)


def combine(earlier, later):
    return (earlier[0] * later[0], later[0] * earlier[1] + later[1])


def local_any(tokens, weights, bias, segment_ids, cotangent):
    width_part, total_rows = tokens.shape
    batch_rows = total_rows // MICRO
    grad_shard = jnp.zeros(weights.shape, jnp.float32)
    bias_total = jnp.zeros(bias.shape, jnp.float32)
    position = jnp.arange(batch_rows) % LEN
    hidden_parts = []
    input_parts = []
    for micro in range(MICRO):
        lower = micro * batch_rows
        upper = lower + batch_rows
        part_in = tokens[:, lower:upper]
        ids = segment_ids[lower:upper]
        cot = cotangent[:, lower:upper].astype(jnp.float32)
        before = jnp.concatenate([ids[:1], ids[:-1]], 0)
        carry_flag = (position > 0) & (ids == before)
        carry_on = jnp.where(carry_flag, 1.0, 0.0).astype(jnp.float32)
        gathered = lax.all_gather(part_in, "chan", axis=0, tiled=True)
        width = gathered.shape[0]
        shifted = jnp.concatenate([jnp.zeros((width, 1), jnp.bfloat16), gathered[:, :-1]], 1)
        previous = jnp.where(carry_flag[None, :], shifted, jnp.zeros((), jnp.bfloat16))
        joined_inputs = jnp.concatenate([gathered, previous], 0)
        preactivation = jnp.einsum(
            "gcr,rl->gcl",
            lax.all_gather(weights, "dp", axis=2, tiled=True),
            joined_inputs,
            preferred_element_type=jnp.float32,
        )
        preactivation = preactivation + bias[:, :, None]
        gate_z = jnp.tanh(preactivation[0])
        forget = jax.nn.sigmoid(preactivation[1])
        output_gate = jax.nn.sigmoid(preactivation[2])
        decay = forget * carry_on[None, :]
        source = (1.0 - forget) * gate_z
        cell = lax.associative_scan(combine, (decay, source), axis=1)[1]
        hidden_parts.append((output_gate * cell).astype(jnp.bfloat16))
        decay_next = jnp.concatenate([decay[:, 1:], jnp.zeros((width_part, 1), jnp.float32)], 1)
        dcell = lax.associative_scan(combine, (decay_next, cot * output_gate), reverse=True, axis=1)[1]
        cell_before = (
            jnp.concatenate([jnp.zeros((width_part, 1), jnp.float32), cell[:, :-1]], 1)
            * carry_on[None, :]
        )
        grad_z = dcell * (1.0 - forget) * (1.0 - gate_z * gate_z)
        grad_f = dcell * (cell_before - gate_z) * forget * (1.0 - forget)
        grad_o = cot * cell * output_gate * (1.0 - output_gate)
        dpre_low = jnp.stack([grad_z, grad_f, grad_o], 0).astype(jnp.bfloat16)
        bias_total = bias_total + jnp.sum(dpre_low.astype(jnp.float32), axis=2)
        weight_term = jnp.einsum(
            "gcl,rl->gcr", dpre_low, joined_inputs, preferred_element_type=jnp.float32
        )
        djoined = jnp.einsum(
            "gcl,gcr->rl",
            dpre_low,
            lax.all_gather(weights, "dp", axis=2, tiled=True),
            preferred_element_type=jnp.float32,
        )
        later = djoined[width:] * carry_on[None, :]
        later = jnp.concatenate([later[:, 1:], jnp.zeros((width, 1), jnp.float32)], 1)
        term = djoined[:width] + later
        input_parts.append(
            lax.psum_scatter(term, "chan", scatter_dimension=0, tiled=True).astype(jnp.bfloat16)
        )
        grad_shard = grad_shard + lax.psum_scatter(weight_term, "dp", scatter_dimension=2, tiled=True)
    bias_grad = lax.psum(bias_total, "dp")
    hidden = jnp.concatenate(hidden_parts, 1)
    input_grad = jnp.concatenate(input_parts, 1)
    return (hidden, input_grad, grad_shard, bias_grad)


def solution(mesh):
    chan, parts = mesh.shape["chan"], mesh.shape["dp"]
    in_specs = (P("chan", "dp"), P(None, "chan", "dp"), P(None, "chan"), P("dp"), P("chan", "dp"))
    out_specs = (P("chan", "dp"), P("chan", "dp"), P(None, "chan", "dp"), P(None, "chan"))

    def run(tokens, weights, bias, segment_ids, cotangent):
        C = tokens.shape[0] // chan
        row_part = weights.shape[2] // parts
        pairs = tokens.shape[1] // parts % (2 * LEN) == 0
        tail = C - LANES
        fits = chan == 4 and parts == 8 and row_part == C and pairs and 0 < 3 * tail < LANES and tail % 32 == 0
        body = functools.partial(local, chan, parts) if fits else local_any
        return jax.shard_map(body, mesh=mesh, in_specs=in_specs, out_specs=out_specs, check_vma=False)(
            tokens, weights, bias, segment_ids, cotangent
        )

    return run
```

```python
import functools

import jax
import jax.numpy as jnp
from jax import lax
from jax.experimental import pallas as pl
from jax.experimental.pallas import tpu as pltpu
from jax.sharding import PartitionSpec as P

LEN = 1024
MICRO = 4
LANES = 128
SEGS = 8
PAD = 8
TILE = 256
UNROLL = 16
FTILE = 1024
CALLS = 2
EARLY = (0, 1, 2, 4)
LATE = (3, 5, 6, 7)
f32 = jnp.float32
bf16 = jnp.bfloat16
ANY = pl.BlockSpec(memory_space=pl.ANY)
VMEM = pl.BlockSpec(memory_space=pltpu.VMEM)
SMEM = pl.BlockSpec(memory_space=pltpu.SMEM)


def dot(a, b, ca, cb):
    return lax.dot_general(a, b, (((ca,), (cb,)), ((), ())), preferred_element_type=f32)


def sigmoid(v):
    return 0.5 * jnp.tanh(0.5 * v) + 0.5


def layer_kernel(k, calls, rows, parts, C, n, *refs):
    first, last = k == 0, k == calls - 1
    refs = list(refs)
    tok, sib, cot, scot, ids, bias, bias_sib, x_near, x_far = refs[:9]
    refs = refs[9:]
    if first:
        w_in, refs = refs[: parts + 1 + len(LATE)], refs[parts + 1 + len(LATE) :]
    else:
        w_in, acc_in, refs = refs[0], refs[1], refs[3:]
    hid, to_sib, dx_px, dx_pd, dx_own = refs[:5]
    refs = refs[5:]
    if last:
        acc_own, acc_sib, refs = refs[0], refs[1], refs[2:]
    else:
        acc_out, refs = refs[0], refs[1:]
    if first:
        w_out, refs = refs[0], refs[1:]
    (xb, wb, cb, pre, zs, fs, os_, cbs, ct, hs, hb, dp, dxb, accb, ab, small, nxt, sums, cl, ca_t, id_b, bb, sem, rsem) = refs
    D = 4 * C
    tl = C - LANES
    steps = n // SEGS
    sp = steps + PAD
    half = 4 * LANES
    me, place = lax.axis_index("chan"), lax.axis_index("dp")
    core = me & 1

    def go(src, dst, i):
        copy = pltpu.make_async_copy(src, dst, sem.at[i])
        copy.start()
        return copy

    def here(r):
        return pl.ds(pl.multiple_of((2 * (k * rows + r) + core) * n, n), n)

    def span(r):
        return pl.ds(pl.multiple_of(r * n, n), n)

    def block(j):
        return pl.ds(pl.multiple_of((me ^ j) * C, 32), C)

    def seg(h):
        return pl.ds(pl.multiple_of(h * sp, 8), steps)

    def id_rows(r):
        return pl.ds(pl.multiple_of((2 * (k * rows + r) + core) * SEGS, SEGS), SEGS)

    def x_copies(r):
        from_row = span(r)
        pairs = (
            (tok.at[:, here(r)], xb.at[block(0), span(r)]),
            (sib.at[:, here(r)], xb.at[block(1), span(r)]),
            (x_near.at[:, from_row], xb.at[block(2), span(r)]),
            (x_far.at[:, from_row], xb.at[block(3), span(r)]),
            (ids.at[id_rows(r)], id_b.at[r]),
        )
        return [pltpu.make_async_copy(a, b, rsem.at[r, i]) for i, (a, b) in enumerate(pairs)]

    def c_copies(r):
        pairs = (
            (cot.at[0:LANES, here(r)], cb.at[0:LANES, span(r)]),
            (scot.at[0:LANES, here(r)], cb.at[LANES : 2 * LANES, span(r)]),
            (cot.at[LANES:C, here(r)], cb.at[2 * LANES : 2 * LANES + tl, span(r)]),
            (scot.at[LANES:C, here(r)], cb.at[2 * LANES + tl : 2 * LANES + 2 * tl, span(r)]),
        )
        return [pltpu.make_async_copy(a, b, rsem.at[r, 5 + i]) for i, (a, b) in enumerate(pairs)]

    def hidden_copies(r):
        pairs = (
            (hb.at[0:LANES, span(r)], hid.at[0:LANES, here(r)]),
            (hb.at[LANES : 2 * LANES, span(r)], to_sib.at[C : C + LANES, span(r)]),
            (hb.at[2 * LANES : 2 * LANES + tl, span(r)], hid.at[LANES:C, here(r)]),
            (hb.at[2 * LANES + tl : 2 * LANES + 2 * tl, span(r)], to_sib.at[C + LANES : 2 * C, span(r)]),
        )
        return [pltpu.make_async_copy(a, b, rsem.at[r, 10 + i]) for i, (a, b) in enumerate(pairs)]

    def grad_copies(r):
        outs = (dx_own, to_sib.at[0:C], dx_px, dx_pd)
        return [
            pltpu.make_async_copy(dxb.at[block(j), span(r)], out.at[:, span(r)], rsem.at[r, 14 + j])
            for j, out in enumerate(outs)
        ]

    for copy in x_copies(0):
        copy.start()
    if first:
        w_copies = []
        for j in range(parts):
            at = pl.ds(pl.multiple_of((place ^ j) * C, 32), C)
            w_copies.append(go(w_in[j], wb.at[at, 0:half], 8 + j))
            if j in EARLY:
                other = w_in[parts].at[EARLY.index(j) * C : (EARLY.index(j) + 1) * C]
            else:
                other = w_in[parts + 1 + LATE.index(j)]
            w_copies.append(go(other, wb.at[at, half : 2 * half], 8 + parts + j))
    else:
        w_copies = [go(w_in, wb, 0)]
    b_copies = [go(bias, bb.at[:, 0:half], 1), go(bias_sib, bb.at[:, half : 2 * half], 3)]
    for copy in c_copies(0):
        copy.start()
    sums[...] = jnp.zeros_like(sums)
    lane = lax.broadcasted_iota(jnp.int32, (SEGS, LANES), 1)
    edge = lax.broadcasted_iota(jnp.int32, (D, LANES), 1) == LANES - 1
    cols = [slice(q * LANES, (q + 1) * LANES) for q in range(3)]
    one = jnp.ones((SEGS, LANES), f32)
    zero = jnp.zeros((SEGS, LANES), f32)

    def strided(ref, t, q):
        return ref[q, pl.ds(t, SEGS, stride=sp), :]

    def now(t):
        return pl.ds(pl.multiple_of(t * SEGS, SEGS), SEGS)

    def row(r, _):
        for copy in x_copies(r):
            copy.wait()
        seg_ids = id_b[r]
        before = pltpu.roll(seg_ids, 1, 1)
        before = jnp.where(lane == 0, pltpu.roll(before, 1, 0), before)
        sub = lax.broadcasted_iota(jnp.int32, (SEGS, steps), 0)
        carry = jnp.where((seg_ids == before) & ((lane > 0) | (sub > 0)), 1.0, 0.0).astype(f32)
        for s in range(SEGS):
            cl[:, s * steps : (s + 1) * steps] = jnp.broadcast_to(carry[s : s + 1, :], (SEGS, steps))
        for t in range(steps):
            ca_t[t * SEGS : (t + 1) * SEGS, :] = jnp.broadcast_to(carry[:, t : t + 1], (SEGS, LANES))
        rb = 32

        def prev_step(i, _):
            o = pl.multiple_of(i * rb, rb)
            v = xb[pl.ds(o, rb), span(r)].astype(f32)
            xb[pl.ds(D + o, rb), span(r)] = (pltpu.roll(v, 1, 1) * cl[0:1, :]).astype(bf16)
            return 0

        lax.fori_loop(0, D // rb, prev_step, 0)

        @pl.when(r == 0)
        def _():
            for copy in w_copies:
                copy.wait()
            for copy in b_copies:
                copy.wait()
            if first:
                go(wb, w_out, 0)
            else:
                go(acc_in, accb, 2)

        for copy in c_copies(r):
            copy.wait()

        @pl.when(r + 1 < rows)
        def _():
            for copy in x_copies(r + 1) + c_copies(r + 1):
                copy.start()

        b = [jnp.broadcast_to(bb[0:1, q * LANES : (q + 1) * LANES], (SEGS, LANES)) for q in range(8)]

        def forward_step(i, _):
            o = pl.multiple_of(r * n + i * FTILE, FTILE)
            v = dot(xb[:, pl.ds(o, FTILE)], wb[...], 0, 0)
            for h in range(FTILE // steps):
                at = seg(i * (FTILE // steps) + h)
                for q in range(8):
                    pre[q, at, :] = v[h * steps : (h + 1) * steps, q * LANES : (q + 1) * LANES]
                c = cb[:, pl.ds(pl.multiple_of(o + h * steps, LANES), steps)].astype(f32).T
                for q in range(3):
                    ct[q, at, :] = c[:, q * LANES : (q + 1) * LANES]
            return 0

        lax.fori_loop(0, n // FTILE, forward_step, 0)

        def gates_step(t, state):
            gain, total = state
            v = [strided(pre, t, q) + b[q] for q in range(8)]
            u, w = v[3], v[7]
            tz = jnp.where(lane < tl, u, pltpu.roll(w, tl, 1))
            tf = jnp.where(lane < tl, pltpu.roll(u, LANES - tl, 1), w)
            to = jnp.where(lane < tl, pltpu.roll(u, LANES - 2 * tl, 1), pltpu.roll(w, LANES - tl, 1))
            z = [jnp.tanh(g) for g in (v[0], v[4], tz)]
            f = [sigmoid(g) for g in (v[1], v[5], tf)]
            o = [sigmoid(g) for g in (v[2], v[6], to)]
            at = now(t)
            ca = ca_t[at, :]
            gains, totals = [], []
            for q in range(3):
                zs[at, cols[q]] = z[q]
                fs[at, cols[q]] = f[q]
                os_[at, cols[q]] = o[q]
                gains.append(gain[q] * (f[q] * ca))
                totals.append(z[q] + f[q] * (ca * total[q] - z[q]))
            return tuple(gains), tuple(totals)

        gain, total = lax.fori_loop(0, steps, gates_step, ((one,) * 3, (zero,) * 3), unroll=UNROLL)
        for q in range(3):
            small[0, :, cols[q]] = gain[q]
            small[1, :, cols[q]] = total[q]
        run = jnp.zeros((1, 3 * LANES), f32)
        for s in range(SEGS):
            small[2, s : s + 1, :] = run
            run = small[0, s : s + 1, :] * run + small[1, s : s + 1, :]
        cell = tuple(small[2, :, cols[q]] for q in range(3))

        def cell_step(t, state):
            cell, back, gain = state
            at = now(t)
            ca = ca_t[at, :]
            cells, backs, gains = [], [], []
            for q in range(3):
                z, f, o = zs[at, cols[q]], fs[at, cols[q]], os_[at, cols[q]]
                prev = ca * cell[q]
                cbs[at, cols[q]] = prev
                new = z + f * (prev - z)
                hs[q, pl.ds(t, SEGS, stride=sp), :] = o * new
                g = jnp.where(t == 0, one, gain[q] * (f * ca))
                cells.append(new)
                gains.append(g)
                backs.append(back[q] + g * (strided(ct, t, q) * o))
            return tuple(cells), tuple(backs), tuple(gains)

        cell, back, gain = lax.fori_loop(0, steps, cell_step, (cell, (zero,) * 3, (one,) * 3), unroll=UNROLL)
        for q in range(3):
            small[0, :, cols[q]] = back[q]
            small[1, :, cols[q]] = gain[q]
            small[3, :, cols[q]] = fs[0:SEGS, cols[q]] * ca_t[0:SEGS, :]
        run = jnp.zeros((1, 3 * LANES), f32)
        for s in range(SEGS - 1, -1, -1):
            small[2, s : s + 1, :] = run
            run = small[3, s : s + 1, :] * (small[0, s : s + 1, :] + small[1, s : s + 1, :] * run)
        later = tuple(small[2, :, cols[q]] for q in range(3))

        def grad_step(i, later):
            t = steps - 1 - i
            at = now(t)
            ca = ca_t[at, :]
            gz, gf, go_, laters = [], [], [], []
            for q in range(3):
                z, f, o, prev = zs[at, cols[q]], fs[at, cols[q]], os_[at, cols[q]], cbs[at, cols[q]]
                c = strided(ct, t, q)
                dc = c * o + later[q]
                laters.append((f * ca) * dc)
                d = prev - z
                u = dc * (1.0 - f)
                gz.append(u * (1.0 - z * z))
                gf.append(u * (f * d))
                go_.append(c * (z + f * d) * (o * (1.0 - o)))
            z, f, o = gz[2], gf[2], go_[2]
            u = jnp.where(
                lane < tl,
                z,
                jnp.where(
                    lane < 2 * tl,
                    pltpu.roll(f, tl, 1),
                    jnp.where(lane < 3 * tl, pltpu.roll(o, 2 * tl, 1), 0.0),
                ),
            )
            w = jnp.where(
                lane < tl,
                pltpu.roll(z, LANES - tl, 1),
                jnp.where(lane < 2 * tl, f, jnp.where(lane < 3 * tl, pltpu.roll(o, tl, 1), 0.0)),
            )
            for q, v in enumerate((gz[0], gf[0], go_[0], u, gz[1], gf[1], go_[1], w)):
                pre[q, pl.ds(t, SEGS, stride=sp), :] = v
            return tuple(laters)

        lax.fori_loop(0, steps, grad_step, later, unroll=UNROLL)

        nxt[...] = jnp.zeros_like(nxt)

        def input_step(i, _):
            i = n // TILE - 1 - i
            o = pl.multiple_of(i * TILE, TILE)
            for h in range(TILE // steps):
                into = pl.ds(pl.multiple_of(r * n + o + h * steps, LANES), steps)
                for q in range(8):
                    v = pre[q, seg(i * (TILE // steps) + h), :].astype(bf16)
                    dp[into, q * LANES : (q + 1) * LANES] = v
                    v = v.astype(f32)
                    a = v[0:SEGS]
                    for s in range(SEGS, steps, SEGS):
                        a = a + v[s : s + SEGS]
                    sums[:, q * LANES : (q + 1) * LANES] += a
                for q in range(3):
                    e = LANES if q < 2 else 2 * tl
                    v = hs[q, seg(i * (TILE // steps) + h), :].T.astype(bf16)
                    hb[q * LANES : q * LANES + e, into] = v[0:e]
            dj = dot(wb[...], dp[pl.ds(pl.multiple_of(r * n + o, TILE), TILE), :], 1, 1)
            after = nxt[...]
            for h in range(TILE // LANES - 1, -1, -1):
                at = slice(h * LANES, (h + 1) * LANES)
                into = pl.ds(pl.multiple_of(r * n + o + h * LANES, LANES), LANES)
                rolled = pltpu.roll(
                    dj[D:, at] * cl[0:1, pl.ds(pl.multiple_of(o + h * LANES, LANES), LANES)], LANES - 1, 1
                )
                dxb[:, into] = (dj[:D, at] + jnp.where(edge, after, rolled)).astype(bf16)
                after = rolled
            nxt[...] = after
            return 0

        lax.fori_loop(0, n // TILE, input_step, 0)
        for copy in hidden_copies(r) + grad_copies(r):
            copy.start()
        return 0

    lax.fori_loop(0, rows, row, 0)
    if not first:
        pltpu.make_async_copy(acc_in, accb, sem.at[2]).wait()
    for q in range(8):
        at = slice(q * LANES, (q + 1) * LANES)
        s = sums[:, at]
        if not first:
            s = s + accb[2 * D :, at]
        if last:
            s = jnp.sum(s, 0, keepdims=True)
            if q >= 4:
                ab[2 * D :, (q - 4) * LANES : (q - 3) * LANES] = in_two(s)
        accb[2 * D :, at] = jnp.broadcast_to(s, (SEGS, LANES))

    def own_copy(i):
        at = pl.ds(pl.multiple_of(i * TILE, TILE), TILE)
        return pltpu.make_async_copy(accb.at[:, at], (acc_own if last else acc_out).at[:, at], sem.at[4 + i])

    def sib_copy(i):
        at = pl.ds(pl.multiple_of(i * TILE, TILE), TILE)
        return pltpu.make_async_copy(ab.at[:, at], acc_sib.at[:, at], sem.at[2 + i])

    def weight_step(i, _):
        at = pl.ds(pl.multiple_of(i * TILE, TILE), TILE)
        v = dot(xb[...], dp[:, at], 1, 0)
        if not first:
            v = v + accb[0 : 2 * D, at]
        accb[0 : 2 * D, at] = v
        own_copy(i).start()
        return 0

    def weight_sib_step(i, _):
        at = pl.ds(pl.multiple_of(half + i * TILE, TILE), TILE)
        v = dot(xb[...], dp[:, at], 1, 0)
        if not first:
            v = v + accb[0 : 2 * D, at]
        ab[0 : 2 * D, pl.ds(pl.multiple_of(i * TILE, TILE), TILE)] = v.astype(bf16)
        sib_copy(i).start()
        return 0

    own_tiles = (half if last else 2 * half) // TILE
    if last:
        lax.fori_loop(0, half // TILE, weight_sib_step, 0)
    lax.fori_loop(0, own_tiles, weight_step, 0)
    for i in range(own_tiles):
        own_copy(i).wait()
    if last:
        for i in range(half // TILE):
            sib_copy(i).wait()
    if first:
        pltpu.make_async_copy(wb, w_out, sem.at[0]).wait()
    for r in range(rows):
        for copy in hidden_copies(r) + grad_copies(r):
            copy.wait()


def layer(k, calls, rows, parts, C, n, tok, sib, cot, scot, ids, biases, x, w, acc, hid):
    first, last = k == 0, k == calls - 1
    D = 4 * C
    N = 8 * LANES
    T = rows * n
    shape = jax.ShapeDtypeStruct
    ins = [tok, sib, cot, scot, ids] + list(biases) + list(x)
    alias = {}
    outs = [shape(tok.shape, bf16), shape((2 * C, T), bf16)] + [shape((C, T), bf16)] * 3
    if first:
        ins += list(w)
    else:
        ins += [w, acc, hid]
        alias = {len(ins) - 1: 0}
        if not last:
            alias[len(ins) - 2] = 5
    if last:
        outs += [shape((2 * D + SEGS, N // 2), f32), shape((2 * D + 16, N // 2), bf16)]
    else:
        outs += [shape((2 * D + SEGS, N), f32)]
    if first:
        outs += [shape((2 * D, N), bf16)]
    w3 = 3 * LANES
    tall = n + SEGS * PAD
    scratch = (
        [
            pltpu.VMEM((2 * D, T), bf16),
            pltpu.VMEM((2 * D, N), bf16),
            pltpu.VMEM((w3, T), bf16),
            pltpu.VMEM((8, tall, LANES), f32),
        ]
        + [pltpu.VMEM((n, w3), f32)] * 4
        + [pltpu.VMEM((3, tall, LANES), f32)] * 2
        + [
            pltpu.VMEM((2 * C, T), bf16),
            pltpu.VMEM((T, N), bf16),
            pltpu.VMEM((D, T), bf16),
            pltpu.VMEM((2 * D + SEGS, N), f32),
            pltpu.VMEM((2 * D + 16, N // 2), bf16),
            pltpu.VMEM((4, SEGS, w3), f32),
            pltpu.VMEM((D, LANES), f32),
            pltpu.VMEM((SEGS, N), f32),
            pltpu.VMEM((SEGS, n), f32),
            pltpu.VMEM((n, LANES), f32),
            pltpu.VMEM((rows, SEGS, LANES), jnp.int32),
            pltpu.VMEM((SEGS, N), f32),
            pltpu.SemaphoreType.DMA((8 + 2 * parts,)),
            pltpu.SemaphoreType.DMA((rows, 18)),
        ]
    )
    return pl.pallas_call(
        functools.partial(layer_kernel, k, calls, rows, parts, C, n),
        out_shape=outs,
        in_specs=[ANY] * len(ins),
        out_specs=[ANY] * len(outs),
        scratch_shapes=scratch,
        input_output_aliases=alias,
        compiler_params=pltpu.CompilerParams(vmem_limit_bytes=60 << 20),
        cost_estimate=pl.CostEstimate(flops=1, bytes_accessed=1, transcendentals=0),
        name="layer",
    )(*ins)


def take_kernel(picks, n, tok, *refs):
    outs, (bufs, sem) = refs[:-2], refs[-2:]
    core = lax.axis_index("chan") & 1
    copies, sends = [], []
    for i, pick in enumerate(picks):
        for j, (pair, mine) in enumerate(pick):
            at = pl.ds(pl.multiple_of((2 * pair + (core if mine else 1 - core)) * n, n), n)
            copies.append(pltpu.make_async_copy(tok.at[:, at], bufs.at[i, :, j * n : (j + 1) * n], sem.at[i, j]))
            copies[-1].start()
    for i, pick in enumerate(picks):
        for copy in copies[i * len(pick) : (i + 1) * len(pick)]:
            copy.wait()
        sends.append(pltpu.make_async_copy(bufs.at[i], outs[i], sem.at[i, 0]))
        sends[-1].start()
    for send in sends:
        send.wait()


def take_rows(picks, C, n, tok):
    width = len(picks[0]) * n
    return pl.pallas_call(
        functools.partial(take_kernel, picks, n),
        out_shape=[jax.ShapeDtypeStruct((C, width), bf16)] * len(picks),
        in_specs=[ANY],
        out_specs=[ANY] * len(picks),
        scratch_shapes=[
            pltpu.VMEM((len(picks), C, width), bf16),
            pltpu.SemaphoreType.DMA((len(picks), len(picks[0]))),
        ],
        cost_estimate=pl.CostEstimate(flops=1, bytes_accessed=1, transcendentals=0),
        name="take",
    )(tok)


def pack_kernel(C, w, b, out, b_out):
    tail = C - LANES
    parts = [w[g, 0:LANES].astype(f32) for g in range(3)] + [w[g, LANES:C].astype(f32) for g in range(3)]
    parts.append(jnp.zeros((LANES - 3 * tail, w.shape[2]), f32))
    out[...] = jnp.concatenate(parts, 0).T.astype(bf16)
    b_out[...] = jnp.zeros_like(b_out)
    for g in range(3):
        b_out[0:1, g * LANES : (g + 1) * LANES] = b[g : g + 1, 0:LANES]
        b_out[0:1, 3 * LANES + g * tail : 3 * LANES + (g + 1) * tail] = b[g : g + 1, LANES:C]


def pack(C, w, b):
    return pl.pallas_call(
        functools.partial(pack_kernel, C),
        out_shape=[
            jax.ShapeDtypeStruct((w.shape[2], 4 * LANES), bf16),
            jax.ShapeDtypeStruct((SEGS, 4 * LANES), f32),
        ],
        in_specs=[VMEM] * 2,
        out_specs=[VMEM] * 2,
        cost_estimate=pl.CostEstimate(flops=1, bytes_accessed=1, transcendentals=0),
        name="pack",
    )(w, b)


def finish_kernel(k, rows, mine, C, n, near, far, *refs):
    total, sem = refs[-2:]
    if mine:
        grad = refs[-3]
    else:
        grad, hid = refs[-4:-2]
    core = lax.axis_index("chan") & 1
    which = core if mine else 1 - core
    copies = []

    def go(src, out, r):
        at = pl.ds(pl.multiple_of((2 * (k * rows + r) + which) * n, n), n)
        copies.append(pltpu.make_async_copy(src, out.at[:, at], sem.at[len(copies)]))
        copies[-1].start()

    for r in range(rows):
        at = slice(r * n, (r + 1) * n)
        if not mine:
            go(near.at[C : 2 * C, at], hid, r)
        total[:, at] = (near[0:C, at].astype(f32) + far[:, at].astype(f32)).astype(bf16)
        go(total.at[:, at], grad, r)
    for copy in copies:
        copy.wait()


def finish(k, rows, mine, C, n, total, near, far, grad, hid=None):
    ins = [near, far]
    specs = [VMEM] * 2
    shape = jax.ShapeDtypeStruct((C, total), bf16)
    outs = [shape]
    alias = {}
    for v in (grad, hid):
        if v is not None:
            alias[len(ins)] = 0 if v is grad else 1
            ins.append(v)
            specs.append(ANY)
    if hid is not None:
        outs.append(shape)
    return pl.pallas_call(
        functools.partial(finish_kernel, k, rows, mine, C, n),
        out_shape=outs,
        in_specs=specs,
        out_specs=[ANY] * len(outs),
        scratch_shapes=[pltpu.VMEM((C, rows * n), bf16), pltpu.SemaphoreType.DMA((2 * rows,))],
        input_output_aliases=alias,
        cost_estimate=pl.CostEstimate(flops=1, bytes_accessed=1, transcendentals=0),
        name="finish",
    )(*ins)


def in_two(v):
    high = v.astype(bf16)
    low = v - high.astype(f32)
    at = lax.broadcasted_iota(jnp.int32, (16, v.shape[1]), 0)
    return jnp.where(at == 0, high.astype(f32), jnp.where(at == 1, low, 0.0)).astype(bf16)


def from_two(v):
    v = v[...].astype(f32)
    return v[0:1] + v[1:2]


def split_kernel(C, own, other, s7, s3, s5, s2, kept):
    place = lax.axis_index("dp")
    b = own[8 * C : 8 * C + 1, :] + from_two(other[8 * C :, :])
    for j, out in ((7, s7), (3, s3), (5, s5), (2, s2)):
        at = pl.ds(pl.multiple_of((place ^ j) * C, 32), C)
        out[0:C] = (own[at, :] + other[at, :].astype(f32)).astype(bf16)
        out[C:] = in_two(b)
    for i, j in enumerate((0, 1, 4, 6)):
        at = pl.ds(pl.multiple_of((place ^ j) * C, 32), C)
        kept[i, 0:C] = own[at, :] + other[at, :].astype(f32)
    kept[0, C : C + 8] = jnp.broadcast_to(b, (8, b.shape[1]))


def split(C, own, other):
    half = own.shape[1]
    message = jax.ShapeDtypeStruct((C + 16, half), bf16)
    return pl.pallas_call(
        functools.partial(split_kernel, C),
        out_shape=[message] * 4 + [jax.ShapeDtypeStruct((4, C + 16, half), f32)],
        in_specs=[VMEM] * 2,
        out_specs=[VMEM] * 5,
        compiler_params=pltpu.CompilerParams(vmem_limit_bytes=40 << 20),
        cost_estimate=pl.CostEstimate(flops=1, bytes_accessed=1, transcendentals=0),
        name="split",
    )(own, other)


def second_kernel(C, kept, r7, r3, r5, s6, s1, k4):
    b = kept[0, C : C + 1]
    s6[0:C] = (kept[3, 0:C] + r7[0:C].astype(f32)).astype(bf16)
    s6[C:] = in_two(b + from_two(r7[C:]))
    s1[0:C] = (kept[1, 0:C] + r3[0:C].astype(f32)).astype(bf16)
    s1[C:] = in_two(b + from_two(r3[C:]))
    k4[0:C] = kept[2, 0:C] + r5[0:C].astype(f32)
    k4[C : C + 8] = jnp.broadcast_to(b + from_two(r5[C:]), (8, b.shape[1]))


def second(C, kept, r7, r3, r5):
    half = kept.shape[2]
    message = jax.ShapeDtypeStruct((C + 16, half), bf16)
    return pl.pallas_call(
        functools.partial(second_kernel, C),
        out_shape=[message] * 2 + [jax.ShapeDtypeStruct((C + 16, half), f32)],
        in_specs=[VMEM] * 4,
        out_specs=[VMEM] * 3,
        cost_estimate=pl.CostEstimate(flops=1, bytes_accessed=1, transcendentals=0),
        name="second",
    )(kept, r7, r3, r5)


def third_kernel(C, k4, r6, s4):
    s4[0:C] = (k4[0:C] + r6[0:C].astype(f32)).astype(bf16)
    s4[C:] = in_two(k4[C : C + 1] + from_two(r6[C:]))


def third(C, k4, r6):
    return pl.pallas_call(
        functools.partial(third_kernel, C),
        out_shape=jax.ShapeDtypeStruct(r6.shape, bf16),
        in_specs=[VMEM] * 2,
        out_specs=VMEM,
        cost_estimate=pl.CostEstimate(flops=1, bytes_accessed=1, transcendentals=0),
        name="third",
    )(k4, r6)


def total_kernel(C, kept, r2, r1, r4, grad, bias):
    v = kept[0, 0:C] + r2[0:C].astype(f32) + (r1[0:C].astype(f32) + r4[0:C].astype(f32))
    t = v.T
    tail = C - LANES
    for g in range(3):
        grad[g, 0:LANES] = t[g * LANES : (g + 1) * LANES]
        grad[g, LANES:C] = t[3 * LANES + g * tail : 3 * LANES + (g + 1) * tail]
    b = kept[0, C : C + 1] + from_two(r2[C:]) + (from_two(r1[C:]) + from_two(r4[C:]))
    for g in range(3):
        bias[g : g + 1, 0:LANES] = b[:, g * LANES : (g + 1) * LANES]
        bias[g : g + 1, LANES:C] = b[:, 3 * LANES + g * tail : 3 * LANES + (g + 1) * tail]


def total_sum(C, kept, r2, r1, r4):
    return pl.pallas_call(
        functools.partial(total_kernel, C),
        out_shape=[jax.ShapeDtypeStruct((3, C, C), f32), jax.ShapeDtypeStruct((3, C), f32)],
        in_specs=[VMEM] * 4,
        out_specs=[VMEM] * 2,
        cost_estimate=pl.CostEstimate(flops=1, bytes_accessed=1, transcendentals=0),
        name="total",
    )(kept, r2, r1, r4)


def local(chan, parts, tokens, weights, bias, segment_ids, cotangent):
    C, total = tokens.shape
    n = LEN
    pairs = total // n // 2
    rows = pairs // CALLS
    me = lax.axis_index("chan")
    core = me & 1

    def chan_move(v, j):
        return lax.ppermute(v, "chan", [(i, i ^ j) for i in range(chan)])

    def dp_move(v, j):
        return lax.ppermute(v, "dp", [(i, i ^ j) for i in range(parts)])

    def after(v, *others):
        return lax.optimization_barrier((v,) + others)[0]

    ids = segment_ids.reshape(2 * pairs * SEGS, n // SEGS)
    def other_rows(k, tok):
        picks = [[(k * rows + r, mine) for r in range(rows)] for mine in (True, False)]
        return take_rows(picks, C, n, tok)

    to_near, to_far = other_rows(0, tokens)
    near, far = chan_move(to_near, 2), chan_move(to_far, 3)
    xs = [(near, far)]
    shard, b_own = pack(C, after(weights, to_near), bias)
    g = {0: shard, 4: dp_move(shard, 4), 1: dp_move(shard, 1), 2: dp_move(shard, 2)}
    sib = chan_move(tokens, 1)
    scot = chan_move(cotangent, 1)
    g4, g1 = lax.optimization_barrier((g[4], g[1], sib))[:2]
    g[6] = dp_move(g4, 2)
    g[5] = dp_move(g4, 1)
    g[3] = dp_move(g1, 2)
    early = chan_move(jnp.concatenate([g[j] for j in EARLY], 0), 1)
    biases = [b_own, chan_move(after(b_own, g[4]), 1)]
    g[7] = dp_move(after(g[6], near, scot), 1)
    w = [g[j] for j in range(parts)] + [early] + [chan_move(g[j], 1) for j in LATE]
    for k in range(1, CALLS):
        to_near, to_far = other_rows(k, after(tokens, g[4]))
        xs.append((chan_move(to_near, 2), chan_move(to_far, 3)))

    acc = hid = grad = None
    moved = []
    for k in range(CALLS):
        out = layer(
            k, CALLS, rows, parts, C, n, tokens, sib, cotangent, scot, ids, biases, xs[k], w, acc, hid
        )
        if k == 0:
            w = out[-1]
        hid, to_sib, d_px, d_pd, own, acc = out[:6]
        if k == CALLS - 1:
            got = [v for m in moved for v in m[1:]]
            to_sib, d_px, d_pd, acc_sib = lax.optimization_barrier((to_sib, d_px, d_pd, out[6], *got))[:4]
            acc_sib = chan_move(acc_sib, 1)
        else:
            to_sib, d_px, d_pd = lax.optimization_barrier((to_sib, d_px, d_pd, *xs[k + 1]))[:3]
        moved.append((own, chan_move(d_px, 2), chan_move(to_sib, 1), chan_move(d_pd, 3)))

    def end(k, mine, *others):
        nonlocal grad, hid
        own, from_px, from_sib, from_pd = moved[k]
        if mine:
            (grad,) = finish(k, rows, True, C, n, total, after(own, *others), from_px, grad)
        else:
            grad, hid = finish(k, rows, False, C, n, total, after(from_sib, *others), from_pd, grad, hid)

    for k in range(CALLS - 1):
        end(k, True)
        end(k, False)
    s7, s3, s5, s2, kept = split(C, after(acc, grad), acc_sib)
    r7, r3, r5 = dp_move(s7, 1), dp_move(s3, 2), dp_move(s5, 1)
    s6, s1, k4 = second(C, kept, r7, r3, r5)
    r6, r1, r2 = dp_move(s6, 2), dp_move(s1, 1), dp_move(s2, 2)
    s4 = third(C, k4, r6)
    r4 = dp_move(s4, 4)
    end(CALLS - 1, True, s4)
    weight_grad, bias_grad = total_sum(C, kept, r2, r1, r4)
    end(CALLS - 1, False, weight_grad)
    return (hid, grad, weight_grad, bias_grad)


def combine(earlier, later):
    return (earlier[0] * later[0], later[0] * earlier[1] + later[1])


def local_any(tokens, weights, bias, segment_ids, cotangent):
    width_part, total_rows = tokens.shape
    batch_rows = total_rows // MICRO
    grad_shard = jnp.zeros(weights.shape, jnp.float32)
    bias_total = jnp.zeros(bias.shape, jnp.float32)
    position = jnp.arange(batch_rows) % LEN
    hidden_parts = []
    input_parts = []
    for micro in range(MICRO):
        lower = micro * batch_rows
        upper = lower + batch_rows
        part_in = tokens[:, lower:upper]
        ids = segment_ids[lower:upper]
        cot = cotangent[:, lower:upper].astype(jnp.float32)
        before = jnp.concatenate([ids[:1], ids[:-1]], 0)
        carry_flag = (position > 0) & (ids == before)
        carry_on = jnp.where(carry_flag, 1.0, 0.0).astype(jnp.float32)
        gathered = lax.all_gather(part_in, "chan", axis=0, tiled=True)
        width = gathered.shape[0]
        shifted = jnp.concatenate([jnp.zeros((width, 1), jnp.bfloat16), gathered[:, :-1]], 1)
        previous = jnp.where(carry_flag[None, :], shifted, jnp.zeros((), jnp.bfloat16))
        joined_inputs = jnp.concatenate([gathered, previous], 0)
        preactivation = jnp.einsum(
            "gcr,rl->gcl",
            lax.all_gather(weights, "dp", axis=2, tiled=True),
            joined_inputs,
            preferred_element_type=jnp.float32,
        )
        preactivation = preactivation + bias[:, :, None]
        gate_z = jnp.tanh(preactivation[0])
        forget = jax.nn.sigmoid(preactivation[1])
        output_gate = jax.nn.sigmoid(preactivation[2])
        decay = forget * carry_on[None, :]
        source = (1.0 - forget) * gate_z
        cell = lax.associative_scan(combine, (decay, source), axis=1)[1]
        hidden_parts.append((output_gate * cell).astype(jnp.bfloat16))
        decay_next = jnp.concatenate([decay[:, 1:], jnp.zeros((width_part, 1), jnp.float32)], 1)
        dcell = lax.associative_scan(combine, (decay_next, cot * output_gate), reverse=True, axis=1)[1]
        cell_before = (
            jnp.concatenate([jnp.zeros((width_part, 1), jnp.float32), cell[:, :-1]], 1)
            * carry_on[None, :]
        )
        grad_z = dcell * (1.0 - forget) * (1.0 - gate_z * gate_z)
        grad_f = dcell * (cell_before - gate_z) * forget * (1.0 - forget)
        grad_o = cot * cell * output_gate * (1.0 - output_gate)
        dpre_low = jnp.stack([grad_z, grad_f, grad_o], 0).astype(jnp.bfloat16)
        bias_total = bias_total + jnp.sum(dpre_low.astype(jnp.float32), axis=2)
        weight_term = jnp.einsum(
            "gcl,rl->gcr", dpre_low, joined_inputs, preferred_element_type=jnp.float32
        )
        djoined = jnp.einsum(
            "gcl,gcr->rl",
            dpre_low,
            lax.all_gather(weights, "dp", axis=2, tiled=True),
            preferred_element_type=jnp.float32,
        )
        later = djoined[width:] * carry_on[None, :]
        later = jnp.concatenate([later[:, 1:], jnp.zeros((width, 1), jnp.float32)], 1)
        term = djoined[:width] + later
        input_parts.append(
            lax.psum_scatter(term, "chan", scatter_dimension=0, tiled=True).astype(jnp.bfloat16)
        )
        grad_shard = grad_shard + lax.psum_scatter(weight_term, "dp", scatter_dimension=2, tiled=True)
    bias_grad = lax.psum(bias_total, "dp")
    hidden = jnp.concatenate(hidden_parts, 1)
    input_grad = jnp.concatenate(input_parts, 1)
    return (hidden, input_grad, grad_shard, bias_grad)


def solution(mesh):
    chan, parts = mesh.shape["chan"], mesh.shape["dp"]
    in_specs = (P("chan", "dp"), P(None, "chan", "dp"), P(None, "chan"), P("dp"), P("chan", "dp"))
    out_specs = (P("chan", "dp"), P("chan", "dp"), P(None, "chan", "dp"), P(None, "chan"))

    def run(tokens, weights, bias, segment_ids, cotangent):
        C = tokens.shape[0] // chan
        row_part = weights.shape[2] // parts
        pairs = tokens.shape[1] // parts % (2 * LEN * CALLS) == 0
        tail = C - LANES
        fits = chan == 4 and parts == 8 and row_part == C and pairs and 0 < 3 * tail < LANES and tail % 32 == 0
        body = functools.partial(local, chan, parts) if fits else local_any
        return jax.shard_map(body, mesh=mesh, in_specs=in_specs, out_specs=out_specs, check_vma=False)(
            tokens, weights, bias, segment_ids, cotangent
        )

    return run
```

```python
import functools

import jax
import jax.numpy as jnp
from jax import lax
from jax.experimental import pallas as pl
from jax.experimental.pallas import tpu as pltpu
from jax.sharding import PartitionSpec as P

LEN = 1024
MICRO = 4
LANES = 128
SEGS = 8
PAD = 8
TILE = 256
UNROLL = 16
FTILE = 1024
TILES = LEN // TILE
CALLS = 2
GROUPS = ((0, 1, 4), (2, 5, 6), (3, 7))
f32 = jnp.float32
bf16 = jnp.bfloat16
ANY = pl.BlockSpec(memory_space=pl.ANY)
VMEM = pl.BlockSpec(memory_space=pltpu.VMEM)
HBM = pl.BlockSpec(memory_space=pltpu.HBM)
SMEM = pl.BlockSpec(memory_space=pltpu.SMEM)


def dot(a, b, ca, cb):
    return lax.dot_general(a, b, (((ca,), (cb,)), ((), ())), preferred_element_type=f32)


def sigmoid(v):
    return 0.5 * jnp.tanh(0.5 * v) + 0.5


def layer_kernel(k, calls, rows, parts, C, n, *refs):
    first, last = k == 0, k == calls - 1
    refs = list(refs)
    tok, sib, cot, scot, ids, bias, bias_sib, x_near, x_far = refs[:9]
    refs = refs[9:]
    if first:
        w_in, refs = refs[: parts + len(GROUPS)], refs[parts + len(GROUPS) :]
    else:
        w_in, acc_in, refs = refs[0], refs[1], refs[3:]
    hid, to_sib, dx_px, dx_pd, dx_own = refs[:5]
    refs = refs[5:]
    if last:
        acc_own, acc_sib, refs = refs[0], refs[1], refs[2:]
    else:
        acc_out, refs = refs[0], refs[1:]
    if first:
        w_out, refs = refs[0], refs[1:]
    (xb, wb, cb, pre, gp, zs, fs, os_, cbs, ct, hs, hb, dp, dxb, accb, ab, small, nxt, sums, cl, ca_t, id_b, bb, sem, rsem) = refs
    D = 4 * C
    tl = C - LANES
    steps = n // SEGS
    sp = steps + PAD
    half = 4 * LANES
    me, place = lax.axis_index("chan"), lax.axis_index("dp")
    core = me & 1

    def go(src, dst, i):
        copy = pltpu.make_async_copy(src, dst, sem.at[i])
        copy.start()
        return copy

    def here(r):
        return pl.ds(pl.multiple_of((2 * (k * rows + r) + core) * n, n), n)

    def span(r):
        return pl.ds(pl.multiple_of(r * n, n), n)

    def block(j):
        return pl.ds(pl.multiple_of((me ^ j) * C, 32), C)

    def seg(h):
        return pl.ds(pl.multiple_of(h * sp, 8), steps)

    def id_rows(r):
        return pl.ds(pl.multiple_of((2 * (k * rows + r) + core) * SEGS, SEGS), SEGS)

    def x_copies(r):
        from_row = span(r)
        pairs = (
            (tok.at[:, here(r)], xb.at[block(0), span(r)]),
            (sib.at[:, here(r)], xb.at[block(1), span(r)]),
            (x_near.at[:, from_row], xb.at[block(2), span(r)]),
            (x_far.at[:, from_row], xb.at[block(3), span(r)]),
            (ids.at[id_rows(r)], id_b.at[r]),
        )
        return [pltpu.make_async_copy(a, b, rsem.at[r, i]) for i, (a, b) in enumerate(pairs)]

    def c_copies(r):
        pairs = (
            (cot.at[0:LANES, here(r)], cb.at[0:LANES, span(r)]),
            (scot.at[0:LANES, here(r)], cb.at[LANES : 2 * LANES, span(r)]),
            (cot.at[LANES:C, here(r)], cb.at[2 * LANES : 2 * LANES + tl, span(r)]),
            (scot.at[LANES:C, here(r)], cb.at[2 * LANES + tl : 2 * LANES + 2 * tl, span(r)]),
        )
        return [pltpu.make_async_copy(a, b, rsem.at[r, 5 + i]) for i, (a, b) in enumerate(pairs)]

    def hidden_copies(r):
        pairs = (
            (hb.at[0:LANES, span(r)], hid.at[0:LANES, here(r)]),
            (hb.at[LANES : 2 * LANES, span(r)], to_sib.at[C : C + LANES, span(r)]),
            (hb.at[2 * LANES : 2 * LANES + tl, span(r)], hid.at[LANES:C, here(r)]),
            (hb.at[2 * LANES + tl : 2 * LANES + 2 * tl, span(r)], to_sib.at[C + LANES : 2 * C, span(r)]),
        )
        return [pltpu.make_async_copy(a, b, rsem.at[r, 10 + i]) for i, (a, b) in enumerate(pairs)]

    def grad_copies(r):
        outs = (dx_own, to_sib.at[0:C], dx_px, dx_pd)
        return [
            pltpu.make_async_copy(dxb.at[block(j), span(r)], out.at[:, span(r)], rsem.at[r, 14 + j])
            for j, out in enumerate(outs)
        ]

    for copy in x_copies(0):
        copy.start()
    if first:
        w_copies = []
        for j in range(parts):
            at = pl.ds(pl.multiple_of((place ^ j) * C, 32), C)
            w_copies.append(go(w_in[j], wb.at[at, 0:half], 8 + j))
            which = [j in group for group in GROUPS].index(True)
            spot = GROUPS[which].index(j)
            other = w_in[parts + which].at[spot * C : (spot + 1) * C]
            w_copies.append(go(other, wb.at[at, half : 2 * half], 8 + parts + j))
    else:
        w_copies = [go(w_in, wb, 0)]
    b_copies = [go(bias, bb.at[:, 0:half], 1), go(bias_sib, bb.at[:, half : 2 * half], 3)]
    for r in range(rows):
        for copy in (x_copies(r) if r else []) + c_copies(r):
            copy.start()
    sums[...] = jnp.zeros_like(sums)
    lane = lax.broadcasted_iota(jnp.int32, (SEGS, LANES), 1)
    edge = lax.broadcasted_iota(jnp.int32, (D, LANES), 1) == LANES - 1
    cols = [slice(q * LANES, (q + 1) * LANES) for q in range(3)]
    one = jnp.ones((SEGS, LANES), f32)
    zero = jnp.zeros((SEGS, LANES), f32)

    def strided(ref, t, q):
        return ref[q, pl.ds(t, SEGS, stride=sp), :]

    def now(t):
        return pl.ds(pl.multiple_of(t * SEGS, SEGS), SEGS)

    def arrive(r):
        for copy in x_copies(r):
            copy.wait()
        seg_ids = id_b[r]
        before = pltpu.roll(seg_ids, 1, 1)
        before = jnp.where(lane == 0, pltpu.roll(before, 1, 0), before)
        sub = lax.broadcasted_iota(jnp.int32, (SEGS, steps), 0)
        carry = jnp.where((seg_ids == before) & ((lane > 0) | (sub > 0)), 1.0, 0.0).astype(f32)
        for s in range(SEGS):
            cl[r, :, s * steps : (s + 1) * steps] = jnp.broadcast_to(carry[s : s + 1, :], (SEGS, steps))
        for t in range(steps):
            ca_t[r, t * SEGS : (t + 1) * SEGS, :] = jnp.broadcast_to(carry[:, t : t + 1], (SEGS, LANES))

    rb = 32

    def previous(r, i):
        o = pl.multiple_of(i * rb, rb)
        v = xb[pl.ds(o, rb), span(r)].astype(f32)
        xb[pl.ds(D + o, rb), span(r)] = (pltpu.roll(v, 1, 1) * cl[r, 0:1, :]).astype(bf16)

    def forward(r, i):
        o = pl.multiple_of(r * n + i * FTILE, FTILE)
        v = dot(xb[:, pl.ds(o, FTILE)], wb[...], 0, 0)
        for h in range(FTILE // steps):
            at = seg(i * (FTILE // steps) + h)
            for q in range(8):
                pre[q, at, :] = v[h * steps : (h + 1) * steps, q * LANES : (q + 1) * LANES]
            c = cb[:, pl.ds(pl.multiple_of(o + h * steps, LANES), steps)].astype(f32).T
            for q in range(3):
                ct[q, at, :] = c[:, q * LANES : (q + 1) * LANES]

    def round_tile(r, i):
        into = pl.ds(pl.multiple_of(r * n + i * steps, LANES), steps)
        for q in range(8):
            v = gp[q, seg(i), :].astype(bf16)
            dp[into, q * LANES : (q + 1) * LANES] = v
            v = v.astype(f32)
            a = v[0:SEGS]
            for s in range(SEGS, steps, SEGS):
                a = a + v[s : s + SEGS]
            sums[:, q * LANES : (q + 1) * LANES] += a
        for q in range(3):
            e = LANES if q < 2 else 2 * tl
            hb[q * LANES : q * LANES + e, into] = hs[q, seg(i), :].T.astype(bf16)[0:e]

    def input_tile(r, i):
        i = n // TILE - 1 - i
        o = pl.multiple_of(i * TILE, TILE)
        dj = dot(wb[...], dp[pl.ds(pl.multiple_of(r * n + o, TILE), TILE), :], 1, 1)
        after = nxt[...]
        for h in range(TILE // LANES - 1, -1, -1):
            at = slice(h * LANES, (h + 1) * LANES)
            into = pl.ds(pl.multiple_of(r * n + o + h * LANES, LANES), LANES)
            rolled = pltpu.roll(
                dj[D:, at] * cl[r, 0:1, pl.ds(pl.multiple_of(o + h * LANES, LANES), LANES)], LANES - 1, 1
            )
            dxb[:, into] = (dj[:D, at] + jnp.where(edge, after, rolled)).astype(bf16)
            after = rolled
        nxt[...] = after

    def weight_tile(r, i, add):
        at = pl.ds(pl.multiple_of(i * TILE, TILE), TILE)
        v = dot(xb[:, span(r)], dp[span(r), at], 1, 0)
        return (v + accb[0 : 2 * D, at] if add else v), at

    def weight_step(r, i):
        v, at = weight_tile(r, i, not (first and r == 0))
        accb[0 : 2 * D, at] = v

    def gates_step(r, b, t, state):
        gain, total = state
        v = [strided(pre, t, q) + b[q] for q in range(8)]
        u, w = v[3], v[7]
        tz = jnp.where(lane < tl, u, pltpu.roll(w, tl, 1))
        tf = jnp.where(lane < tl, pltpu.roll(u, LANES - tl, 1), w)
        to = jnp.where(lane < tl, pltpu.roll(u, LANES - 2 * tl, 1), pltpu.roll(w, LANES - tl, 1))
        z = [jnp.tanh(g) for g in (v[0], v[4], tz)]
        f = [sigmoid(g) for g in (v[1], v[5], tf)]
        o = [sigmoid(g) for g in (v[2], v[6], to)]
        at = now(t)
        ca = ca_t[r, at, :]
        gains, totals = [], []
        for q in range(3):
            zs[at, cols[q]] = z[q]
            fs[at, cols[q]] = f[q]
            os_[at, cols[q]] = o[q]
            gains.append(gain[q] * (f[q] * ca))
            totals.append(z[q] + f[q] * (ca * total[q] - z[q]))
        return tuple(gains), tuple(totals)

    def cell_step(r, t, state):
        cell, back, gain = state
        at = now(t)
        ca = ca_t[r, at, :]
        cells, backs, gains = [], [], []
        for q in range(3):
            z, f, o = zs[at, cols[q]], fs[at, cols[q]], os_[at, cols[q]]
            prev = ca * cell[q]
            cbs[at, cols[q]] = prev
            new = z + f * (prev - z)
            hs[q, pl.ds(t, SEGS, stride=sp), :] = o * new
            g = jnp.where(t == 0, one, gain[q] * (f * ca))
            cells.append(new)
            gains.append(g)
            backs.append(back[q] + g * (strided(ct, t, q) * o))
        return tuple(cells), tuple(backs), tuple(gains)

    def grad_step(r, i, later):
        t = steps - 1 - i
        at = now(t)
        ca = ca_t[r, at, :]
        gz, gf, go_, laters = [], [], [], []
        for q in range(3):
            z, f, o, prev = zs[at, cols[q]], fs[at, cols[q]], os_[at, cols[q]], cbs[at, cols[q]]
            c = strided(ct, t, q)
            dc = c * o + later[q]
            laters.append((f * ca) * dc)
            d = prev - z
            u = dc * (1.0 - f)
            gz.append(u * (1.0 - z * z))
            gf.append(u * (f * d))
            go_.append(c * (z + f * d) * (o * (1.0 - o)))
        z, f, o = gz[2], gf[2], go_[2]
        u = jnp.where(
            lane < tl,
            z,
            jnp.where(
                lane < 2 * tl,
                pltpu.roll(f, tl, 1),
                jnp.where(lane < 3 * tl, pltpu.roll(o, 2 * tl, 1), 0.0),
            ),
        )
        w = jnp.where(
            lane < tl,
            pltpu.roll(z, LANES - tl, 1),
            jnp.where(lane < 2 * tl, f, jnp.where(lane < 3 * tl, pltpu.roll(o, tl, 1), 0.0)),
        )
        for q, v in enumerate((gz[0], gf[0], go_[0], u, gz[1], gf[1], go_[1], w)):
            gp[q, pl.ds(t, SEGS, stride=sp), :] = v
        return tuple(laters)

    def scan(step, state, beside=None):
        if beside is None:
            return lax.fori_loop(0, steps, step, state, unroll=UNROLL)
        count = steps // TILES

        def body(i, state):
            beside(i)
            for u in range(count):
                state = step(i * count + u, state)
            return state

        return lax.fori_loop(0, TILES, body, state)

    def row(r):
        b = [jnp.broadcast_to(bb[0:1, q * LANES : (q + 1) * LANES], (SEGS, LANES)) for q in range(8)]
        inputs = weights = None
        if r > 0:
            nxt[...] = jnp.zeros_like(nxt)
            inputs, weights = functools.partial(input_tile, r - 1), functools.partial(weight_step, r - 1)
        gain, total = scan(functools.partial(gates_step, r, b), ((one,) * 3, (zero,) * 3), inputs)
        if r > 0:
            for copy in grad_copies(r - 1):
                copy.start()
            if r == 1 and not first:
                pltpu.make_async_copy(acc_in, accb, sem.at[2]).wait()
        for q in range(3):
            small[0, :, cols[q]] = gain[q]
            small[1, :, cols[q]] = total[q]
        run = jnp.zeros((1, 3 * LANES), f32)
        for s in range(SEGS):
            small[2, s : s + 1, :] = run
            run = small[0, s : s + 1, :] * run + small[1, s : s + 1, :]
        cell = tuple(small[2, :, cols[q]] for q in range(3))
        cell, back, gain = scan(functools.partial(cell_step, r), (cell, (zero,) * 3, (one,) * 3))
        for q in range(3):
            small[0, :, cols[q]] = back[q]
            small[1, :, cols[q]] = gain[q]
            small[3, :, cols[q]] = fs[0:SEGS, cols[q]] * ca_t[r, 0:SEGS, :]
        run = jnp.zeros((1, 3 * LANES), f32)
        for s in range(SEGS - 1, -1, -1):
            small[2, s : s + 1, :] = run
            run = small[3, s : s + 1, :] * (small[0, s : s + 1, :] + small[1, s : s + 1, :] * run)
        later = tuple(small[2, :, cols[q]] for q in range(3))
        scan(functools.partial(grad_step, r), later, weights)

    arrive(0)
    lax.fori_loop(0, D // rb, lambda i, _: (previous(0, i), 0)[1], 0)
    for r in range(1, rows):
        arrive(r)
    for copy in w_copies + b_copies:
        copy.wait()
    if first:
        go(wb, w_out, 0)
    else:
        go(acc_in, accb, 2)
    for r in range(rows):
        for copy in c_copies(r):
            copy.wait()

        def forward_step(i, _):
            forward(r, i)
            if r + 1 < rows:
                for j in range(D // rb * FTILE // n):
                    previous(r + 1, i * (D // rb * FTILE // n) + j)
            if r > 0:
                for j in range(FTILE // steps):
                    round_tile(r - 1, i * (FTILE // steps) + j)
            return 0

        lax.fori_loop(0, n // FTILE, forward_step, 0)
        if r > 0:
            for copy in hidden_copies(r - 1):
                copy.start()
        row(r)
    end = rows - 1
    nxt[...] = jnp.zeros_like(nxt)
    if end == 0 and not first:
        pltpu.make_async_copy(acc_in, accb, sem.at[2]).wait()

    def input_step(i, _):
        for j in range(TILE // steps):
            round_tile(end, (TILES - 1 - i) * (TILE // steps) + j)
        input_tile(end, i)
        return 0

    lax.fori_loop(0, TILES, input_step, 0)
    for copy in hidden_copies(end) + grad_copies(end):
        copy.start()
    for q in range(8):
        at = slice(q * LANES, (q + 1) * LANES)
        s = sums[:, at]
        if not first:
            s = s + accb[2 * D :, at]
        if last:
            s = jnp.sum(s, 0, keepdims=True)
            if q >= 4:
                ab[2 * D :, (q - 4) * LANES : (q - 3) * LANES] = in_two(s)
        accb[2 * D :, at] = jnp.broadcast_to(s, (SEGS, LANES))

    def own_copy(i):
        at = pl.ds(pl.multiple_of(i * TILE, TILE), TILE)
        return pltpu.make_async_copy(accb.at[:, at], (acc_own if last else acc_out).at[:, at], sem.at[4 + i])

    def sib_copy(i):
        at = pl.ds(pl.multiple_of(i * TILE, TILE), TILE)
        return pltpu.make_async_copy(ab.at[:, at], acc_sib.at[:, at], sem.at[2 + i])

    def own_step(i, _):
        v, at = weight_tile(end, i, not (first and rows == 1))
        accb[0 : 2 * D, at] = v
        own_copy(i).start()
        return 0

    def sib_step(i, _):
        v, _ = weight_tile(end, half // TILE + i, not (first and rows == 1))
        ab[0 : 2 * D, pl.ds(pl.multiple_of(i * TILE, TILE), TILE)] = v.astype(bf16)
        sib_copy(i).start()
        return 0

    own_tiles = (half if last else 2 * half) // TILE
    if last:
        lax.fori_loop(0, half // TILE, sib_step, 0)
    lax.fori_loop(0, own_tiles, own_step, 0)
    for i in range(own_tiles):
        own_copy(i).wait()
    if last:
        for i in range(half // TILE):
            sib_copy(i).wait()
    if first:
        pltpu.make_async_copy(wb, w_out, sem.at[0]).wait()
    for r in range(rows):
        for copy in hidden_copies(r) + grad_copies(r):
            copy.wait()


def layer(k, calls, rows, parts, C, n, tok, sib, cot, scot, ids, biases, x, w, acc, hid):
    first, last = k == 0, k == calls - 1
    D = 4 * C
    N = 8 * LANES
    T = rows * n
    shape = jax.ShapeDtypeStruct
    ins = [tok, sib, cot, scot, ids] + list(biases) + list(x)
    alias = {}
    outs = [shape(tok.shape, bf16), shape((2 * C, T), bf16)] + [shape((C, T), bf16)] * 3
    if first:
        ins += list(w)
    else:
        ins += [w, acc, hid]
        alias = {len(ins) - 1: 0}
        if not last:
            alias[len(ins) - 2] = 5
    if last:
        outs += [shape((2 * D + SEGS, N // 2), f32), shape((2 * D + 16, N // 2), bf16)]
    else:
        outs += [shape((2 * D + SEGS, N), f32)]
    if first:
        outs += [shape((2 * D, N), bf16)]
    w3 = 3 * LANES
    tall = n + SEGS * PAD
    scratch = (
        [
            pltpu.VMEM((2 * D, T), bf16),
            pltpu.VMEM((2 * D, N), bf16),
            pltpu.VMEM((w3, T), bf16),
            pltpu.VMEM((8, tall, LANES), f32),
            pltpu.VMEM((8, tall, LANES), f32),
        ]
        + [pltpu.VMEM((n, w3), f32)] * 4
        + [pltpu.VMEM((3, tall, LANES), f32)] * 2
        + [
            pltpu.VMEM((2 * C, T), bf16),
            pltpu.VMEM((T, N), bf16),
            pltpu.VMEM((D, T), bf16),
            pltpu.VMEM((2 * D + SEGS, N), f32),
            pltpu.VMEM((2 * D + 16, N // 2), bf16),
            pltpu.VMEM((4, SEGS, w3), f32),
            pltpu.VMEM((D, LANES), f32),
            pltpu.VMEM((SEGS, N), f32),
            pltpu.VMEM((rows, SEGS, n), f32),
            pltpu.VMEM((rows, n, LANES), f32),
            pltpu.VMEM((rows, SEGS, LANES), jnp.int32),
            pltpu.VMEM((SEGS, N), f32),
            pltpu.SemaphoreType.DMA((8 + 2 * parts,)),
            pltpu.SemaphoreType.DMA((rows, 18)),
        ]
    )
    return pl.pallas_call(
        functools.partial(layer_kernel, k, calls, rows, parts, C, n),
        out_shape=outs,
        in_specs=[ANY] * len(ins),
        out_specs=[ANY] * len(outs),
        scratch_shapes=scratch,
        input_output_aliases=alias,
        compiler_params=pltpu.CompilerParams(vmem_limit_bytes=60 << 20),
        cost_estimate=pl.CostEstimate(flops=1, bytes_accessed=1, transcendentals=0),
        name="layer",
    )(*ins)


def take_kernel(picks, n, tok, *refs):
    outs, (bufs, sem) = refs[:-2], refs[-2:]
    core = lax.axis_index("chan") & 1
    copies, sends = [], []
    for i, pick in enumerate(picks):
        for j, (pair, mine) in enumerate(pick):
            at = pl.ds(pl.multiple_of((2 * pair + (core if mine else 1 - core)) * n, n), n)
            copies.append(pltpu.make_async_copy(tok.at[:, at], bufs.at[i, :, j * n : (j + 1) * n], sem.at[i, j]))
            copies[-1].start()
    for i, pick in enumerate(picks):
        for copy in copies[i * len(pick) : (i + 1) * len(pick)]:
            copy.wait()
        sends.append(pltpu.make_async_copy(bufs.at[i], outs[i], sem.at[i, 0]))
        sends[-1].start()
    for send in sends:
        send.wait()


def take_rows(picks, C, n, tok):
    width = len(picks[0]) * n
    return pl.pallas_call(
        functools.partial(take_kernel, picks, n),
        out_shape=[jax.ShapeDtypeStruct((C, width), bf16)] * len(picks),
        in_specs=[ANY],
        out_specs=[ANY] * len(picks),
        scratch_shapes=[
            pltpu.VMEM((len(picks), C, width), bf16),
            pltpu.SemaphoreType.DMA((len(picks), len(picks[0]))),
        ],
        cost_estimate=pl.CostEstimate(flops=1, bytes_accessed=1, transcendentals=0),
        name="take",
    )(tok)


def pack_kernel(C, w, b, out, b_out):
    tail = C - LANES
    parts = [w[g, 0:LANES].astype(f32) for g in range(3)] + [w[g, LANES:C].astype(f32) for g in range(3)]
    parts.append(jnp.zeros((LANES - 3 * tail, w.shape[2]), f32))
    out[...] = jnp.concatenate(parts, 0).T.astype(bf16)
    b_out[...] = jnp.zeros_like(b_out)
    for g in range(3):
        b_out[0:1, g * LANES : (g + 1) * LANES] = b[g : g + 1, 0:LANES]
        b_out[0:1, 3 * LANES + g * tail : 3 * LANES + (g + 1) * tail] = b[g : g + 1, LANES:C]


def pack(C, w, b):
    return pl.pallas_call(
        functools.partial(pack_kernel, C),
        out_shape=[
            jax.ShapeDtypeStruct((w.shape[2], 4 * LANES), bf16),
            jax.ShapeDtypeStruct((SEGS, 4 * LANES), f32),
        ],
        in_specs=[VMEM] * 2,
        out_specs=[VMEM] * 2,
        cost_estimate=pl.CostEstimate(flops=1, bytes_accessed=1, transcendentals=0),
        name="pack",
    )(w, b)


def finish_kernel(k, rows, mine, C, n, near, far, *refs):
    total, sem = refs[-2:]
    if mine:
        grad = refs[-3]
    else:
        grad, hid = refs[-4:-2]
    core = lax.axis_index("chan") & 1
    which = core if mine else 1 - core
    copies = []

    def go(src, out, r):
        at = pl.ds(pl.multiple_of((2 * (k * rows + r) + which) * n, n), n)
        copies.append(pltpu.make_async_copy(src, out.at[:, at], sem.at[len(copies)]))
        copies[-1].start()

    for r in range(rows):
        at = slice(r * n, (r + 1) * n)
        if not mine:
            go(near.at[C : 2 * C, at], hid, r)
        total[:, at] = (near[0:C, at].astype(f32) + far[:, at].astype(f32)).astype(bf16)
        go(total.at[:, at], grad, r)
    for copy in copies:
        copy.wait()


def finish(k, rows, mine, C, n, total, near, far, grad, hid=None):
    ins = [near, far]
    specs = [VMEM] * 2
    shape = jax.ShapeDtypeStruct((C, total), bf16)
    outs = [shape]
    alias = {}
    for v in (grad, hid):
        if v is not None:
            alias[len(ins)] = 0 if v is grad else 1
            ins.append(v)
            specs.append(ANY)
    if hid is not None:
        outs.append(shape)
    return pl.pallas_call(
        functools.partial(finish_kernel, k, rows, mine, C, n),
        out_shape=outs,
        in_specs=specs,
        out_specs=[ANY] * len(outs),
        scratch_shapes=[pltpu.VMEM((C, rows * n), bf16), pltpu.SemaphoreType.DMA((2 * rows,))],
        input_output_aliases=alias,
        cost_estimate=pl.CostEstimate(flops=1, bytes_accessed=1, transcendentals=0),
        name="finish",
    )(*ins)


def in_two(v):
    high = v.astype(bf16)
    low = v - high.astype(f32)
    at = lax.broadcasted_iota(jnp.int32, (16, v.shape[1]), 0)
    return jnp.where(at == 0, high.astype(f32), jnp.where(at == 1, low, 0.0)).astype(bf16)


def from_two(v):
    v = v[...].astype(f32)
    return v[0:1] + v[1:2]


def split_kernel(C, own, other, s7, s3, s5, s2, k0, k1, k4, k6, bufs, kept, sem):
    place = lax.axis_index("dp")
    b = own[8 * C : 8 * C + 1, :] + from_two(other[8 * C :, :])
    two = in_two(b)
    copies = []
    for i, (j, out) in enumerate(((7, s7), (3, s3), (5, s5), (2, s2))):
        at = pl.ds(pl.multiple_of((place ^ j) * C, 32), C)
        bufs[i, 0:C] = (own[at, :] + other[at, :].astype(f32)).astype(bf16)
        bufs[i, C:] = two
        copies.append(pltpu.make_async_copy(bufs.at[i], out, sem.at[i]))
        copies[-1].start()
    for i, (j, out) in enumerate(((6, k6), (1, k1), (4, k4), (0, k0))):
        at = pl.ds(pl.multiple_of((place ^ j) * C, 32), C)
        kept[i, 0:C] = own[at, :] + other[at, :].astype(f32)
        kept[i, C : C + 8] = jnp.broadcast_to(b, (8, b.shape[1]))
        copies.append(pltpu.make_async_copy(kept.at[i, 0 : C + 8], out, sem.at[4 + i]))
        copies[-1].start()
    for copy in copies:
        copy.wait()


def split(C, own, other):
    half = own.shape[1]
    message = jax.ShapeDtypeStruct((C + 16, half), bf16)
    return pl.pallas_call(
        functools.partial(split_kernel, C),
        out_shape=[message] * 4 + [jax.ShapeDtypeStruct((C + 8, half), f32)] * 4,
        in_specs=[VMEM] * 2,
        out_specs=[HBM] * 8,
        scratch_shapes=[
            pltpu.VMEM((4, C + 16, half), bf16),
            pltpu.VMEM((4, C + 8, half), f32),
            pltpu.SemaphoreType.DMA((8,)),
        ],
        compiler_params=pltpu.CompilerParams(vmem_limit_bytes=62 << 20),
        cost_estimate=pl.CostEstimate(flops=1, bytes_accessed=1, transcendentals=0),
        name="split",
    )(own, other)


def second_kernel(C, k6, k1, r7, r3, s6, s1, bufs, sem):
    b = k6[C : C + 1]
    copies = []
    for i, (k, r, out) in enumerate(((k6, r7, s6), (k1, r3, s1))):
        bufs[i, 0:C] = (k[0:C] + r[0:C].astype(f32)).astype(bf16)
        bufs[i, C:] = in_two(b + from_two(r[C:]))
        copies.append(pltpu.make_async_copy(bufs.at[i], out, sem.at[i]))
        copies[-1].start()
    for copy in copies:
        copy.wait()


def second(C, k6, k1, r7, r3):
    message = jax.ShapeDtypeStruct(r7.shape, bf16)
    return pl.pallas_call(
        functools.partial(second_kernel, C),
        out_shape=[message] * 2,
        in_specs=[VMEM] * 4,
        out_specs=[HBM] * 2,
        scratch_shapes=[pltpu.VMEM((2,) + r7.shape, bf16), pltpu.SemaphoreType.DMA((2,))],
        cost_estimate=pl.CostEstimate(flops=1, bytes_accessed=1, transcendentals=0),
        name="second",
    )(k6, k1, r7, r3)


def third_kernel(C, k4, r5, r6, s4, buf, sem):
    buf[0:C] = (k4[0:C] + r5[0:C].astype(f32) + r6[0:C].astype(f32)).astype(bf16)
    buf[C:] = in_two(k4[C : C + 1] + from_two(r5[C:]) + from_two(r6[C:]))
    copy = pltpu.make_async_copy(buf, s4, sem)
    copy.start()
    copy.wait()


def third(C, k4, r5, r6):
    return pl.pallas_call(
        functools.partial(third_kernel, C),
        out_shape=jax.ShapeDtypeStruct(r6.shape, bf16),
        in_specs=[VMEM] * 3,
        out_specs=HBM,
        scratch_shapes=[pltpu.VMEM(r6.shape, bf16), pltpu.SemaphoreType.DMA],
        cost_estimate=pl.CostEstimate(flops=1, bytes_accessed=1, transcendentals=0),
        name="third",
    )(k4, r5, r6)


def total_kernel(C, k0, r2, r1, r4, grad, bias, buf, b_buf, sem):
    v = k0[0:C] + r2[0:C].astype(f32) + (r1[0:C].astype(f32) + r4[0:C].astype(f32))
    t = v.T
    tail = C - LANES
    b = k0[C : C + 1] + from_two(r2[C:]) + (from_two(r1[C:]) + from_two(r4[C:]))
    for g in range(3):
        buf[g, 0:LANES] = t[g * LANES : (g + 1) * LANES]
        buf[g, LANES:C] = t[3 * LANES + g * tail : 3 * LANES + (g + 1) * tail]
        b_buf[g : g + 1, 0:LANES] = b[:, g * LANES : (g + 1) * LANES]
        b_buf[g : g + 1, LANES:C] = b[:, 3 * LANES + g * tail : 3 * LANES + (g + 1) * tail]
    copies = [pltpu.make_async_copy(buf, grad, sem.at[0]), pltpu.make_async_copy(b_buf, bias, sem.at[1])]
    for copy in copies:
        copy.start()
    for copy in copies:
        copy.wait()


def total_sum(C, k0, r2, r1, r4):
    shapes = ((3, C, C), (3, C))
    return pl.pallas_call(
        functools.partial(total_kernel, C),
        out_shape=[jax.ShapeDtypeStruct(shape, f32) for shape in shapes],
        in_specs=[VMEM] * 4,
        out_specs=[HBM] * 2,
        scratch_shapes=[pltpu.VMEM(shape, f32) for shape in shapes] + [pltpu.SemaphoreType.DMA((2,))],
        cost_estimate=pl.CostEstimate(flops=1, bytes_accessed=1, transcendentals=0),
        name="total",
    )(k0, r2, r1, r4)


def local(chan, parts, tokens, weights, bias, segment_ids, cotangent):
    C, total = tokens.shape
    n = LEN
    pairs = total // n // 2
    rows = pairs // CALLS
    me = lax.axis_index("chan")
    core = me & 1

    def chan_move(v, j):
        return lax.ppermute(v, "chan", [(i, i ^ j) for i in range(chan)])

    def dp_move(v, j):
        return lax.ppermute(v, "dp", [(i, i ^ j) for i in range(parts)])

    def after(v, *others):
        return lax.optimization_barrier((v,) + others)[0]

    ids = segment_ids.reshape(2 * pairs * SEGS, n // SEGS)
    def other_rows(k, tok):
        picks = [[(k * rows + r, mine) for r in range(rows)] for mine in (True, False)]
        return take_rows(picks, C, n, tok)

    to_near, to_far = other_rows(0, tokens)
    near, far = chan_move(to_near, 2), chan_move(to_far, 3)
    xs = [(near, far)]
    shard, b_own = pack(C, after(weights, to_near), bias)
    sib = chan_move(tokens, 1)
    scot = chan_move(cotangent, 1)
    g = {0: shard, 4: dp_move(shard, 4), 1: dp_move(shard, 1)}
    def to_sibling(group):
        return chan_move(jnp.concatenate([g[j] for j in group], 0), 1)

    g4, own = lax.optimization_barrier((g[4], shard, sib))[:2]
    g[6] = dp_move(g4, 2)
    g[5] = dp_move(g4, 1)
    w_sib = [to_sibling(GROUPS[0])]
    biases = [b_own, chan_move(after(b_own, g[4]), 1)]
    g[2] = dp_move(own, 2)
    g6, g1 = lax.optimization_barrier((g[6], g[1], near, scot))[:2]
    g[7] = dp_move(g6, 1)
    g[3] = dp_move(g1, 2)
    w_sib.append(to_sibling(GROUPS[1]))
    g[3] = after(g[3], far)
    w_sib.append(to_sibling(GROUPS[2]))
    w = [g[j] for j in range(parts)] + w_sib
    for k in range(1, CALLS):
        to_near, to_far = other_rows(k, after(tokens, g[6]))
        xs.append((chan_move(to_near, 2), chan_move(to_far, 3)))

    acc = hid = grad = None
    moved = []
    for k in range(CALLS):
        out = layer(
            k, CALLS, rows, parts, C, n, tokens, sib, cotangent, scot, ids, biases, xs[k], w, acc, hid
        )
        if k == 0:
            w = out[-1]
        hid, to_sib, d_px, d_pd, own, acc = out[:6]
        if k == CALLS - 1:
            got = [v for m in moved for v in m[1:]]
            to_sib, d_px, d_pd, acc_sib = lax.optimization_barrier((to_sib, d_px, d_pd, out[6], *got))[:4]
            acc_sib = chan_move(acc_sib, 1)
        else:
            to_sib, d_px, d_pd = lax.optimization_barrier((to_sib, d_px, d_pd, *xs[k + 1]))[:3]
        moved.append((own, chan_move(d_px, 2), chan_move(to_sib, 1), chan_move(d_pd, 3)))

    def end(k, mine, *others):
        nonlocal grad, hid
        own, from_px, from_sib, from_pd = moved[k]
        if mine:
            (grad,) = finish(k, rows, True, C, n, total, after(own, *others), from_px, grad)
        else:
            grad, hid = finish(k, rows, False, C, n, total, after(from_sib, *others), from_pd, grad, hid)

    s7, s3, s5, s2, k0, k1, k4, k6 = split(C, acc, after(acc_sib, moved[-1][2]))
    r7, r3 = dp_move(s7, 1), dp_move(s3, 2)
    for k in range(CALLS - 1):
        end(k, True, s7)
    s6, s1 = second(C, k6, k1, r7, after(r3, grad))
    r5, r2 = dp_move(after(s5, r7), 1), dp_move(after(s2, r3), 2)
    r6, r1 = dp_move(s6, 2), dp_move(s1, 1)
    for k in range(CALLS - 1):
        end(k, False, s6)
    s4 = third(C, k4, r5, after(r6, grad, r1, r2))
    r4 = dp_move(s4, 4)
    end(CALLS - 1, True, s4)
    end(CALLS - 1, False, s4)
    weight_grad, bias_grad = total_sum(C, k0, r2, r1, after(r4, grad))
    return (hid, grad, weight_grad, bias_grad)


def combine(earlier, later):
    return (earlier[0] * later[0], later[0] * earlier[1] + later[1])


def local_any(tokens, weights, bias, segment_ids, cotangent):
    width_part, total_rows = tokens.shape
    batch_rows = total_rows // MICRO
    grad_shard = jnp.zeros(weights.shape, jnp.float32)
    bias_total = jnp.zeros(bias.shape, jnp.float32)
    position = jnp.arange(batch_rows) % LEN
    hidden_parts = []
    input_parts = []
    for micro in range(MICRO):
        lower = micro * batch_rows
        upper = lower + batch_rows
        part_in = tokens[:, lower:upper]
        ids = segment_ids[lower:upper]
        cot = cotangent[:, lower:upper].astype(jnp.float32)
        before = jnp.concatenate([ids[:1], ids[:-1]], 0)
        carry_flag = (position > 0) & (ids == before)
        carry_on = jnp.where(carry_flag, 1.0, 0.0).astype(jnp.float32)
        gathered = lax.all_gather(part_in, "chan", axis=0, tiled=True)
        width = gathered.shape[0]
        shifted = jnp.concatenate([jnp.zeros((width, 1), jnp.bfloat16), gathered[:, :-1]], 1)
        previous = jnp.where(carry_flag[None, :], shifted, jnp.zeros((), jnp.bfloat16))
        joined_inputs = jnp.concatenate([gathered, previous], 0)
        preactivation = jnp.einsum(
            "gcr,rl->gcl",
            lax.all_gather(weights, "dp", axis=2, tiled=True),
            joined_inputs,
            preferred_element_type=jnp.float32,
        )
        preactivation = preactivation + bias[:, :, None]
        gate_z = jnp.tanh(preactivation[0])
        forget = jax.nn.sigmoid(preactivation[1])
        output_gate = jax.nn.sigmoid(preactivation[2])
        decay = forget * carry_on[None, :]
        source = (1.0 - forget) * gate_z
        cell = lax.associative_scan(combine, (decay, source), axis=1)[1]
        hidden_parts.append((output_gate * cell).astype(jnp.bfloat16))
        decay_next = jnp.concatenate([decay[:, 1:], jnp.zeros((width_part, 1), jnp.float32)], 1)
        dcell = lax.associative_scan(combine, (decay_next, cot * output_gate), reverse=True, axis=1)[1]
        cell_before = (
            jnp.concatenate([jnp.zeros((width_part, 1), jnp.float32), cell[:, :-1]], 1)
            * carry_on[None, :]
        )
        grad_z = dcell * (1.0 - forget) * (1.0 - gate_z * gate_z)
        grad_f = dcell * (cell_before - gate_z) * forget * (1.0 - forget)
        grad_o = cot * cell * output_gate * (1.0 - output_gate)
        dpre_low = jnp.stack([grad_z, grad_f, grad_o], 0).astype(jnp.bfloat16)
        bias_total = bias_total + jnp.sum(dpre_low.astype(jnp.float32), axis=2)
        weight_term = jnp.einsum(
            "gcl,rl->gcr", dpre_low, joined_inputs, preferred_element_type=jnp.float32
        )
        djoined = jnp.einsum(
            "gcl,gcr->rl",
            dpre_low,
            lax.all_gather(weights, "dp", axis=2, tiled=True),
            preferred_element_type=jnp.float32,
        )
        later = djoined[width:] * carry_on[None, :]
        later = jnp.concatenate([later[:, 1:], jnp.zeros((width, 1), jnp.float32)], 1)
        term = djoined[:width] + later
        input_parts.append(
            lax.psum_scatter(term, "chan", scatter_dimension=0, tiled=True).astype(jnp.bfloat16)
        )
        grad_shard = grad_shard + lax.psum_scatter(weight_term, "dp", scatter_dimension=2, tiled=True)
    bias_grad = lax.psum(bias_total, "dp")
    hidden = jnp.concatenate(hidden_parts, 1)
    input_grad = jnp.concatenate(input_parts, 1)
    return (hidden, input_grad, grad_shard, bias_grad)


def solution(mesh):
    chan, parts = mesh.shape["chan"], mesh.shape["dp"]
    in_specs = (P("chan", "dp"), P(None, "chan", "dp"), P(None, "chan"), P("dp"), P("chan", "dp"))
    out_specs = (P("chan", "dp"), P("chan", "dp"), P(None, "chan", "dp"), P(None, "chan"))

    def run(tokens, weights, bias, segment_ids, cotangent):
        C = tokens.shape[0] // chan
        row_part = weights.shape[2] // parts
        pairs = tokens.shape[1] // parts % (2 * LEN * CALLS) == 0
        tail = C - LANES
        fits = chan == 4 and parts == 8 and row_part == C and pairs and 0 < 3 * tail < LANES and tail % 32 == 0
        body = functools.partial(local, chan, parts) if fits else local_any
        return jax.shard_map(body, mesh=mesh, in_specs=in_specs, out_specs=out_specs, check_vma=False)(
            tokens, weights, bias, segment_ids, cotangent
        )

    return run
```

```python
import functools

import jax
import jax.numpy as jnp
from jax import lax
from jax.experimental import pallas as pl
from jax.experimental.pallas import tpu as pltpu
from jax.sharding import PartitionSpec as P

LEN = 1024
MICRO = 4
LANES = 128
SEGS = 8
PAD = 8
TILE = 256
UNROLL = 16
FTILE = 1024
TILES = LEN // TILE
CALLS = 2
GROUPS = ((0, 1, 4), (2, 5, 6), (3, 7))
f32 = jnp.float32
bf16 = jnp.bfloat16
ANY = pl.BlockSpec(memory_space=pl.ANY)
VMEM = pl.BlockSpec(memory_space=pltpu.VMEM)
HBM = pl.BlockSpec(memory_space=pltpu.HBM)
SMEM = pl.BlockSpec(memory_space=pltpu.SMEM)


def dot(a, b, ca, cb):
    return lax.dot_general(a, b, (((ca,), (cb,)), ((), ())), preferred_element_type=f32)


def sigmoid(v):
    return 0.5 * jnp.tanh(0.5 * v) + 0.5


def layer_kernel(k, calls, rows, parts, C, n, *refs):
    first, last = k == 0, k == calls - 1
    refs = list(refs)
    tok, sib, cot, scot, ids, bias, bias_sib, x_near, x_far = refs[:9]
    refs = refs[9:]
    if first:
        w_in, refs = refs[: parts + len(GROUPS)], refs[parts + len(GROUPS) :]
    else:
        w_in, acc_in, refs = refs[0], refs[1], refs[3:]
    hid, to_sib, dx_px, dx_pd, dx_own = refs[:5]
    refs = refs[5:]
    if last:
        acc_own, acc_sib, refs = refs[0], refs[1], refs[2:]
    else:
        acc_out, refs = refs[0], refs[1:]
    if first:
        w_out, refs = refs[0], refs[1:]
    (xb, wb, cb, pre, gp, zs, fs, os_, cbs, ct, hs, hb, dp, dxb, accb, ab, small, nxt, sums, cl, ca_t, id_b, bb, sem, rsem) = refs
    D = 4 * C
    tl = C - LANES
    steps = n // SEGS
    sp = steps + PAD
    half = 4 * LANES
    me, place = lax.axis_index("chan"), lax.axis_index("dp")
    core = me & 1

    def go(src, dst, i):
        copy = pltpu.make_async_copy(src, dst, sem.at[i])
        copy.start()
        return copy

    def here(r):
        return pl.ds(pl.multiple_of((2 * (k * rows + r) + core) * n, n), n)

    def span(r):
        return pl.ds(pl.multiple_of(r * n, n), n)

    def block(j):
        return pl.ds(pl.multiple_of((me ^ j) * C, 32), C)

    def seg(h):
        return pl.ds(pl.multiple_of(h * sp, 8), steps)

    def id_rows(r):
        return pl.ds(pl.multiple_of((2 * (k * rows + r) + core) * SEGS, SEGS), SEGS)

    def x_copies(r):
        from_row = span(r)
        pairs = (
            (tok.at[:, here(r)], xb.at[block(0), span(r)]),
            (sib.at[:, here(r)], xb.at[block(1), span(r)]),
            (x_near.at[:, from_row], xb.at[block(2), span(r)]),
            (x_far.at[:, from_row], xb.at[block(3), span(r)]),
            (ids.at[id_rows(r)], id_b.at[r]),
        )
        return [pltpu.make_async_copy(a, b, rsem.at[r, i]) for i, (a, b) in enumerate(pairs)]

    def c_copies(r):
        pairs = (
            (cot.at[0:LANES, here(r)], cb.at[0:LANES, span(r)]),
            (scot.at[0:LANES, here(r)], cb.at[LANES : 2 * LANES, span(r)]),
            (cot.at[LANES:C, here(r)], cb.at[2 * LANES : 2 * LANES + tl, span(r)]),
            (scot.at[LANES:C, here(r)], cb.at[2 * LANES + tl : 2 * LANES + 2 * tl, span(r)]),
        )
        return [pltpu.make_async_copy(a, b, rsem.at[r, 5 + i]) for i, (a, b) in enumerate(pairs)]

    def hidden_copies(r):
        pairs = (
            (hb.at[0:LANES, span(r)], hid.at[0:LANES, here(r)]),
            (hb.at[LANES : 2 * LANES, span(r)], to_sib.at[C : C + LANES, span(r)]),
            (hb.at[2 * LANES : 2 * LANES + tl, span(r)], hid.at[LANES:C, here(r)]),
            (hb.at[2 * LANES + tl : 2 * LANES + 2 * tl, span(r)], to_sib.at[C + LANES : 2 * C, span(r)]),
        )
        return [pltpu.make_async_copy(a, b, rsem.at[r, 10 + i]) for i, (a, b) in enumerate(pairs)]

    def grad_copies(r):
        outs = (dx_own, to_sib.at[0:C], dx_px, dx_pd)
        return [
            pltpu.make_async_copy(dxb.at[block(j), span(r)], out.at[:, span(r)], rsem.at[r, 14 + j])
            for j, out in enumerate(outs)
        ]

    for copy in x_copies(0):
        copy.start()
    if first:
        w_copies = []
        for j in range(parts):
            at = pl.ds(pl.multiple_of((place ^ j) * C, 32), C)
            w_copies.append(go(w_in[j], wb.at[at, 0:half], 8 + j))
            which = [j in group for group in GROUPS].index(True)
            spot = GROUPS[which].index(j)
            other = w_in[parts + which].at[spot * C : (spot + 1) * C]
            w_copies.append(go(other, wb.at[at, half : 2 * half], 8 + parts + j))
    else:
        w_copies = [go(w_in, wb, 0)]
    b_copies = [go(bias, bb.at[:, 0:half], 1), go(bias_sib, bb.at[:, half : 2 * half], 3)]
    for r in range(rows):
        for copy in (x_copies(r) if r else []) + c_copies(r):
            copy.start()
    sums[...] = jnp.zeros_like(sums)
    lane = lax.broadcasted_iota(jnp.int32, (SEGS, LANES), 1)
    edge = lax.broadcasted_iota(jnp.int32, (D, LANES), 1) == LANES - 1
    cols = [slice(q * LANES, (q + 1) * LANES) for q in range(3)]
    one = jnp.ones((SEGS, LANES), f32)
    zero = jnp.zeros((SEGS, LANES), f32)

    def strided(ref, t, q):
        return ref[q, pl.ds(t, SEGS, stride=sp), :]

    def now(t):
        return pl.ds(pl.multiple_of(t * SEGS, SEGS), SEGS)

    def arrive(r):
        for copy in x_copies(r):
            copy.wait()
        seg_ids = id_b[r]
        before = pltpu.roll(seg_ids, 1, 1)
        before = jnp.where(lane == 0, pltpu.roll(before, 1, 0), before)
        sub = lax.broadcasted_iota(jnp.int32, (SEGS, steps), 0)
        carry = jnp.where((seg_ids == before) & ((lane > 0) | (sub > 0)), 1.0, 0.0).astype(f32)
        for s in range(SEGS):
            cl[r, :, s * steps : (s + 1) * steps] = jnp.broadcast_to(carry[s : s + 1, :], (SEGS, steps))
        for t in range(steps):
            ca_t[r, t * SEGS : (t + 1) * SEGS, :] = jnp.broadcast_to(carry[:, t : t + 1], (SEGS, LANES))

    rb = 32

    def previous(r, i):
        o = pl.multiple_of(i * rb, rb)
        v = xb[pl.ds(o, rb), span(r)].astype(f32)
        xb[pl.ds(D + o, rb), span(r)] = (pltpu.roll(v, 1, 1) * cl[r, 0:1, :]).astype(bf16)

    def forward(r, i):
        o = pl.multiple_of(r * n + i * FTILE, FTILE)
        v = dot(xb[:, pl.ds(o, FTILE)], wb[...], 0, 0)
        for h in range(FTILE // steps):
            at = seg(i * (FTILE // steps) + h)
            for q in range(8):
                pre[q, at, :] = v[h * steps : (h + 1) * steps, q * LANES : (q + 1) * LANES]
            c = cb[:, pl.ds(pl.multiple_of(o + h * steps, LANES), steps)].astype(f32).T
            for q in range(3):
                ct[q, at, :] = c[:, q * LANES : (q + 1) * LANES]

    def round_tile(r, i):
        into = pl.ds(pl.multiple_of(r * n + i * steps, LANES), steps)
        for q in range(8):
            v = gp[q, seg(i), :].astype(bf16)
            dp[into, q * LANES : (q + 1) * LANES] = v
            v = v.astype(f32)
            a = v[0:SEGS]
            for s in range(SEGS, steps, SEGS):
                a = a + v[s : s + SEGS]
            sums[:, q * LANES : (q + 1) * LANES] += a
        for q in range(3):
            e = LANES if q < 2 else 2 * tl
            hb[q * LANES : q * LANES + e, into] = hs[q, seg(i), :].T.astype(bf16)[0:e]

    def input_tile(r, i):
        i = n // TILE - 1 - i
        o = pl.multiple_of(i * TILE, TILE)
        dj = dot(wb[...], dp[pl.ds(pl.multiple_of(r * n + o, TILE), TILE), :], 1, 1)
        after = nxt[...]
        for h in range(TILE // LANES - 1, -1, -1):
            at = slice(h * LANES, (h + 1) * LANES)
            into = pl.ds(pl.multiple_of(r * n + o + h * LANES, LANES), LANES)
            rolled = pltpu.roll(
                dj[D:, at] * cl[r, 0:1, pl.ds(pl.multiple_of(o + h * LANES, LANES), LANES)], LANES - 1, 1
            )
            dxb[:, into] = (dj[:D, at] + jnp.where(edge, after, rolled)).astype(bf16)
            after = rolled
        nxt[...] = after

    def weight_tile(r, i, add):
        at = pl.ds(pl.multiple_of(i * TILE, TILE), TILE)
        v = dot(xb[:, span(r)], dp[span(r), at], 1, 0)
        return (v + accb[0 : 2 * D, at] if add else v), at

    def weight_step(r, i):
        v, at = weight_tile(r, i, not (first and r == 0))
        accb[0 : 2 * D, at] = v

    def gates_step(r, b, t, state):
        gain, total = state
        v = [strided(pre, t, q) + b[q] for q in range(8)]
        u, w = v[3], v[7]
        tz = jnp.where(lane < tl, u, pltpu.roll(w, tl, 1))
        tf = jnp.where(lane < tl, pltpu.roll(u, LANES - tl, 1), w)
        to = jnp.where(lane < tl, pltpu.roll(u, LANES - 2 * tl, 1), pltpu.roll(w, LANES - tl, 1))
        z = [jnp.tanh(g) for g in (v[0], v[4], tz)]
        f = [sigmoid(g) for g in (v[1], v[5], tf)]
        o = [sigmoid(g) for g in (v[2], v[6], to)]
        at = now(t)
        ca = ca_t[r, at, :]
        gains, totals = [], []
        for q in range(3):
            zs[at, cols[q]] = z[q]
            fs[at, cols[q]] = f[q]
            os_[at, cols[q]] = o[q]
            gains.append(gain[q] * (f[q] * ca))
            totals.append(z[q] + f[q] * (ca * total[q] - z[q]))
        return tuple(gains), tuple(totals)

    def cell_step(r, t, state):
        cell, back, gain = state
        at = now(t)
        ca = ca_t[r, at, :]
        cells, backs, gains = [], [], []
        for q in range(3):
            z, f, o = zs[at, cols[q]], fs[at, cols[q]], os_[at, cols[q]]
            prev = ca * cell[q]
            cbs[at, cols[q]] = prev
            new = z + f * (prev - z)
            hs[q, pl.ds(t, SEGS, stride=sp), :] = o * new
            g = jnp.where(t == 0, one, gain[q] * (f * ca))
            cells.append(new)
            gains.append(g)
            backs.append(back[q] + g * (strided(ct, t, q) * o))
        return tuple(cells), tuple(backs), tuple(gains)

    def grad_step(r, i, later):
        t = steps - 1 - i
        at = now(t)
        ca = ca_t[r, at, :]
        gz, gf, go_, laters = [], [], [], []
        for q in range(3):
            z, f, o, prev = zs[at, cols[q]], fs[at, cols[q]], os_[at, cols[q]], cbs[at, cols[q]]
            c = strided(ct, t, q)
            dc = c * o + later[q]
            laters.append((f * ca) * dc)
            d = prev - z
            u = dc * (1.0 - f)
            gz.append(u * (1.0 - z * z))
            gf.append(u * (f * d))
            go_.append(c * (z + f * d) * (o * (1.0 - o)))
        z, f, o = gz[2], gf[2], go_[2]
        u = jnp.where(
            lane < tl,
            z,
            jnp.where(
                lane < 2 * tl,
                pltpu.roll(f, tl, 1),
                jnp.where(lane < 3 * tl, pltpu.roll(o, 2 * tl, 1), 0.0),
            ),
        )
        w = jnp.where(
            lane < tl,
            pltpu.roll(z, LANES - tl, 1),
            jnp.where(lane < 2 * tl, f, jnp.where(lane < 3 * tl, pltpu.roll(o, tl, 1), 0.0)),
        )
        for q, v in enumerate((gz[0], gf[0], go_[0], u, gz[1], gf[1], go_[1], w)):
            gp[q, pl.ds(t, SEGS, stride=sp), :] = v
        return tuple(laters)

    def scan(step, state, beside=None):
        if beside is None:
            return lax.fori_loop(0, steps, step, state, unroll=UNROLL)
        count = steps // TILES

        def body(i, state):
            beside(i)
            for u in range(count):
                state = step(i * count + u, state)
            return state

        return lax.fori_loop(0, TILES, body, state)

    def row(r):
        b = [jnp.broadcast_to(bb[0:1, q * LANES : (q + 1) * LANES], (SEGS, LANES)) for q in range(8)]
        inputs = weights = None
        if r > 0:
            nxt[...] = jnp.zeros_like(nxt)
            inputs, weights = functools.partial(input_tile, r - 1), functools.partial(weight_step, r - 1)
        gain, total = scan(functools.partial(gates_step, r, b), ((one,) * 3, (zero,) * 3), inputs)
        if r > 0:
            for copy in grad_copies(r - 1):
                copy.start()
            if r == 1 and not first:
                pltpu.make_async_copy(acc_in, accb, sem.at[2]).wait()
        for q in range(3):
            small[0, :, cols[q]] = gain[q]
            small[1, :, cols[q]] = total[q]
        run = jnp.zeros((1, 3 * LANES), f32)
        for s in range(SEGS):
            small[2, s : s + 1, :] = run
            run = small[0, s : s + 1, :] * run + small[1, s : s + 1, :]
        cell = tuple(small[2, :, cols[q]] for q in range(3))
        cell, back, gain = scan(functools.partial(cell_step, r), (cell, (zero,) * 3, (one,) * 3))
        for q in range(3):
            small[0, :, cols[q]] = back[q]
            small[1, :, cols[q]] = gain[q]
            small[3, :, cols[q]] = fs[0:SEGS, cols[q]] * ca_t[r, 0:SEGS, :]
        run = jnp.zeros((1, 3 * LANES), f32)
        for s in range(SEGS - 1, -1, -1):
            small[2, s : s + 1, :] = run
            run = small[3, s : s + 1, :] * (small[0, s : s + 1, :] + small[1, s : s + 1, :] * run)
        later = tuple(small[2, :, cols[q]] for q in range(3))
        scan(functools.partial(grad_step, r), later, weights)

    arrive(0)
    lax.fori_loop(0, D // rb, lambda i, _: (previous(0, i), 0)[1], 0)
    for r in range(1, rows):
        arrive(r)
    for copy in w_copies + b_copies:
        copy.wait()
    if first:
        go(wb, w_out, 0)
    else:
        go(acc_in, accb, 2)
    for r in range(rows):
        for copy in c_copies(r):
            copy.wait()

        def forward_step(i, _):
            forward(r, i)
            if r + 1 < rows:
                for j in range(D // rb * FTILE // n):
                    previous(r + 1, i * (D // rb * FTILE // n) + j)
            if r > 0:
                for j in range(FTILE // steps):
                    round_tile(r - 1, i * (FTILE // steps) + j)
            return 0

        lax.fori_loop(0, n // FTILE, forward_step, 0)
        if r > 0:
            for copy in hidden_copies(r - 1):
                copy.start()
        row(r)
    end = rows - 1
    nxt[...] = jnp.zeros_like(nxt)
    if end == 0 and not first:
        pltpu.make_async_copy(acc_in, accb, sem.at[2]).wait()

    def input_step(i, _):
        for j in range(TILE // steps):
            round_tile(end, (TILES - 1 - i) * (TILE // steps) + j)
        input_tile(end, i)
        return 0

    lax.fori_loop(0, TILES, input_step, 0)
    for copy in hidden_copies(end) + grad_copies(end):
        copy.start()
    for q in range(8):
        at = slice(q * LANES, (q + 1) * LANES)
        s = sums[:, at]
        if not first:
            s = s + accb[2 * D :, at]
        if last:
            s = jnp.sum(s, 0, keepdims=True)
            if q >= 4:
                ab[2 * D :, (q - 4) * LANES : (q - 3) * LANES] = in_two(s)
        accb[2 * D :, at] = jnp.broadcast_to(s, (SEGS, LANES))

    def own_copy(i):
        at = pl.ds(pl.multiple_of(i * TILE, TILE), TILE)
        return pltpu.make_async_copy(accb.at[:, at], (acc_own if last else acc_out).at[:, at], sem.at[4 + i])

    def sib_copy(i):
        at = pl.ds(pl.multiple_of(i * TILE, TILE), TILE)
        return pltpu.make_async_copy(ab.at[:, at], acc_sib.at[:, at], sem.at[2 + i])

    def own_step(i, _):
        v, at = weight_tile(end, i, not (first and rows == 1))
        accb[0 : 2 * D, at] = v
        own_copy(i).start()
        return 0

    def sib_step(i, _):
        v, _ = weight_tile(end, half // TILE + i, not (first and rows == 1))
        ab[0 : 2 * D, pl.ds(pl.multiple_of(i * TILE, TILE), TILE)] = v.astype(bf16)
        sib_copy(i).start()
        return 0

    own_tiles = (half if last else 2 * half) // TILE
    if last:
        lax.fori_loop(0, half // TILE, sib_step, 0)
    lax.fori_loop(0, own_tiles, own_step, 0)
    for i in range(own_tiles):
        own_copy(i).wait()
    if last:
        for i in range(half // TILE):
            sib_copy(i).wait()
    if first:
        pltpu.make_async_copy(wb, w_out, sem.at[0]).wait()
    for r in range(rows):
        for copy in hidden_copies(r) + grad_copies(r):
            copy.wait()


def layer(k, calls, rows, parts, C, n, tok, sib, cot, scot, ids, biases, x, w, acc, hid):
    first, last = k == 0, k == calls - 1
    D = 4 * C
    N = 8 * LANES
    T = rows * n
    shape = jax.ShapeDtypeStruct
    ins = [tok, sib, cot, scot, ids] + list(biases) + list(x)
    alias = {}
    outs = [shape(tok.shape, bf16), shape((2 * C, T), bf16)] + [shape((C, T), bf16)] * 3
    if first:
        ins += list(w)
    else:
        ins += [w, acc, hid]
        alias = {len(ins) - 1: 0}
        if not last:
            alias[len(ins) - 2] = 5
    if last:
        outs += [shape((2 * D + SEGS, N // 2), f32), shape((2 * D + SEGS, N // 2), bf16)]
    else:
        outs += [shape((2 * D + SEGS, N), f32)]
    if first:
        outs += [shape((2 * D, N), bf16)]
    w3 = 3 * LANES
    tall = n + SEGS * PAD
    scratch = (
        [
            pltpu.VMEM((2 * D, T), bf16),
            pltpu.VMEM((2 * D, N), bf16),
            pltpu.VMEM((w3, T), bf16),
            pltpu.VMEM((8, tall, LANES), f32),
            pltpu.VMEM((8, tall, LANES), f32),
        ]
        + [pltpu.VMEM((n, w3), f32)] * 4
        + [pltpu.VMEM((3, tall, LANES), f32)] * 2
        + [
            pltpu.VMEM((2 * C, T), bf16),
            pltpu.VMEM((T, N), bf16),
            pltpu.VMEM((D, T), bf16),
            pltpu.VMEM((2 * D + SEGS, N), f32),
            pltpu.VMEM((2 * D + SEGS, N // 2), bf16),
            pltpu.VMEM((4, SEGS, w3), f32),
            pltpu.VMEM((D, LANES), f32),
            pltpu.VMEM((SEGS, N), f32),
            pltpu.VMEM((rows, SEGS, n), f32),
            pltpu.VMEM((rows, n, LANES), f32),
            pltpu.VMEM((rows, SEGS, LANES), jnp.int32),
            pltpu.VMEM((SEGS, N), f32),
            pltpu.SemaphoreType.DMA((8 + 2 * parts,)),
            pltpu.SemaphoreType.DMA((rows, 18)),
        ]
    )
    return pl.pallas_call(
        functools.partial(layer_kernel, k, calls, rows, parts, C, n),
        out_shape=outs,
        in_specs=[ANY] * len(ins),
        out_specs=[ANY] * len(outs),
        scratch_shapes=scratch,
        input_output_aliases=alias,
        compiler_params=pltpu.CompilerParams(vmem_limit_bytes=60 << 20),
        cost_estimate=pl.CostEstimate(flops=1, bytes_accessed=1, transcendentals=0),
        name="layer",
    )(*ins)


def take_kernel(picks, n, tok, *refs):
    outs, (bufs, sem) = refs[:-2], refs[-2:]
    core = lax.axis_index("chan") & 1
    copies, sends = [], []
    for i, pick in enumerate(picks):
        for j, (pair, mine) in enumerate(pick):
            at = pl.ds(pl.multiple_of((2 * pair + (core if mine else 1 - core)) * n, n), n)
            copies.append(pltpu.make_async_copy(tok.at[:, at], bufs.at[i, :, j * n : (j + 1) * n], sem.at[i, j]))
            copies[-1].start()
    for i, pick in enumerate(picks):
        for copy in copies[i * len(pick) : (i + 1) * len(pick)]:
            copy.wait()
        sends.append(pltpu.make_async_copy(bufs.at[i], outs[i], sem.at[i, 0]))
        sends[-1].start()
    for send in sends:
        send.wait()


def take_rows(picks, C, n, tok):
    width = len(picks[0]) * n
    return pl.pallas_call(
        functools.partial(take_kernel, picks, n),
        out_shape=[jax.ShapeDtypeStruct((C, width), bf16)] * len(picks),
        in_specs=[ANY],
        out_specs=[ANY] * len(picks),
        scratch_shapes=[
            pltpu.VMEM((len(picks), C, width), bf16),
            pltpu.SemaphoreType.DMA((len(picks), len(picks[0]))),
        ],
        compiler_params=pltpu.CompilerParams(vmem_limit_bytes=8 << 20),
        cost_estimate=pl.CostEstimate(flops=1, bytes_accessed=1, transcendentals=0),
        name="take",
    )(tok)


def pack_kernel(C, w, b, out, b_out):
    tail = C - LANES
    parts = [w[g, 0:LANES].astype(f32) for g in range(3)] + [w[g, LANES:C].astype(f32) for g in range(3)]
    parts.append(jnp.zeros((LANES - 3 * tail, w.shape[2]), f32))
    out[...] = jnp.concatenate(parts, 0).T.astype(bf16)
    b_out[...] = jnp.zeros_like(b_out)
    for g in range(3):
        b_out[0:1, g * LANES : (g + 1) * LANES] = b[g : g + 1, 0:LANES]
        b_out[0:1, 3 * LANES + g * tail : 3 * LANES + (g + 1) * tail] = b[g : g + 1, LANES:C]


def pack(C, w, b):
    return pl.pallas_call(
        functools.partial(pack_kernel, C),
        out_shape=[
            jax.ShapeDtypeStruct((w.shape[2], 4 * LANES), bf16),
            jax.ShapeDtypeStruct((SEGS, 4 * LANES), f32),
        ],
        in_specs=[VMEM] * 2,
        out_specs=[VMEM] * 2,
        compiler_params=pltpu.CompilerParams(vmem_limit_bytes=4 << 20),
        cost_estimate=pl.CostEstimate(flops=1, bytes_accessed=1, transcendentals=0),
        name="pack",
    )(w, b)


def finish_kernel(k, rows, mine, C, n, near, far, *refs):
    total, sem = refs[-2:]
    if mine:
        grad = refs[-3]
    else:
        grad, hid = refs[-4:-2]
    core = lax.axis_index("chan") & 1
    which = core if mine else 1 - core
    copies = []

    def go(src, out, r):
        at = pl.ds(pl.multiple_of((2 * (k * rows + r) + which) * n, n), n)
        copies.append(pltpu.make_async_copy(src, out.at[:, at], sem.at[len(copies)]))
        copies[-1].start()

    for r in range(rows):
        at = slice(r * n, (r + 1) * n)
        if not mine:
            go(near.at[C : 2 * C, at], hid, r)
        total[:, at] = (near[0:C, at].astype(f32) + far[:, at].astype(f32)).astype(bf16)
        go(total.at[:, at], grad, r)
    for copy in copies:
        copy.wait()


def finish(k, rows, mine, C, n, total, near, far, grad, hid=None):
    ins = [near, far]
    specs = [VMEM] * 2
    shape = jax.ShapeDtypeStruct((C, total), bf16)
    outs = [shape]
    alias = {}
    for v in (grad, hid):
        if v is not None:
            alias[len(ins)] = 0 if v is grad else 1
            ins.append(v)
            specs.append(ANY)
    if hid is not None:
        outs.append(shape)
    return pl.pallas_call(
        functools.partial(finish_kernel, k, rows, mine, C, n),
        out_shape=outs,
        in_specs=specs,
        out_specs=[ANY] * len(outs),
        scratch_shapes=[pltpu.VMEM((C, rows * n), bf16), pltpu.SemaphoreType.DMA((2 * rows,))],
        input_output_aliases=alias,
        compiler_params=pltpu.CompilerParams(vmem_limit_bytes=8 << 20),
        cost_estimate=pl.CostEstimate(flops=1, bytes_accessed=1, transcendentals=0),
        name="finish",
    )(*ins)


def in_two(v):
    high = v.astype(bf16)
    low = v - high.astype(f32)
    at = lax.broadcasted_iota(jnp.int32, (SEGS, v.shape[1]), 0)
    return jnp.where(at == 0, high.astype(f32), jnp.where(at == 1, low, 0.0)).astype(bf16)


def from_two(v):
    v = v[...].astype(f32)
    return v[0:1] + v[1:2]


def split_kernel(C, own, other, s7, s3, s5, s2, k0, k1, k4, k6, bufs, kept, sem):
    place = lax.axis_index("dp")
    b = own[8 * C : 8 * C + 1, :] + from_two(other[8 * C :, :])
    two = in_two(b)
    copies = []
    for i, (j, out) in enumerate(((7, s7), (3, s3), (5, s5), (2, s2))):
        at = pl.ds(pl.multiple_of((place ^ j) * C, 32), C)
        bufs[i, 0:C] = (own[at, :] + other[at, :].astype(f32)).astype(bf16)
        bufs[i, C:] = two
        copies.append(pltpu.make_async_copy(bufs.at[i], out, sem.at[i]))
        copies[-1].start()
    for i, (j, out) in enumerate(((6, k6), (1, k1), (4, k4), (0, k0))):
        at = pl.ds(pl.multiple_of((place ^ j) * C, 32), C)
        kept[i, 0:C] = own[at, :] + other[at, :].astype(f32)
        kept[i, C : C + 8] = jnp.broadcast_to(b, (8, b.shape[1]))
        copies.append(pltpu.make_async_copy(kept.at[i, 0 : C + 8], out, sem.at[4 + i]))
        copies[-1].start()
    for copy in copies:
        copy.wait()


def split(C, own, other):
    half = own.shape[1]
    message = jax.ShapeDtypeStruct((C + SEGS, half), bf16)
    return pl.pallas_call(
        functools.partial(split_kernel, C),
        out_shape=[message] * 4 + [jax.ShapeDtypeStruct((C + 8, half), f32)] * 4,
        in_specs=[VMEM] * 2,
        out_specs=[HBM] * 8,
        scratch_shapes=[
            pltpu.VMEM((4, C + SEGS, half), bf16),
            pltpu.VMEM((4, C + 8, half), f32),
            pltpu.SemaphoreType.DMA((8,)),
        ],
        compiler_params=pltpu.CompilerParams(vmem_limit_bytes=16 << 20),
        cost_estimate=pl.CostEstimate(flops=1, bytes_accessed=1, transcendentals=0),
        name="split",
    )(own, other)


def second_kernel(C, k6, k1, r7, r3, s6, s1, bufs, sem):
    b = k6[C : C + 1]
    copies = []
    for i, (k, r, out) in enumerate(((k6, r7, s6), (k1, r3, s1))):
        bufs[i, 0:C] = (k[0:C] + r[0:C].astype(f32)).astype(bf16)
        bufs[i, C:] = in_two(b + from_two(r[C:]))
        copies.append(pltpu.make_async_copy(bufs.at[i], out, sem.at[i]))
        copies[-1].start()
    for copy in copies:
        copy.wait()


def second(C, k6, k1, r7, r3):
    message = jax.ShapeDtypeStruct(r7.shape, bf16)
    return pl.pallas_call(
        functools.partial(second_kernel, C),
        out_shape=[message] * 2,
        in_specs=[VMEM] * 4,
        out_specs=[HBM] * 2,
        scratch_shapes=[pltpu.VMEM((2,) + r7.shape, bf16), pltpu.SemaphoreType.DMA((2,))],
        compiler_params=pltpu.CompilerParams(vmem_limit_bytes=4 << 20),
        cost_estimate=pl.CostEstimate(flops=1, bytes_accessed=1, transcendentals=0),
        name="second",
    )(k6, k1, r7, r3)


def third_kernel(C, k4, r5, r6, s4, buf, sem):
    buf[0:C] = (k4[0:C] + r5[0:C].astype(f32) + r6[0:C].astype(f32)).astype(bf16)
    buf[C:] = in_two(k4[C : C + 1] + from_two(r5[C:]) + from_two(r6[C:]))
    copy = pltpu.make_async_copy(buf, s4, sem)
    copy.start()
    copy.wait()


def third(C, k4, r5, r6):
    return pl.pallas_call(
        functools.partial(third_kernel, C),
        out_shape=jax.ShapeDtypeStruct(r6.shape, bf16),
        in_specs=[VMEM] * 3,
        out_specs=HBM,
        scratch_shapes=[pltpu.VMEM(r6.shape, bf16), pltpu.SemaphoreType.DMA],
        compiler_params=pltpu.CompilerParams(vmem_limit_bytes=4 << 20),
        cost_estimate=pl.CostEstimate(flops=1, bytes_accessed=1, transcendentals=0),
        name="third",
    )(k4, r5, r6)


def total_kernel(C, k0, r2, r1, r4, grad, bias, buf, b_buf, sem):
    v = k0[0:C] + r2[0:C].astype(f32) + (r1[0:C].astype(f32) + r4[0:C].astype(f32))
    t = v.T
    tail = C - LANES
    b = k0[C : C + 1] + from_two(r2[C:]) + (from_two(r1[C:]) + from_two(r4[C:]))
    for g in range(3):
        buf[g, 0:LANES] = t[g * LANES : (g + 1) * LANES]
        buf[g, LANES:C] = t[3 * LANES + g * tail : 3 * LANES + (g + 1) * tail]
        b_buf[g : g + 1, 0:LANES] = b[:, g * LANES : (g + 1) * LANES]
        b_buf[g : g + 1, LANES:C] = b[:, 3 * LANES + g * tail : 3 * LANES + (g + 1) * tail]
    copies = [pltpu.make_async_copy(buf, grad, sem.at[0]), pltpu.make_async_copy(b_buf, bias, sem.at[1])]
    for copy in copies:
        copy.start()
    for copy in copies:
        copy.wait()


def total_sum(C, k0, r2, r1, r4):
    shapes = ((3, C, C), (3, C))
    return pl.pallas_call(
        functools.partial(total_kernel, C),
        out_shape=[jax.ShapeDtypeStruct(shape, f32) for shape in shapes],
        in_specs=[VMEM] * 4,
        out_specs=[HBM] * 2,
        scratch_shapes=[pltpu.VMEM(shape, f32) for shape in shapes] + [pltpu.SemaphoreType.DMA((2,))],
        compiler_params=pltpu.CompilerParams(vmem_limit_bytes=4 << 20),
        cost_estimate=pl.CostEstimate(flops=1, bytes_accessed=1, transcendentals=0),
        name="total",
    )(k0, r2, r1, r4)


def local(chan, parts, tokens, weights, bias, segment_ids, cotangent):
    C, total = tokens.shape
    n = LEN
    pairs = total // n // 2
    rows = pairs // CALLS
    me = lax.axis_index("chan")
    core = me & 1

    def chan_move(v, j):
        return lax.ppermute(v, "chan", [(i, i ^ j) for i in range(chan)])

    def dp_move(v, j):
        return lax.ppermute(v, "dp", [(i, i ^ j) for i in range(parts)])

    def after(v, *others):
        return lax.optimization_barrier((v,) + others)[0]

    ids = segment_ids.reshape(2 * pairs * SEGS, n // SEGS)
    def other_rows(k, tok):
        picks = [[(k * rows + r, mine) for r in range(rows)] for mine in (True, False)]
        return take_rows(picks, C, n, tok)

    to_near, to_far = other_rows(0, tokens)
    near, far = chan_move(to_near, 2), chan_move(to_far, 3)
    xs = [(near, far)]
    shard, b_own = pack(C, after(weights, to_near), bias)
    sib = chan_move(tokens, 1)
    scot = chan_move(cotangent, 1)
    g = {0: shard, 4: dp_move(shard, 4), 1: dp_move(shard, 1)}
    def to_sibling(group):
        return chan_move(jnp.concatenate([g[j] for j in group], 0), 1)

    g4, own = lax.optimization_barrier((g[4], shard, sib))[:2]
    g[6] = dp_move(g4, 2)
    g[5] = dp_move(g4, 1)
    w_sib = [to_sibling(GROUPS[0])]
    biases = [b_own, chan_move(after(b_own, g[4]), 1)]
    g[2] = dp_move(own, 2)
    g6, g1 = lax.optimization_barrier((g[6], g[1], near, scot))[:2]
    g[7] = dp_move(g6, 1)
    g[3] = dp_move(g1, 2)
    w_sib.append(to_sibling(GROUPS[1]))
    g[3] = after(g[3], far)
    w_sib.append(to_sibling(GROUPS[2]))
    w = [g[j] for j in range(parts)] + w_sib
    for k in range(1, CALLS):
        to_near, to_far = other_rows(k, after(tokens, g[6]))
        xs.append((chan_move(to_near, 2), chan_move(to_far, 3)))

    acc = hid = grad = None
    moved = []
    for k in range(CALLS):
        out = layer(
            k, CALLS, rows, parts, C, n, tokens, sib, cotangent, scot, ids, biases, xs[k], w, acc, hid
        )
        if k == 0:
            w = out[-1]
        hid, to_sib, d_px, d_pd, own, acc = out[:6]
        if k == CALLS - 1:
            got = [v for m in moved for v in m[1:]]
            to_sib, d_px, d_pd, acc_sib = lax.optimization_barrier((to_sib, d_px, d_pd, out[6], *got))[:4]
            acc_sib = chan_move(acc_sib, 1)
        else:
            to_sib, d_px, d_pd = lax.optimization_barrier((to_sib, d_px, d_pd, *xs[k + 1]))[:3]
        moved.append((own, chan_move(d_px, 2), chan_move(to_sib, 1), chan_move(d_pd, 3)))

    def end(k, mine, *others):
        nonlocal grad, hid
        own, from_px, from_sib, from_pd = moved[k]
        if mine:
            (grad,) = finish(k, rows, True, C, n, total, after(own, *others), from_px, grad)
        else:
            grad, hid = finish(k, rows, False, C, n, total, after(from_sib, *others), from_pd, grad, hid)

    s7, s3, s5, s2, k0, k1, k4, k6 = split(C, acc, after(acc_sib, moved[-1][2]))
    r7, r3, r5 = dp_move(s7, 1), dp_move(s3, 2), dp_move(s5, 1)
    for k in range(CALLS - 1):
        end(k, True, s7)
    s6, s1 = second(C, k6, k1, r7, after(r3, grad))
    r6, r1, r2 = dp_move(s6, 2), dp_move(s1, 1), dp_move(after(s2, r3), 2)
    for k in range(CALLS - 1):
        end(k, False, s6, r5)
    s4 = third(C, k4, r5, after(r6, grad, r1, r2))
    r4 = dp_move(s4, 4)
    end(CALLS - 1, True, s4)
    end(CALLS - 1, False, s4)
    weight_grad, bias_grad = total_sum(C, k0, r2, r1, after(r4, grad))
    return (hid, grad, weight_grad, bias_grad)


def combine(earlier, later):
    return (earlier[0] * later[0], later[0] * earlier[1] + later[1])


def local_any(tokens, weights, bias, segment_ids, cotangent):
    width_part, total_rows = tokens.shape
    batch_rows = total_rows // MICRO
    grad_shard = jnp.zeros(weights.shape, jnp.float32)
    bias_total = jnp.zeros(bias.shape, jnp.float32)
    position = jnp.arange(batch_rows) % LEN
    hidden_parts = []
    input_parts = []
    for micro in range(MICRO):
        lower = micro * batch_rows
        upper = lower + batch_rows
        part_in = tokens[:, lower:upper]
        ids = segment_ids[lower:upper]
        cot = cotangent[:, lower:upper].astype(jnp.float32)
        before = jnp.concatenate([ids[:1], ids[:-1]], 0)
        carry_flag = (position > 0) & (ids == before)
        carry_on = jnp.where(carry_flag, 1.0, 0.0).astype(jnp.float32)
        gathered = lax.all_gather(part_in, "chan", axis=0, tiled=True)
        width = gathered.shape[0]
        shifted = jnp.concatenate([jnp.zeros((width, 1), jnp.bfloat16), gathered[:, :-1]], 1)
        previous = jnp.where(carry_flag[None, :], shifted, jnp.zeros((), jnp.bfloat16))
        joined_inputs = jnp.concatenate([gathered, previous], 0)
        preactivation = jnp.einsum(
            "gcr,rl->gcl",
            lax.all_gather(weights, "dp", axis=2, tiled=True),
            joined_inputs,
            preferred_element_type=jnp.float32,
        )
        preactivation = preactivation + bias[:, :, None]
        gate_z = jnp.tanh(preactivation[0])
        forget = jax.nn.sigmoid(preactivation[1])
        output_gate = jax.nn.sigmoid(preactivation[2])
        decay = forget * carry_on[None, :]
        source = (1.0 - forget) * gate_z
        cell = lax.associative_scan(combine, (decay, source), axis=1)[1]
        hidden_parts.append((output_gate * cell).astype(jnp.bfloat16))
        decay_next = jnp.concatenate([decay[:, 1:], jnp.zeros((width_part, 1), jnp.float32)], 1)
        dcell = lax.associative_scan(combine, (decay_next, cot * output_gate), reverse=True, axis=1)[1]
        cell_before = (
            jnp.concatenate([jnp.zeros((width_part, 1), jnp.float32), cell[:, :-1]], 1)
            * carry_on[None, :]
        )
        grad_z = dcell * (1.0 - forget) * (1.0 - gate_z * gate_z)
        grad_f = dcell * (cell_before - gate_z) * forget * (1.0 - forget)
        grad_o = cot * cell * output_gate * (1.0 - output_gate)
        dpre_low = jnp.stack([grad_z, grad_f, grad_o], 0).astype(jnp.bfloat16)
        bias_total = bias_total + jnp.sum(dpre_low.astype(jnp.float32), axis=2)
        weight_term = jnp.einsum(
            "gcl,rl->gcr", dpre_low, joined_inputs, preferred_element_type=jnp.float32
        )
        djoined = jnp.einsum(
            "gcl,gcr->rl",
            dpre_low,
            lax.all_gather(weights, "dp", axis=2, tiled=True),
            preferred_element_type=jnp.float32,
        )
        later = djoined[width:] * carry_on[None, :]
        later = jnp.concatenate([later[:, 1:], jnp.zeros((width, 1), jnp.float32)], 1)
        term = djoined[:width] + later
        input_parts.append(
            lax.psum_scatter(term, "chan", scatter_dimension=0, tiled=True).astype(jnp.bfloat16)
        )
        grad_shard = grad_shard + lax.psum_scatter(weight_term, "dp", scatter_dimension=2, tiled=True)
    bias_grad = lax.psum(bias_total, "dp")
    hidden = jnp.concatenate(hidden_parts, 1)
    input_grad = jnp.concatenate(input_parts, 1)
    return (hidden, input_grad, grad_shard, bias_grad)


def solution(mesh):
    chan, parts = mesh.shape["chan"], mesh.shape["dp"]
    in_specs = (P("chan", "dp"), P(None, "chan", "dp"), P(None, "chan"), P("dp"), P("chan", "dp"))
    out_specs = (P("chan", "dp"), P("chan", "dp"), P(None, "chan", "dp"), P(None, "chan"))

    def run(tokens, weights, bias, segment_ids, cotangent):
        C = tokens.shape[0] // chan
        row_part = weights.shape[2] // parts
        pairs = tokens.shape[1] // parts % (2 * LEN * CALLS) == 0
        tail = C - LANES
        fits = chan == 4 and parts == 8 and row_part == C and pairs and 0 < 3 * tail < LANES and tail % 32 == 0
        body = functools.partial(local, chan, parts) if fits else local_any
        return jax.shard_map(body, mesh=mesh, in_specs=in_specs, out_specs=out_specs, check_vma=False)(
            tokens, weights, bias, segment_ids, cotangent
        )

    return run
```

```python
import functools

import jax
import jax.numpy as jnp
from jax import lax
from jax.experimental import pallas as pl
from jax.experimental.pallas import tpu as pltpu
from jax.sharding import PartitionSpec as P

LEN = 1024
MICRO = 4
LANES = 128
SEGS = 8
PAD = 8
TILE = 256
UNROLL = 16
FTILE = 1024
TILES = LEN // TILE
CALLS = 2
REST = (3, 5, 2, 6, 1, 4, 0)
GROUPS = ((0, 1, 4), (2, 5, 6), (3, 7))
f32 = jnp.float32
bf16 = jnp.bfloat16
ANY = pl.BlockSpec(memory_space=pl.ANY)
VMEM = pl.BlockSpec(memory_space=pltpu.VMEM)
HBM = pl.BlockSpec(memory_space=pltpu.HBM)
SMEM = pl.BlockSpec(memory_space=pltpu.SMEM)


def dot(a, b, ca, cb):
    return lax.dot_general(a, b, (((ca,), (cb,)), ((), ())), preferred_element_type=f32)


def sigmoid(v):
    return 0.5 * jnp.tanh(0.5 * v) + 0.5


def layer_kernel(k, calls, rows, parts, C, n, *refs):
    first, last = k == 0, k == calls - 1
    refs = list(refs)
    tok, sib, cot, scot, ids, bias, bias_sib, x_near, x_far = refs[:9]
    refs = refs[9:]
    if first:
        w_in, refs = refs[: parts + len(GROUPS)], refs[parts + len(GROUPS) :]
    else:
        w_in, acc_in, refs = refs[0], refs[1], refs[3:]
    hid, to_sib, dx_px, dx_pd, dx_own = refs[:5]
    refs = refs[5:]
    if last:
        own_first, own_rest, sib_first, sib_rest, refs = *refs[:4], refs[4:]
    else:
        acc_out, refs = refs[0], refs[1:]
    if first:
        w_out, refs = refs[0], refs[1:]
    (xb, wb, cb, pre, gp, zs, fs, os_, cbs, ct, hs, hb, dp, dxb, accb, ab, nxt, sums, cl, ca_t, id_b, bb, sem, rsem, osem) = refs
    D = 4 * C
    tl = C - LANES
    steps = n // SEGS
    sp = steps + PAD
    half = 4 * LANES
    me, place = lax.axis_index("chan"), lax.axis_index("dp")
    core = me & 1

    def go(src, dst, i):
        copy = pltpu.make_async_copy(src, dst, sem.at[i])
        copy.start()
        return copy

    def here(r):
        return pl.ds(pl.multiple_of((2 * (k * rows + r) + core) * n, n), n)

    def span(r):
        return pl.ds(pl.multiple_of(r * n, n), n)

    def block(j):
        return pl.ds(pl.multiple_of((me ^ j) * C, 32), C)

    def seg(h):
        return pl.ds(pl.multiple_of(h * sp, 8), steps)

    def id_rows(r):
        return pl.ds(pl.multiple_of((2 * (k * rows + r) + core) * SEGS, SEGS), SEGS)

    def x_copies(r):
        from_row = span(r)
        pairs = (
            (tok.at[:, here(r)], xb.at[block(0), span(r)]),
            (sib.at[:, here(r)], xb.at[block(1), span(r)]),
            (x_near.at[:, from_row], xb.at[block(2), span(r)]),
            (x_far.at[:, from_row], xb.at[block(3), span(r)]),
            (ids.at[id_rows(r)], id_b.at[r]),
        )
        return [pltpu.make_async_copy(a, b, rsem.at[r, i]) for i, (a, b) in enumerate(pairs)]

    def c_copies(r):
        pairs = (
            (cot.at[0:LANES, here(r)], cb.at[0:LANES, span(r)]),
            (scot.at[0:LANES, here(r)], cb.at[LANES : 2 * LANES, span(r)]),
            (cot.at[LANES:C, here(r)], cb.at[2 * LANES : 2 * LANES + tl, span(r)]),
            (scot.at[LANES:C, here(r)], cb.at[2 * LANES + tl : 2 * LANES + 2 * tl, span(r)]),
        )
        return [pltpu.make_async_copy(a, b, rsem.at[r, 5 + i]) for i, (a, b) in enumerate(pairs)]

    def hidden_copies(r):
        pairs = (
            (hb.at[0:LANES, span(r)], hid.at[0:LANES, here(r)]),
            (hb.at[LANES : 2 * LANES, span(r)], to_sib.at[C : C + LANES, span(r)]),
            (hb.at[2 * LANES : 2 * LANES + tl, span(r)], hid.at[LANES:C, here(r)]),
            (hb.at[2 * LANES + tl : 2 * LANES + 2 * tl, span(r)], to_sib.at[C + LANES : 2 * C, span(r)]),
        )
        return [pltpu.make_async_copy(a, b, rsem.at[r, 10 + i]) for i, (a, b) in enumerate(pairs)]

    def grad_copies(r):
        outs = (dx_own, to_sib.at[0:C], dx_px, dx_pd)
        return [
            pltpu.make_async_copy(dxb.at[block(j), span(r)], out.at[:, span(r)], rsem.at[r, 14 + j])
            for j, out in enumerate(outs)
        ]

    for copy in x_copies(0):
        copy.start()
    if first:
        w_copies = []
        for j in range(parts):
            at = pl.ds(pl.multiple_of((place ^ j) * C, 32), C)
            w_copies.append(go(w_in[j], wb.at[at, 0:half], 8 + j))
            which = [j in group for group in GROUPS].index(True)
            spot = GROUPS[which].index(j)
            other = w_in[parts + which].at[spot * C : (spot + 1) * C]
            w_copies.append(go(other, wb.at[at, half : 2 * half], 8 + parts + j))
    else:
        w_copies = [go(w_in, wb, 0)]
    b_copies = [go(bias, bb.at[:, 0:half], 1), go(bias_sib, bb.at[:, half : 2 * half], 3)]
    for r in range(rows):
        for copy in (x_copies(r) if r else []) + c_copies(r):
            copy.start()
    sums[...] = jnp.zeros_like(sums)
    lane = lax.broadcasted_iota(jnp.int32, (SEGS, LANES), 1)
    edge = lax.broadcasted_iota(jnp.int32, (D, LANES), 1) == LANES - 1
    cols = [slice(q * LANES, (q + 1) * LANES) for q in range(3)]
    one = jnp.ones((SEGS, LANES), f32)
    zero = jnp.zeros((SEGS, LANES), f32)

    def strided(ref, t, q):
        return ref[q, pl.ds(t, SEGS, stride=sp), :]

    def now(t):
        return pl.ds(pl.multiple_of(t * SEGS, SEGS), SEGS)

    def arrive(r):
        for copy in x_copies(r):
            copy.wait()
        seg_ids = id_b[r]
        before = pltpu.roll(seg_ids, 1, 1)
        before = jnp.where(lane == 0, pltpu.roll(before, 1, 0), before)
        sub = lax.broadcasted_iota(jnp.int32, (SEGS, steps), 0)
        carry = jnp.where((seg_ids == before) & ((lane > 0) | (sub > 0)), 1.0, 0.0).astype(f32)
        for s in range(SEGS):
            cl[r, :, s * steps : (s + 1) * steps] = jnp.broadcast_to(carry[s : s + 1, :], (SEGS, steps))
        for t in range(steps):
            ca_t[r, t * SEGS : (t + 1) * SEGS, :] = jnp.broadcast_to(carry[:, t : t + 1], (SEGS, LANES))

    rb = 32

    def previous(r, i):
        o = pl.multiple_of(i * rb, rb)
        v = xb[pl.ds(o, rb), span(r)].astype(f32)
        xb[pl.ds(D + o, rb), span(r)] = (pltpu.roll(v, 1, 1) * cl[r, 0:1, :]).astype(bf16)

    def forward(r, i):
        o = pl.multiple_of(r * n + i * FTILE, FTILE)
        v = dot(xb[:, pl.ds(o, FTILE)], wb[...], 0, 0)
        for h in range(FTILE // steps):
            at = seg(i * (FTILE // steps) + h)
            for q in range(8):
                pre[q, at, :] = v[h * steps : (h + 1) * steps, q * LANES : (q + 1) * LANES]
            c = cb[:, pl.ds(pl.multiple_of(o + h * steps, LANES), steps)].astype(f32).T
            for q in range(3):
                ct[q, at, :] = c[:, q * LANES : (q + 1) * LANES]

    def round_tile(r, i):
        into = pl.ds(pl.multiple_of(r * n + i * steps, LANES), steps)
        for q in range(8):
            v = gp[q, seg(i), :].astype(bf16)
            dp[into, q * LANES : (q + 1) * LANES] = v
            v = v.astype(f32)
            a = v[0:SEGS]
            for s in range(SEGS, steps, SEGS):
                a = a + v[s : s + SEGS]
            sums[:, q * LANES : (q + 1) * LANES] += a
        for q in range(3):
            e = LANES if q < 2 else 2 * tl
            hb[q * LANES : q * LANES + e, into] = hs[q, seg(i), :].T.astype(bf16)[0:e]

    def input_tile(r, i):
        i = n // TILE - 1 - i
        o = pl.multiple_of(i * TILE, TILE)
        dj = dot(wb[...], dp[pl.ds(pl.multiple_of(r * n + o, TILE), TILE), :], 1, 1)
        after = nxt[...]
        for h in range(TILE // LANES - 1, -1, -1):
            at = slice(h * LANES, (h + 1) * LANES)
            into = pl.ds(pl.multiple_of(r * n + o + h * LANES, LANES), LANES)
            rolled = pltpu.roll(
                dj[D:, at] * cl[r, 0:1, pl.ds(pl.multiple_of(o + h * LANES, LANES), LANES)], LANES - 1, 1
            )
            dxb[:, into] = (dj[:D, at] + jnp.where(edge, after, rolled)).astype(bf16)
            after = rolled
        nxt[...] = after

    def weight_tile(r, i, add):
        at = pl.ds(pl.multiple_of(i * TILE, TILE), TILE)
        v = dot(xb[:, span(r)], dp[span(r), at], 1, 0)
        return (v + accb[0 : 2 * D, at] if add else v), at

    def weight_step(r, i):
        v, at = weight_tile(r, i, not (first and r == 0))
        accb[0 : 2 * D, at] = v

    def gates_step(r, b, t, state):
        gain, total = state
        v = [strided(pre, t, q) + b[q] for q in range(8)]
        u, w = v[3], v[7]
        tz = jnp.where(lane < tl, u, pltpu.roll(w, tl, 1))
        tf = jnp.where(lane < tl, pltpu.roll(u, LANES - tl, 1), w)
        to = jnp.where(lane < tl, pltpu.roll(u, LANES - 2 * tl, 1), pltpu.roll(w, LANES - tl, 1))
        z = [jnp.tanh(g) for g in (v[0], v[4], tz)]
        f = [sigmoid(g) for g in (v[1], v[5], tf)]
        o = [sigmoid(g) for g in (v[2], v[6], to)]
        at = now(t)
        ca = ca_t[r, at, :]
        gains, totals = [], []
        for q in range(3):
            zs[at, cols[q]] = z[q]
            fs[at, cols[q]] = f[q]
            os_[at, cols[q]] = o[q]
            gains.append(gain[q] * (f[q] * ca))
            totals.append(z[q] + f[q] * (ca * total[q] - z[q]))
        return tuple(gains), tuple(totals)

    def cell_step(r, t, state):
        cell, back, gain = state
        at = now(t)
        ca = ca_t[r, at, :]
        cells, backs, gains = [], [], []
        for q in range(3):
            z, f, o = zs[at, cols[q]], fs[at, cols[q]], os_[at, cols[q]]
            prev = ca * cell[q]
            cbs[at, cols[q]] = prev
            new = z + f * (prev - z)
            hs[q, pl.ds(t, SEGS, stride=sp), :] = o * new
            g = jnp.where(t == 0, one, gain[q] * (f * ca))
            cells.append(new)
            gains.append(g)
            backs.append(back[q] + g * (strided(ct, t, q) * o))
        return tuple(cells), tuple(backs), tuple(gains)

    def grad_step(r, i, later):
        t = steps - 1 - i
        at = now(t)
        ca = ca_t[r, at, :]
        gz, gf, go_, laters = [], [], [], []
        for q in range(3):
            z, f, o, prev = zs[at, cols[q]], fs[at, cols[q]], os_[at, cols[q]], cbs[at, cols[q]]
            c = strided(ct, t, q)
            dc = c * o + later[q]
            laters.append((f * ca) * dc)
            d = prev - z
            u = dc * (1.0 - f)
            gz.append(u * (1.0 - z * z))
            gf.append(u * (f * d))
            go_.append(c * (z + f * d) * (o * (1.0 - o)))
        z, f, o = gz[2], gf[2], go_[2]
        u = jnp.where(
            lane < tl,
            z,
            jnp.where(
                lane < 2 * tl,
                pltpu.roll(f, tl, 1),
                jnp.where(lane < 3 * tl, pltpu.roll(o, 2 * tl, 1), 0.0),
            ),
        )
        w = jnp.where(
            lane < tl,
            pltpu.roll(z, LANES - tl, 1),
            jnp.where(lane < 2 * tl, f, jnp.where(lane < 3 * tl, pltpu.roll(o, tl, 1), 0.0)),
        )
        for q, v in enumerate((gz[0], gf[0], go_[0], u, gz[1], gf[1], go_[1], w)):
            gp[q, pl.ds(t, SEGS, stride=sp), :] = v
        return tuple(laters)

    def scan(step, state, beside=None):
        if beside is None:
            return lax.fori_loop(0, steps, step, state, unroll=UNROLL)
        count = steps // TILES

        def body(i, state):
            beside(i)
            for u in range(count):
                state = step(i * count + u, state)
            return state

        return lax.fori_loop(0, TILES, body, state)

    def combine_segments(gain, total, backward):
        sub = lax.broadcasted_iota(jnp.int32, (SEGS, LANES), 0)
        d = 1
        while d < SEGS:
            there = sub < SEGS - d if backward else sub >= d
            by = SEGS - d if backward else d
            total = total + gain * jnp.where(there, pltpu.roll(total, by, 0), 0.0)
            gain = gain * jnp.where(there, pltpu.roll(gain, by, 0), 1.0)
            d *= 2
        there = sub < SEGS - 1 if backward else sub >= 1
        return jnp.where(there, pltpu.roll(total, SEGS - 1 if backward else 1, 0), 0.0)

    def row(r):
        b = [jnp.broadcast_to(bb[0:1, q * LANES : (q + 1) * LANES], (SEGS, LANES)) for q in range(8)]
        inputs = weights = None
        if r > 0:
            nxt[...] = jnp.zeros_like(nxt)
            inputs, weights = functools.partial(input_tile, r - 1), functools.partial(weight_step, r - 1)
        gain, total = scan(functools.partial(gates_step, r, b), ((one,) * 3, (zero,) * 3), inputs)
        if r > 0:
            for copy in grad_copies(r - 1):
                copy.start()
            if r == 1 and not first:
                pltpu.make_async_copy(acc_in, accb, sem.at[2]).wait()
        cell = tuple(combine_segments(gain[q], total[q], False) for q in range(3))
        cell, back, gain = scan(functools.partial(cell_step, r), (cell, (zero,) * 3, (one,) * 3))
        enter = [fs[0:SEGS, cols[q]] * ca_t[r, 0:SEGS, :] for q in range(3)]
        later = tuple(combine_segments(enter[q] * gain[q], enter[q] * back[q], True) for q in range(3))
        scan(functools.partial(grad_step, r), later, weights)

    arrive(0)
    lax.fori_loop(0, D // rb, lambda i, _: (previous(0, i), 0)[1], 0)
    for r in range(1, rows):
        arrive(r)
    for copy in w_copies + b_copies:
        copy.wait()
    if first:
        go(wb, w_out, 0)
    else:
        go(acc_in, accb, 2)
    for r in range(rows):
        for copy in c_copies(r):
            copy.wait()

        def forward_step(i, _):
            forward(r, i)
            if r + 1 < rows:
                for j in range(D // rb * FTILE // n):
                    previous(r + 1, i * (D // rb * FTILE // n) + j)
            if r > 0:
                for j in range(FTILE // steps):
                    round_tile(r - 1, i * (FTILE // steps) + j)
            return 0

        lax.fori_loop(0, n // FTILE, forward_step, 0)
        if r > 0:
            for copy in hidden_copies(r - 1):
                copy.start()
        row(r)
    end = rows - 1
    nxt[...] = jnp.zeros_like(nxt)
    if end == 0 and not first:
        pltpu.make_async_copy(acc_in, accb, sem.at[2]).wait()

    def input_step(i, _):
        for j in range(TILE // steps):
            round_tile(end, (TILES - 1 - i) * (TILE // steps) + j)
        input_tile(end, i)
        return 0

    lax.fori_loop(0, TILES, input_step, 0)
    for copy in hidden_copies(end) + grad_copies(end):
        copy.start()
    for q in range(8):
        at = slice(q * LANES, (q + 1) * LANES)
        s = sums[:, at]
        if not first:
            s = s + accb[2 * D :, at]
        if last:
            s = jnp.sum(s, 0, keepdims=True)
            if q >= 4:
                ab[2 * D :, (q - 4) * LANES : (q - 3) * LANES] = in_two(s)
        accb[2 * D :, at] = jnp.broadcast_to(s, (SEGS, LANES))

    def blocks_out(source, first_out, rest_out, which, i):
        at = pl.ds(pl.multiple_of(i * TILE, TILE), TILE)
        copies = []
        for place_in, j in enumerate((7,) + REST):
            rows_in = pl.ds(pl.multiple_of((place ^ j) * C, 32), C)
            out = first_out.at[0:C, at] if j == 7 else rest_out.at[(place_in - 1) * C : place_in * C, at]
            copies.append(pltpu.make_async_copy(source.at[rows_in, at], out, osem.at[which, i, place_in]))
        return copies

    def own_copies(i):
        if last:
            return blocks_out(accb, own_first, own_rest, 0, i)
        at = pl.ds(pl.multiple_of(i * TILE, TILE), TILE)
        return [pltpu.make_async_copy(accb.at[:, at], acc_out.at[:, at], sem.at[4 + i])]

    def own_step(i, _):
        v, at = weight_tile(end, i, not (first and rows == 1))
        accb[0 : 2 * D, at] = v
        for copy in own_copies(i):
            copy.start()
        return 0

    def sib_step(i, _):
        v, _ = weight_tile(end, half // TILE + i, not (first and rows == 1))
        ab[0 : 2 * D, pl.ds(pl.multiple_of(i * TILE, TILE), TILE)] = v.astype(bf16)
        for copy in blocks_out(ab, sib_first, sib_rest, 1, i):
            copy.start()
        return 0

    own_tiles = (half if last else 2 * half) // TILE
    tails = []
    if last:
        tails = [
            go(accb.at[2 * D :, 0:half], own_first.at[C:], 4),
            go(ab.at[2 * D :], sib_first.at[C:], 5),
        ]
        lax.fori_loop(0, half // TILE, sib_step, 0)
    lax.fori_loop(0, own_tiles, own_step, 0)
    for i in range(own_tiles):
        tails += own_copies(i)
    if last:
        for i in range(half // TILE):
            tails += blocks_out(ab, sib_first, sib_rest, 1, i)
    for copy in tails:
        copy.wait()
    if first:
        pltpu.make_async_copy(wb, w_out, sem.at[0]).wait()
    for r in range(rows):
        for copy in hidden_copies(r) + grad_copies(r):
            copy.wait()


def layer(k, calls, rows, parts, C, n, tok, sib, cot, scot, ids, biases, x, w, acc, hid):
    first, last = k == 0, k == calls - 1
    D = 4 * C
    N = 8 * LANES
    T = rows * n
    shape = jax.ShapeDtypeStruct
    ins = [tok, sib, cot, scot, ids] + list(biases) + list(x)
    alias = {}
    outs = [shape(tok.shape, bf16), shape((2 * C, T), bf16)] + [shape((C, T), bf16)] * 3
    if first:
        ins += list(w)
    else:
        ins += [w, acc, hid]
        alias = {len(ins) - 1: 0}
        if not last:
            alias[len(ins) - 2] = 5
    if last:
        for kind in (f32, bf16):
            outs += [shape((C + SEGS, N // 2), kind), shape((len(REST) * C, N // 2), kind)]
    else:
        outs += [shape((2 * D + SEGS, N), f32)]
    if first:
        outs += [shape((2 * D, N), bf16)]
    w3 = 3 * LANES
    tall = n + SEGS * PAD
    scratch = (
        [
            pltpu.VMEM((2 * D, T), bf16),
            pltpu.VMEM((2 * D, N), bf16),
            pltpu.VMEM((w3, T), bf16),
            pltpu.VMEM((8, tall, LANES), f32),
            pltpu.VMEM((8, tall, LANES), f32),
        ]
        + [pltpu.VMEM((n, w3), f32)] * 4
        + [pltpu.VMEM((3, tall, LANES), f32)] * 2
        + [
            pltpu.VMEM((2 * C, T), bf16),
            pltpu.VMEM((T, N), bf16),
            pltpu.VMEM((D, T), bf16),
            pltpu.VMEM((2 * D + SEGS, N), f32),
            pltpu.VMEM((2 * D + SEGS, N // 2), bf16),
            pltpu.VMEM((D, LANES), f32),
            pltpu.VMEM((SEGS, N), f32),
            pltpu.VMEM((rows, SEGS, n), f32),
            pltpu.VMEM((rows, n, LANES), f32),
            pltpu.VMEM((rows, SEGS, LANES), jnp.int32),
            pltpu.VMEM((SEGS, N), f32),
            pltpu.SemaphoreType.DMA((8 + 2 * parts,)),
            pltpu.SemaphoreType.DMA((rows, 18)),
            pltpu.SemaphoreType.DMA((2, N // 2 // TILE, 1 + len(REST))),
        ]
    )
    return pl.pallas_call(
        functools.partial(layer_kernel, k, calls, rows, parts, C, n),
        out_shape=outs,
        in_specs=[ANY] * len(ins),
        out_specs=[ANY] * len(outs),
        scratch_shapes=scratch,
        input_output_aliases=alias,
        compiler_params=pltpu.CompilerParams(vmem_limit_bytes=60 << 20),
        cost_estimate=pl.CostEstimate(flops=1, bytes_accessed=1, transcendentals=0),
        name="layer",
    )(*ins)


def take_kernel(picks, n, tok, *refs):
    outs, (bufs, sem) = refs[:-2], refs[-2:]
    core = lax.axis_index("chan") & 1
    copies, sends = [], []
    for i, pick in enumerate(picks):
        for j, (pair, mine) in enumerate(pick):
            at = pl.ds(pl.multiple_of((2 * pair + (core if mine else 1 - core)) * n, n), n)
            copies.append(pltpu.make_async_copy(tok.at[:, at], bufs.at[i, :, j * n : (j + 1) * n], sem.at[i, j]))
            copies[-1].start()
    for i, pick in enumerate(picks):
        for copy in copies[i * len(pick) : (i + 1) * len(pick)]:
            copy.wait()
        sends.append(pltpu.make_async_copy(bufs.at[i], outs[i], sem.at[i, 0]))
        sends[-1].start()
    for send in sends:
        send.wait()


def take_rows(picks, C, n, tok):
    width = len(picks[0]) * n
    return pl.pallas_call(
        functools.partial(take_kernel, picks, n),
        out_shape=[jax.ShapeDtypeStruct((C, width), bf16)] * len(picks),
        in_specs=[ANY],
        out_specs=[ANY] * len(picks),
        scratch_shapes=[
            pltpu.VMEM((len(picks), C, width), bf16),
            pltpu.SemaphoreType.DMA((len(picks), len(picks[0]))),
        ],
        compiler_params=pltpu.CompilerParams(vmem_limit_bytes=8 << 20),
        cost_estimate=pl.CostEstimate(flops=1, bytes_accessed=1, transcendentals=0),
        name="take",
    )(tok)


def pack_kernel(C, w, b, out, b_out):
    tail = C - LANES
    parts = [w[g, 0:LANES].astype(f32) for g in range(3)] + [w[g, LANES:C].astype(f32) for g in range(3)]
    parts.append(jnp.zeros((LANES - 3 * tail, w.shape[2]), f32))
    out[...] = jnp.concatenate(parts, 0).T.astype(bf16)
    b_out[...] = jnp.zeros_like(b_out)
    for g in range(3):
        b_out[0:1, g * LANES : (g + 1) * LANES] = b[g : g + 1, 0:LANES]
        b_out[0:1, 3 * LANES + g * tail : 3 * LANES + (g + 1) * tail] = b[g : g + 1, LANES:C]


def pack(C, w, b):
    return pl.pallas_call(
        functools.partial(pack_kernel, C),
        out_shape=[
            jax.ShapeDtypeStruct((w.shape[2], 4 * LANES), bf16),
            jax.ShapeDtypeStruct((SEGS, 4 * LANES), f32),
        ],
        in_specs=[VMEM] * 2,
        out_specs=[VMEM] * 2,
        compiler_params=pltpu.CompilerParams(vmem_limit_bytes=4 << 20),
        cost_estimate=pl.CostEstimate(flops=1, bytes_accessed=1, transcendentals=0),
        name="pack",
    )(w, b)


def finish_kernel(k, rows, mine, C, n, near, far, *refs):
    total, sem = refs[-2:]
    if mine:
        grad = refs[-3]
    else:
        grad, hid = refs[-4:-2]
    core = lax.axis_index("chan") & 1
    which = core if mine else 1 - core
    copies = []

    def go(src, out, r):
        at = pl.ds(pl.multiple_of((2 * (k * rows + r) + which) * n, n), n)
        copies.append(pltpu.make_async_copy(src, out.at[:, at], sem.at[len(copies)]))
        copies[-1].start()

    for r in range(rows):
        at = slice(r * n, (r + 1) * n)
        if not mine:
            go(near.at[C : 2 * C, at], hid, r)
        total[:, at] = (near[0:C, at].astype(f32) + far[:, at].astype(f32)).astype(bf16)
        go(total.at[:, at], grad, r)
    for copy in copies:
        copy.wait()


def finish(k, rows, mine, C, n, total, near, far, grad, hid=None):
    ins = [near, far]
    specs = [VMEM] * 2
    shape = jax.ShapeDtypeStruct((C, total), bf16)
    outs = [shape]
    alias = {}
    for v in (grad, hid):
        if v is not None:
            alias[len(ins)] = 0 if v is grad else 1
            ins.append(v)
            specs.append(ANY)
    if hid is not None:
        outs.append(shape)
    return pl.pallas_call(
        functools.partial(finish_kernel, k, rows, mine, C, n),
        out_shape=outs,
        in_specs=specs,
        out_specs=[ANY] * len(outs),
        scratch_shapes=[pltpu.VMEM((C, rows * n), bf16), pltpu.SemaphoreType.DMA((2 * rows,))],
        input_output_aliases=alias,
        compiler_params=pltpu.CompilerParams(vmem_limit_bytes=8 << 20),
        cost_estimate=pl.CostEstimate(flops=1, bytes_accessed=1, transcendentals=0),
        name="finish",
    )(*ins)


def in_two(v):
    high = v.astype(bf16)
    low = v - high.astype(f32)
    at = lax.broadcasted_iota(jnp.int32, (SEGS, v.shape[1]), 0)
    return jnp.where(at == 0, high.astype(f32), jnp.where(at == 1, low, 0.0)).astype(bf16)


def from_two(v):
    v = v[...].astype(f32)
    return v[0:1] + v[1:2]


def leaf_kernel(C, own, other, out, b_out):
    b = own[C : C + 1] + from_two(other[C:])
    out[0:C] = (own[0:C] + other[0:C].astype(f32)).astype(bf16)
    out[C:] = in_two(b)
    b_out[...] = jnp.broadcast_to(b, (SEGS, b.shape[1]))


def leaf(C, own, other):
    half = own.shape[1]
    return pl.pallas_call(
        functools.partial(leaf_kernel, C),
        out_shape=[jax.ShapeDtypeStruct((C + SEGS, half), bf16), jax.ShapeDtypeStruct((SEGS, half), f32)],
        in_specs=[VMEM] * 2,
        out_specs=[VMEM] * 2,
        compiler_params=pltpu.CompilerParams(vmem_limit_bytes=4 << 20),
        cost_estimate=pl.CostEstimate(flops=1, bytes_accessed=1, transcendentals=0),
        name="leaf",
    )(own, other)


def split_kernel(C, own, other, b, s3, s5, s2, k6, k1, k4, k0):
    two = in_two(b[0:1])
    for i, out in enumerate((s3, s5, s2, k6, k1, k4, k0)):
        at = slice(i * C, (i + 1) * C)
        v = own[at, :] + other[at, :].astype(f32)
        if i < 3:
            out[0:C] = v.astype(bf16)
            out[C:] = two
        else:
            out[0:C] = v
            out[C:] = b[...]


def split(C, own, other, b):
    half = own.shape[1]
    shape = (C + SEGS, half)
    return pl.pallas_call(
        functools.partial(split_kernel, C),
        out_shape=[jax.ShapeDtypeStruct(shape, bf16)] * 3 + [jax.ShapeDtypeStruct(shape, f32)] * 4,
        in_specs=[VMEM] * 3,
        out_specs=[VMEM] * 7,
        compiler_params=pltpu.CompilerParams(vmem_limit_bytes=16 << 20),
        cost_estimate=pl.CostEstimate(flops=1, bytes_accessed=1, transcendentals=0),
        name="split",
    )(own, other, b)


def pass_on_kernel(C, kept, *refs):
    out = refs[-1]
    v, b = kept[0:C], kept[C : C + 1]
    for r in refs[:-1]:
        v = v + r[0:C].astype(f32)
        b = b + from_two(r[C:])
    out[0:C] = v.astype(bf16)
    out[C:] = in_two(b)


def pass_on(C, kept, *received):
    return pl.pallas_call(
        functools.partial(pass_on_kernel, C),
        out_shape=jax.ShapeDtypeStruct(kept.shape, bf16),
        in_specs=[VMEM] * (1 + len(received)),
        out_specs=VMEM,
        compiler_params=pltpu.CompilerParams(vmem_limit_bytes=4 << 20),
        cost_estimate=pl.CostEstimate(flops=1, bytes_accessed=1, transcendentals=0),
        name="pass_on",
    )(kept, *received)


def total_kernel(C, k0, r2, r1, r4, grad, bias, buf, b_buf, sem):
    v = k0[0:C] + r2[0:C].astype(f32) + (r1[0:C].astype(f32) + r4[0:C].astype(f32))
    t = v.T
    tail = C - LANES
    b = k0[C : C + 1] + from_two(r2[C:]) + (from_two(r1[C:]) + from_two(r4[C:]))
    for g in range(3):
        buf[g, 0:LANES] = t[g * LANES : (g + 1) * LANES]
        buf[g, LANES:C] = t[3 * LANES + g * tail : 3 * LANES + (g + 1) * tail]
        b_buf[g : g + 1, 0:LANES] = b[:, g * LANES : (g + 1) * LANES]
        b_buf[g : g + 1, LANES:C] = b[:, 3 * LANES + g * tail : 3 * LANES + (g + 1) * tail]
    copies = [pltpu.make_async_copy(buf, grad, sem.at[0]), pltpu.make_async_copy(b_buf, bias, sem.at[1])]
    for copy in copies:
        copy.start()
    for copy in copies:
        copy.wait()


def total_sum(C, k0, r2, r1, r4):
    shapes = ((3, C, C), (3, C))
    return pl.pallas_call(
        functools.partial(total_kernel, C),
        out_shape=[jax.ShapeDtypeStruct(shape, f32) for shape in shapes],
        in_specs=[VMEM] * 4,
        out_specs=[HBM] * 2,
        scratch_shapes=[pltpu.VMEM(shape, f32) for shape in shapes] + [pltpu.SemaphoreType.DMA((2,))],
        compiler_params=pltpu.CompilerParams(vmem_limit_bytes=4 << 20),
        cost_estimate=pl.CostEstimate(flops=1, bytes_accessed=1, transcendentals=0),
        name="total",
    )(k0, r2, r1, r4)


def local(chan, parts, tokens, weights, bias, segment_ids, cotangent):
    C, total = tokens.shape
    n = LEN
    pairs = total // n // 2
    rows = pairs // CALLS
    me = lax.axis_index("chan")
    core = me & 1

    def chan_move(v, j):
        return lax.ppermute(v, "chan", [(i, i ^ j) for i in range(chan)])

    def dp_move(v, j):
        return lax.ppermute(v, "dp", [(i, i ^ j) for i in range(parts)])

    def after(v, *others):
        return lax.optimization_barrier((v,) + others)[0]

    ids = segment_ids.reshape(2 * pairs * SEGS, n // SEGS)
    def other_rows(k, tok):
        picks = [[(k * rows + r, mine) for r in range(rows)] for mine in (True, False)]
        return take_rows(picks, C, n, tok)

    to_near, to_far = other_rows(0, tokens)
    near, far = chan_move(to_near, 2), chan_move(to_far, 3)
    xs = [(near, far)]
    shard, b_own = pack(C, after(weights, to_near), bias)
    sib = chan_move(tokens, 1)
    scot = chan_move(cotangent, 1)
    g = {0: shard, 4: dp_move(shard, 4), 1: dp_move(shard, 1)}
    def to_sibling(group):
        return chan_move(jnp.concatenate([g[j] for j in group], 0), 1)

    g4, own = lax.optimization_barrier((g[4], shard, sib))[:2]
    g[6] = dp_move(g4, 2)
    g[5] = dp_move(g4, 1)
    w_sib = [to_sibling(GROUPS[0])]
    biases = [b_own, chan_move(after(b_own, far), 1)]
    g[2] = dp_move(own, 2)
    g6, g1 = lax.optimization_barrier((g[6], g[1], near, scot))[:2]
    g[7] = dp_move(g6, 1)
    g[3] = dp_move(g1, 2)
    w_sib.append(to_sibling(GROUPS[1]))
    w_sib.append(to_sibling(GROUPS[2]))
    w = [g[j] for j in range(parts)] + w_sib
    for k in range(1, CALLS):
        to_near, to_far = other_rows(k, after(tokens, g[6]))
        xs.append((chan_move(to_near, 2), chan_move(to_far, 3)))

    acc = hid = grad = None
    moved = []
    for k in range(CALLS):
        out = layer(k, CALLS, rows, parts, C, n, tokens, sib, cotangent, scot, ids, biases, xs[k], w, acc, hid)
        if k == 0:
            w = out[-1]
        hid, to_sib, d_px, d_pd, own, acc = out[:6]
        if k == CALLS - 1:
            own_first, own_rest, sib_first, sib_rest = out[5:9]
            got = [v for m in moved for v in m[1:]]
            to_sib, d_px, d_pd, sib_first, sib_rest = lax.optimization_barrier(
                (to_sib, d_px, d_pd, sib_first, sib_rest, *got)
            )[:5]
            sib_first, sib_rest = chan_move(sib_first, 1), chan_move(sib_rest, 1)
        else:
            to_sib, d_px, d_pd = lax.optimization_barrier((to_sib, d_px, d_pd, *xs[k + 1]))[:3]
        moved.append((own, chan_move(d_px, 2), chan_move(to_sib, 1), chan_move(d_pd, 3)))

    def end(k, mine, *others):
        nonlocal grad, hid
        own, from_px, from_sib, from_pd = moved[k]
        if mine:
            (grad,) = finish(k, rows, True, C, n, total, after(own, *others), from_px, grad)
        else:
            grad, hid = finish(k, rows, False, C, n, total, after(from_sib, *others), from_pd, grad, hid)

    s7, b = leaf(C, own_first, sib_first)
    r7 = dp_move(s7, 1)
    for k in range(CALLS - 1):
        end(k, True, s7)
    s3, s5, s2, k6, k1, k4, k0 = split(C, own_rest, after(sib_rest, moved[-1][2], grad), b)
    r3, r5 = dp_move(s3, 2), dp_move(s5, 1)
    s6 = pass_on(C, k6, r7)
    r6 = dp_move(s6, 2)
    for k in range(CALLS - 1):
        end(k, False, s6, r5)
    r1, r2 = dp_move(pass_on(C, k1, after(r3, grad)), 1), dp_move(after(s2, r3), 2)
    s4 = pass_on(C, k4, r5, after(r6, grad))
    r4 = dp_move(s4, 4)
    end(CALLS - 1, True, s4, r1)
    end(CALLS - 1, False, s4)
    weight_grad, bias_grad = total_sum(C, k0, r2, r1, after(r4, grad))
    return (hid, grad, weight_grad, bias_grad)


def combine(earlier, later):
    return (earlier[0] * later[0], later[0] * earlier[1] + later[1])


def local_any(tokens, weights, bias, segment_ids, cotangent):
    width_part, total_rows = tokens.shape
    batch_rows = total_rows // MICRO
    grad_shard = jnp.zeros(weights.shape, jnp.float32)
    bias_total = jnp.zeros(bias.shape, jnp.float32)
    position = jnp.arange(batch_rows) % LEN
    hidden_parts = []
    input_parts = []
    for micro in range(MICRO):
        lower = micro * batch_rows
        upper = lower + batch_rows
        part_in = tokens[:, lower:upper]
        ids = segment_ids[lower:upper]
        cot = cotangent[:, lower:upper].astype(jnp.float32)
        before = jnp.concatenate([ids[:1], ids[:-1]], 0)
        carry_flag = (position > 0) & (ids == before)
        carry_on = jnp.where(carry_flag, 1.0, 0.0).astype(jnp.float32)
        gathered = lax.all_gather(part_in, "chan", axis=0, tiled=True)
        width = gathered.shape[0]
        shifted = jnp.concatenate([jnp.zeros((width, 1), jnp.bfloat16), gathered[:, :-1]], 1)
        previous = jnp.where(carry_flag[None, :], shifted, jnp.zeros((), jnp.bfloat16))
        joined_inputs = jnp.concatenate([gathered, previous], 0)
        preactivation = jnp.einsum(
            "gcr,rl->gcl",
            lax.all_gather(weights, "dp", axis=2, tiled=True),
            joined_inputs,
            preferred_element_type=jnp.float32,
        )
        preactivation = preactivation + bias[:, :, None]
        gate_z = jnp.tanh(preactivation[0])
        forget = jax.nn.sigmoid(preactivation[1])
        output_gate = jax.nn.sigmoid(preactivation[2])
        decay = forget * carry_on[None, :]
        source = (1.0 - forget) * gate_z
        cell = lax.associative_scan(combine, (decay, source), axis=1)[1]
        hidden_parts.append((output_gate * cell).astype(jnp.bfloat16))
        decay_next = jnp.concatenate([decay[:, 1:], jnp.zeros((width_part, 1), jnp.float32)], 1)
        dcell = lax.associative_scan(combine, (decay_next, cot * output_gate), reverse=True, axis=1)[1]
        cell_before = (
            jnp.concatenate([jnp.zeros((width_part, 1), jnp.float32), cell[:, :-1]], 1)
            * carry_on[None, :]
        )
        grad_z = dcell * (1.0 - forget) * (1.0 - gate_z * gate_z)
        grad_f = dcell * (cell_before - gate_z) * forget * (1.0 - forget)
        grad_o = cot * cell * output_gate * (1.0 - output_gate)
        dpre_low = jnp.stack([grad_z, grad_f, grad_o], 0).astype(jnp.bfloat16)
        bias_total = bias_total + jnp.sum(dpre_low.astype(jnp.float32), axis=2)
        weight_term = jnp.einsum(
            "gcl,rl->gcr", dpre_low, joined_inputs, preferred_element_type=jnp.float32
        )
        djoined = jnp.einsum(
            "gcl,gcr->rl",
            dpre_low,
            lax.all_gather(weights, "dp", axis=2, tiled=True),
            preferred_element_type=jnp.float32,
        )
        later = djoined[width:] * carry_on[None, :]
        later = jnp.concatenate([later[:, 1:], jnp.zeros((width, 1), jnp.float32)], 1)
        term = djoined[:width] + later
        input_parts.append(
            lax.psum_scatter(term, "chan", scatter_dimension=0, tiled=True).astype(jnp.bfloat16)
        )
        grad_shard = grad_shard + lax.psum_scatter(weight_term, "dp", scatter_dimension=2, tiled=True)
    bias_grad = lax.psum(bias_total, "dp")
    hidden = jnp.concatenate(hidden_parts, 1)
    input_grad = jnp.concatenate(input_parts, 1)
    return (hidden, input_grad, grad_shard, bias_grad)


def solution(mesh):
    chan, parts = mesh.shape["chan"], mesh.shape["dp"]
    in_specs = (P("chan", "dp"), P(None, "chan", "dp"), P(None, "chan"), P("dp"), P("chan", "dp"))
    out_specs = (P("chan", "dp"), P("chan", "dp"), P(None, "chan", "dp"), P(None, "chan"))

    def run(tokens, weights, bias, segment_ids, cotangent):
        C = tokens.shape[0] // chan
        row_part = weights.shape[2] // parts
        pairs = tokens.shape[1] // parts % (2 * LEN * CALLS) == 0
        tail = C - LANES
        fits = chan == 4 and parts == 8 and row_part == C and pairs and 0 < 3 * tail < LANES and tail % 32 == 0
        body = functools.partial(local, chan, parts) if fits else local_any
        return jax.shard_map(body, mesh=mesh, in_specs=in_specs, out_specs=out_specs, check_vma=False)(
            tokens, weights, bias, segment_ids, cotangent
        )

    return run
```

```python
import functools

import jax
import jax.numpy as jnp
from jax import lax
from jax.experimental import pallas as pl
from jax.experimental.pallas import tpu as pltpu
from jax.sharding import PartitionSpec as P

LEN = 1024
MICRO = 4
LANES = 128
SEGS = 8
PAD = 8
TILE = 512
UNROLL = 16
FTILE = 1024
TILES = LEN // TILE
CALLS = 2
REST = (3, 5, 2, 6, 1, 4, 0)
GROUPS = ((0, 1, 4), (2, 5, 6), (3, 7))
f32 = jnp.float32
bf16 = jnp.bfloat16
ANY = pl.BlockSpec(memory_space=pl.ANY)
VMEM = pl.BlockSpec(memory_space=pltpu.VMEM)
HBM = pl.BlockSpec(memory_space=pltpu.HBM)
SMEM = pl.BlockSpec(memory_space=pltpu.SMEM)


def dot(a, b, ca, cb):
    return lax.dot_general(a, b, (((ca,), (cb,)), ((), ())), preferred_element_type=f32)


def sigmoid(v):
    return 0.5 * jnp.tanh(0.5 * v) + 0.5


def layer_kernel(k, calls, rows, parts, C, n, *refs):
    first, last = k == 0, k == calls - 1
    refs = list(refs)
    tok, sib, cot, scot, ids, bias, bias_sib, x_near, x_far = refs[:9]
    refs = refs[9:]
    if first:
        w_in, refs = refs[: parts + len(GROUPS)], refs[parts + len(GROUPS) :]
    else:
        w_in, acc_in, refs = refs[0], refs[1], refs[3:]
    hid, to_sib, dx_px, dx_pd, dx_own = refs[:5]
    refs = refs[5:]
    if last:
        own_first, own_rest, sib_first, sib_rest, refs = *refs[:4], refs[4:]
    else:
        acc_out, refs = refs[0], refs[1:]
    if first:
        w_out, refs = refs[0], refs[1:]
    (xb, wb, cb, pre, gp, zs, fs, os_, cbs, ct, hs, hb, dp, dxb, accb, ab, nxt, sums, cl, ca_t, id_b, bb, sem, rsem, osem) = refs
    D = 4 * C
    tl = C - LANES
    steps = n // SEGS
    sp = steps + PAD
    half = 4 * LANES
    me, place = lax.axis_index("chan"), lax.axis_index("dp")
    core = me & 1

    def go(src, dst, i):
        copy = pltpu.make_async_copy(src, dst, sem.at[i])
        copy.start()
        return copy

    def here(r):
        return pl.ds(pl.multiple_of((2 * (k * rows + r) + core) * n, n), n)

    def span(r):
        return pl.ds(pl.multiple_of(r * n, n), n)

    def block(j):
        return pl.ds(pl.multiple_of((me ^ j) * C, 32), C)

    def seg(h):
        return pl.ds(pl.multiple_of(h * sp, 8), steps)

    def id_rows(r):
        return pl.ds(pl.multiple_of((2 * (k * rows + r) + core) * SEGS, SEGS), SEGS)

    def x_copies(r):
        from_row = span(r)
        pairs = (
            (tok.at[:, here(r)], xb.at[block(0), span(r)]),
            (sib.at[:, here(r)], xb.at[block(1), span(r)]),
            (x_near.at[:, from_row], xb.at[block(2), span(r)]),
            (x_far.at[:, from_row], xb.at[block(3), span(r)]),
            (ids.at[id_rows(r)], id_b.at[r]),
        )
        return [pltpu.make_async_copy(a, b, rsem.at[r, i]) for i, (a, b) in enumerate(pairs)]

    def c_copies(r):
        pairs = (
            (cot.at[0:LANES, here(r)], cb.at[0:LANES, span(r)]),
            (scot.at[0:LANES, here(r)], cb.at[LANES : 2 * LANES, span(r)]),
            (cot.at[LANES:C, here(r)], cb.at[2 * LANES : 2 * LANES + tl, span(r)]),
            (scot.at[LANES:C, here(r)], cb.at[2 * LANES + tl : 2 * LANES + 2 * tl, span(r)]),
        )
        return [pltpu.make_async_copy(a, b, rsem.at[r, 5 + i]) for i, (a, b) in enumerate(pairs)]

    def hidden_copies(r):
        pairs = (
            (hb.at[0:LANES, span(r)], hid.at[0:LANES, here(r)]),
            (hb.at[LANES : 2 * LANES, span(r)], to_sib.at[C : C + LANES, span(r)]),
            (hb.at[2 * LANES : 2 * LANES + tl, span(r)], hid.at[LANES:C, here(r)]),
            (hb.at[2 * LANES + tl : 2 * LANES + 2 * tl, span(r)], to_sib.at[C + LANES : 2 * C, span(r)]),
        )
        return [pltpu.make_async_copy(a, b, rsem.at[r, 10 + i]) for i, (a, b) in enumerate(pairs)]

    def grad_copies(r):
        outs = (dx_own, to_sib.at[0:C], dx_px, dx_pd)
        return [
            pltpu.make_async_copy(dxb.at[block(j), span(r)], out.at[:, span(r)], rsem.at[r, 14 + j])
            for j, out in enumerate(outs)
        ]

    for copy in x_copies(0):
        copy.start()
    if first:
        w_copies = []
        for j in range(parts):
            at = pl.ds(pl.multiple_of((place ^ j) * C, 32), C)
            w_copies.append(go(w_in[j], wb.at[at, 0:half], 8 + j))
            which = [j in group for group in GROUPS].index(True)
            spot = GROUPS[which].index(j)
            other = w_in[parts + which].at[spot * C : (spot + 1) * C]
            w_copies.append(go(other, wb.at[at, half : 2 * half], 8 + parts + j))
    else:
        w_copies = [go(w_in, wb, 0)]
    b_copies = [go(bias, bb.at[:, 0:half], 1), go(bias_sib, bb.at[:, half : 2 * half], 3)]
    for r in range(rows):
        for copy in (x_copies(r) if r else []) + c_copies(r):
            copy.start()
    sums[...] = jnp.zeros_like(sums)
    lane = lax.broadcasted_iota(jnp.int32, (SEGS, LANES), 1)
    edge = lax.broadcasted_iota(jnp.int32, (D, LANES), 1) == LANES - 1
    cols = [slice(q * LANES, (q + 1) * LANES) for q in range(3)]
    one = jnp.ones((SEGS, LANES), f32)
    zero = jnp.zeros((SEGS, LANES), f32)

    def strided(ref, t, q):
        return ref[q, pl.ds(t, SEGS, stride=sp), :]

    def now(t):
        return pl.ds(pl.multiple_of(t * SEGS, SEGS), SEGS)

    def arrive(r):
        for copy in x_copies(r):
            copy.wait()
        seg_ids = id_b[r]
        before = pltpu.roll(seg_ids, 1, 1)
        before = jnp.where(lane == 0, pltpu.roll(before, 1, 0), before)
        sub = lax.broadcasted_iota(jnp.int32, (SEGS, steps), 0)
        carry = jnp.where((seg_ids == before) & ((lane > 0) | (sub > 0)), 1.0, 0.0).astype(f32)
        for s in range(SEGS):
            cl[r, :, s * steps : (s + 1) * steps] = jnp.broadcast_to(carry[s : s + 1, :], (SEGS, steps))
        for t in range(steps):
            ca_t[r, t * SEGS : (t + 1) * SEGS, :] = jnp.broadcast_to(carry[:, t : t + 1], (SEGS, LANES))

    rb = 32

    def previous(r, i):
        o = pl.multiple_of(i * rb, rb)
        v = xb[pl.ds(o, rb), span(r)].astype(f32)
        xb[pl.ds(D + o, rb), span(r)] = (pltpu.roll(v, 1, 1) * cl[r, 0:1, :]).astype(bf16)

    def forward(r, i):
        o = pl.multiple_of(r * n + i * FTILE, FTILE)
        v = dot(xb[:, pl.ds(o, FTILE)], wb[...], 0, 0)
        for h in range(FTILE // steps):
            at = seg(i * (FTILE // steps) + h)
            for q in range(8):
                pre[q, at, :] = v[h * steps : (h + 1) * steps, q * LANES : (q + 1) * LANES]
            c = cb[:, pl.ds(pl.multiple_of(o + h * steps, LANES), steps)].astype(f32).T
            for q in range(3):
                ct[q, at, :] = c[:, q * LANES : (q + 1) * LANES]

    def round_tile(r, i):
        into = pl.ds(pl.multiple_of(r * n + i * steps, LANES), steps)
        for q in range(8):
            v = gp[q, seg(i), :].astype(bf16)
            dp[into, q * LANES : (q + 1) * LANES] = v
            v = v.astype(f32)
            a = v[0:SEGS]
            for s in range(SEGS, steps, SEGS):
                a = a + v[s : s + SEGS]
            sums[:, q * LANES : (q + 1) * LANES] += a
        for q in range(3):
            e = LANES if q < 2 else 2 * tl
            hb[q * LANES : q * LANES + e, into] = hs[q, seg(i), :].T.astype(bf16)[0:e]

    def input_tile(r, i):
        i = n // TILE - 1 - i
        o = pl.multiple_of(i * TILE, TILE)
        dj = dot(wb[...], dp[pl.ds(pl.multiple_of(r * n + o, TILE), TILE), :], 1, 1)
        after = nxt[...]
        for h in range(TILE // LANES - 1, -1, -1):
            at = slice(h * LANES, (h + 1) * LANES)
            into = pl.ds(pl.multiple_of(r * n + o + h * LANES, LANES), LANES)
            rolled = pltpu.roll(
                dj[D:, at] * cl[r, 0:1, pl.ds(pl.multiple_of(o + h * LANES, LANES), LANES)], LANES - 1, 1
            )
            dxb[:, into] = (dj[:D, at] + jnp.where(edge, after, rolled)).astype(bf16)
            after = rolled
        nxt[...] = after

    def weight_tile(r, i, add):
        at = pl.ds(pl.multiple_of(i * TILE, TILE), TILE)
        v = dot(xb[:, span(r)], dp[span(r), at], 1, 0)
        return (v + accb[0 : 2 * D, at] if add else v), at

    def weight_step(r, i):
        v, at = weight_tile(r, i, not (first and r == 0))
        accb[0 : 2 * D, at] = v

    def gates_step(r, b, t, state):
        gain, total = state
        v = [strided(pre, t, q) + b[q] for q in range(8)]
        u, w = v[3], v[7]
        tz = jnp.where(lane < tl, u, pltpu.roll(w, tl, 1))
        tf = jnp.where(lane < tl, pltpu.roll(u, LANES - tl, 1), w)
        to = jnp.where(lane < tl, pltpu.roll(u, LANES - 2 * tl, 1), pltpu.roll(w, LANES - tl, 1))
        z = [jnp.tanh(g) for g in (v[0], v[4], tz)]
        f = [sigmoid(g) for g in (v[1], v[5], tf)]
        o = [sigmoid(g) for g in (v[2], v[6], to)]
        at = now(t)
        ca = ca_t[r, at, :]
        gains, totals = [], []
        for q in range(3):
            zs[at, cols[q]] = z[q]
            fs[at, cols[q]] = f[q]
            os_[at, cols[q]] = o[q]
            gains.append(gain[q] * (f[q] * ca))
            totals.append(z[q] + f[q] * (ca * total[q] - z[q]))
        return tuple(gains), tuple(totals)

    def cell_step(r, t, state):
        cell, back, gain = state
        at = now(t)
        ca = ca_t[r, at, :]
        cells, backs, gains = [], [], []
        for q in range(3):
            z, f, o = zs[at, cols[q]], fs[at, cols[q]], os_[at, cols[q]]
            prev = ca * cell[q]
            cbs[at, cols[q]] = prev
            new = z + f * (prev - z)
            hs[q, pl.ds(t, SEGS, stride=sp), :] = o * new
            g = jnp.where(t == 0, one, gain[q] * (f * ca))
            cells.append(new)
            gains.append(g)
            backs.append(back[q] + g * (strided(ct, t, q) * o))
        return tuple(cells), tuple(backs), tuple(gains)

    def grad_step(r, i, later):
        t = steps - 1 - i
        at = now(t)
        ca = ca_t[r, at, :]
        gz, gf, go_, laters = [], [], [], []
        for q in range(3):
            z, f, o, prev = zs[at, cols[q]], fs[at, cols[q]], os_[at, cols[q]], cbs[at, cols[q]]
            c = strided(ct, t, q)
            dc = c * o + later[q]
            laters.append((f * ca) * dc)
            d = prev - z
            u = dc * (1.0 - f)
            gz.append(u * (1.0 - z * z))
            gf.append(u * (f * d))
            go_.append(c * (z + f * d) * (o * (1.0 - o)))
        z, f, o = gz[2], gf[2], go_[2]
        u = jnp.where(
            lane < tl,
            z,
            jnp.where(
                lane < 2 * tl,
                pltpu.roll(f, tl, 1),
                jnp.where(lane < 3 * tl, pltpu.roll(o, 2 * tl, 1), 0.0),
            ),
        )
        w = jnp.where(
            lane < tl,
            pltpu.roll(z, LANES - tl, 1),
            jnp.where(lane < 2 * tl, f, jnp.where(lane < 3 * tl, pltpu.roll(o, tl, 1), 0.0)),
        )
        for q, v in enumerate((gz[0], gf[0], go_[0], u, gz[1], gf[1], go_[1], w)):
            gp[q, pl.ds(t, SEGS, stride=sp), :] = v
        return tuple(laters)

    def scan(step, state, beside=None):
        if beside is None:
            return lax.fori_loop(0, steps, step, state, unroll=UNROLL)
        count = steps // TILES

        def body(i, state):
            beside(i)
            for u in range(count):
                state = step(i * count + u, state)
            return state

        return lax.fori_loop(0, TILES, body, state)

    def combine_segments(gain, total, backward):
        sub = lax.broadcasted_iota(jnp.int32, (SEGS, LANES), 0)
        d = 1
        while d < SEGS:
            there = sub < SEGS - d if backward else sub >= d
            by = SEGS - d if backward else d
            total = total + gain * jnp.where(there, pltpu.roll(total, by, 0), 0.0)
            gain = gain * jnp.where(there, pltpu.roll(gain, by, 0), 1.0)
            d *= 2
        there = sub < SEGS - 1 if backward else sub >= 1
        return jnp.where(there, pltpu.roll(total, SEGS - 1 if backward else 1, 0), 0.0)

    def row(r):
        b = [jnp.broadcast_to(bb[0:1, q * LANES : (q + 1) * LANES], (SEGS, LANES)) for q in range(8)]
        inputs = weights = None
        if r > 0:
            nxt[...] = jnp.zeros_like(nxt)
            inputs, weights = functools.partial(input_tile, r - 1), functools.partial(weight_step, r - 1)
        gain, total = scan(functools.partial(gates_step, r, b), ((one,) * 3, (zero,) * 3), inputs)
        if r > 0:
            for copy in grad_copies(r - 1):
                copy.start()
            if r == 1 and not first:
                pltpu.make_async_copy(acc_in, accb, sem.at[2]).wait()
        cell = tuple(combine_segments(gain[q], total[q], False) for q in range(3))
        cell, back, gain = scan(functools.partial(cell_step, r), (cell, (zero,) * 3, (one,) * 3), weights)
        enter = [fs[0:SEGS, cols[q]] * ca_t[r, 0:SEGS, :] for q in range(3)]
        later = tuple(combine_segments(enter[q] * gain[q], enter[q] * back[q], True) for q in range(3))
        scan(functools.partial(grad_step, r), later)

    arrive(0)
    lax.fori_loop(0, D // rb, lambda i, _: (previous(0, i), 0)[1], 0)
    for r in range(1, rows):
        arrive(r)
    for copy in w_copies + b_copies:
        copy.wait()
    if first:
        go(wb, w_out, 0)
    else:
        go(acc_in, accb, 2)
    for r in range(rows):
        for copy in c_copies(r):
            copy.wait()

        def forward_step(i, _):
            forward(r, i)
            if r + 1 < rows:
                for j in range(D // rb * FTILE // n):
                    previous(r + 1, i * (D // rb * FTILE // n) + j)
            if r > 0:
                for j in range(FTILE // steps):
                    round_tile(r - 1, i * (FTILE // steps) + j)
            return 0

        lax.fori_loop(0, n // FTILE, forward_step, 0)
        if r > 0:
            for copy in hidden_copies(r - 1):
                copy.start()
        row(r)
    end = rows - 1
    nxt[...] = jnp.zeros_like(nxt)
    if end == 0 and not first:
        pltpu.make_async_copy(acc_in, accb, sem.at[2]).wait()

    def input_step(i, _):
        for j in range(TILE // steps):
            round_tile(end, (TILES - 1 - i) * (TILE // steps) + j)
        input_tile(end, i)
        return 0

    lax.fori_loop(0, TILES, input_step, 0)
    for copy in hidden_copies(end) + grad_copies(end):
        copy.start()
    for q in range(8):
        at = slice(q * LANES, (q + 1) * LANES)
        s = sums[:, at]
        if not first:
            s = s + accb[2 * D :, at]
        if last:
            s = jnp.sum(s, 0, keepdims=True)
            if q >= 4:
                ab[2 * D :, (q - 4) * LANES : (q - 3) * LANES] = in_two(s)
        accb[2 * D :, at] = jnp.broadcast_to(s, (SEGS, LANES))

    def blocks_out(source, first_out, rest_out, which, i):
        at = pl.ds(pl.multiple_of(i * TILE, TILE), TILE)
        copies = []
        for place_in, j in enumerate((7,) + REST):
            rows_in = pl.ds(pl.multiple_of((place ^ j) * C, 32), C)
            out = first_out.at[0:C, at] if j == 7 else rest_out.at[(place_in - 1) * C : place_in * C, at]
            copies.append(pltpu.make_async_copy(source.at[rows_in, at], out, osem.at[which, i, place_in]))
        return copies

    def own_copies(i):
        if last:
            return blocks_out(accb, own_first, own_rest, 0, i)
        at = pl.ds(pl.multiple_of(i * TILE, TILE), TILE)
        return [pltpu.make_async_copy(accb.at[:, at], acc_out.at[:, at], sem.at[4 + i])]

    def own_step(i, _):
        v, at = weight_tile(end, i, not (first and rows == 1))
        accb[0 : 2 * D, at] = v
        for copy in own_copies(i):
            copy.start()
        return 0

    def sib_step(i, _):
        v, _ = weight_tile(end, half // TILE + i, not (first and rows == 1))
        ab[0 : 2 * D, pl.ds(pl.multiple_of(i * TILE, TILE), TILE)] = v.astype(bf16)
        for copy in blocks_out(ab, sib_first, sib_rest, 1, i):
            copy.start()
        return 0

    own_tiles = (half if last else 2 * half) // TILE
    tails = []
    if last:
        tails = [
            go(accb.at[2 * D :, 0:half], own_first.at[C:], 4),
            go(ab.at[2 * D :], sib_first.at[C:], 5),
        ]
        lax.fori_loop(0, half // TILE, sib_step, 0)
    lax.fori_loop(0, own_tiles, own_step, 0)
    for i in range(own_tiles):
        tails += own_copies(i)
    if last:
        for i in range(half // TILE):
            tails += blocks_out(ab, sib_first, sib_rest, 1, i)
    for copy in tails:
        copy.wait()
    if first:
        pltpu.make_async_copy(wb, w_out, sem.at[0]).wait()
    for r in range(rows):
        for copy in hidden_copies(r) + grad_copies(r):
            copy.wait()


def layer(k, calls, rows, parts, C, n, tok, sib, cot, scot, ids, biases, x, w, acc, hid):
    first, last = k == 0, k == calls - 1
    D = 4 * C
    N = 8 * LANES
    T = rows * n
    shape = jax.ShapeDtypeStruct
    ins = [tok, sib, cot, scot, ids] + list(biases) + list(x)
    alias = {}
    outs = [shape(tok.shape, bf16), shape((2 * C, T), bf16)] + [shape((C, T), bf16)] * 3
    if first:
        ins += list(w)
    else:
        ins += [w, acc, hid]
        alias = {len(ins) - 1: 0}
        if not last:
            alias[len(ins) - 2] = 5
    if last:
        for kind in (f32, bf16):
            outs += [shape((C + SEGS, N // 2), kind), shape((len(REST) * C, N // 2), kind)]
    else:
        outs += [shape((2 * D + SEGS, N), f32)]
    if first:
        outs += [shape((2 * D, N), bf16)]
    w3 = 3 * LANES
    tall = n + SEGS * PAD
    scratch = (
        [
            pltpu.VMEM((2 * D, T), bf16),
            pltpu.VMEM((2 * D, N), bf16),
            pltpu.VMEM((w3, T), bf16),
            pltpu.VMEM((8, tall, LANES), f32),
            pltpu.VMEM((8, tall, LANES), f32),
        ]
        + [pltpu.VMEM((n, w3), f32)] * 4
        + [pltpu.VMEM((3, tall, LANES), f32)] * 2
        + [
            pltpu.VMEM((2 * C, T), bf16),
            pltpu.VMEM((T, N), bf16),
            pltpu.VMEM((D, T), bf16),
            pltpu.VMEM((2 * D + SEGS, N), f32),
            pltpu.VMEM((2 * D + SEGS, N // 2), bf16),
            pltpu.VMEM((D, LANES), f32),
            pltpu.VMEM((SEGS, N), f32),
            pltpu.VMEM((rows, SEGS, n), f32),
            pltpu.VMEM((rows, n, LANES), f32),
            pltpu.VMEM((rows, SEGS, LANES), jnp.int32),
            pltpu.VMEM((SEGS, N), f32),
            pltpu.SemaphoreType.DMA((8 + 2 * parts,)),
            pltpu.SemaphoreType.DMA((rows, 18)),
            pltpu.SemaphoreType.DMA((2, N // 2 // TILE, 1 + len(REST))),
        ]
    )
    return pl.pallas_call(
        functools.partial(layer_kernel, k, calls, rows, parts, C, n),
        out_shape=outs,
        in_specs=[ANY] * len(ins),
        out_specs=[ANY] * len(outs),
        scratch_shapes=scratch,
        input_output_aliases=alias,
        compiler_params=pltpu.CompilerParams(vmem_limit_bytes=60 << 20),
        cost_estimate=pl.CostEstimate(flops=1, bytes_accessed=1, transcendentals=0),
        name="layer",
    )(*ins)


def take_kernel(picks, n, tok, *refs):
    outs, (bufs, sem) = refs[:-2], refs[-2:]
    core = lax.axis_index("chan") & 1
    copies, sends = [], []
    for i, pick in enumerate(picks):
        for j, (pair, mine) in enumerate(pick):
            at = pl.ds(pl.multiple_of((2 * pair + (core if mine else 1 - core)) * n, n), n)
            copies.append(pltpu.make_async_copy(tok.at[:, at], bufs.at[i, :, j * n : (j + 1) * n], sem.at[i, j]))
            copies[-1].start()
    for i, pick in enumerate(picks):
        for copy in copies[i * len(pick) : (i + 1) * len(pick)]:
            copy.wait()
        sends.append(pltpu.make_async_copy(bufs.at[i], outs[i], sem.at[i, 0]))
        sends[-1].start()
    for send in sends:
        send.wait()


def take_rows(picks, C, n, tok):
    width = len(picks[0]) * n
    return pl.pallas_call(
        functools.partial(take_kernel, picks, n),
        out_shape=[jax.ShapeDtypeStruct((C, width), bf16)] * len(picks),
        in_specs=[ANY],
        out_specs=[ANY] * len(picks),
        scratch_shapes=[
            pltpu.VMEM((len(picks), C, width), bf16),
            pltpu.SemaphoreType.DMA((len(picks), len(picks[0]))),
        ],
        compiler_params=pltpu.CompilerParams(vmem_limit_bytes=8 << 20),
        cost_estimate=pl.CostEstimate(flops=1, bytes_accessed=1, transcendentals=0),
        name="take",
    )(tok)


def pack_kernel(C, w, b, out, b_out):
    tail = C - LANES
    parts = [w[g, 0:LANES].astype(f32) for g in range(3)] + [w[g, LANES:C].astype(f32) for g in range(3)]
    parts.append(jnp.zeros((LANES - 3 * tail, w.shape[2]), f32))
    out[...] = jnp.concatenate(parts, 0).T.astype(bf16)
    b_out[...] = jnp.zeros_like(b_out)
    for g in range(3):
        b_out[0:1, g * LANES : (g + 1) * LANES] = b[g : g + 1, 0:LANES]
        b_out[0:1, 3 * LANES + g * tail : 3 * LANES + (g + 1) * tail] = b[g : g + 1, LANES:C]


def pack(C, w, b):
    return pl.pallas_call(
        functools.partial(pack_kernel, C),
        out_shape=[
            jax.ShapeDtypeStruct((w.shape[2], 4 * LANES), bf16),
            jax.ShapeDtypeStruct((SEGS, 4 * LANES), f32),
        ],
        in_specs=[VMEM] * 2,
        out_specs=[VMEM] * 2,
        compiler_params=pltpu.CompilerParams(vmem_limit_bytes=4 << 20),
        cost_estimate=pl.CostEstimate(flops=1, bytes_accessed=1, transcendentals=0),
        name="pack",
    )(w, b)


def finish_kernel(k, rows, mine, C, n, near, far, *refs):
    total, sem = refs[-2:]
    if mine:
        grad = refs[-3]
    else:
        grad, hid = refs[-4:-2]
    core = lax.axis_index("chan") & 1
    which = core if mine else 1 - core
    copies = []

    def go(src, out, r):
        at = pl.ds(pl.multiple_of((2 * (k * rows + r) + which) * n, n), n)
        copies.append(pltpu.make_async_copy(src, out.at[:, at], sem.at[len(copies)]))
        copies[-1].start()

    for r in range(rows):
        at = slice(r * n, (r + 1) * n)
        if not mine:
            go(near.at[C : 2 * C, at], hid, r)
        total[:, at] = (near[0:C, at].astype(f32) + far[:, at].astype(f32)).astype(bf16)
        go(total.at[:, at], grad, r)
    for copy in copies:
        copy.wait()


def finish(k, rows, mine, C, n, total, near, far, grad, hid=None):
    ins = [near, far]
    specs = [VMEM] * 2
    shape = jax.ShapeDtypeStruct((C, total), bf16)
    outs = [shape]
    alias = {}
    for v in (grad, hid):
        if v is not None:
            alias[len(ins)] = 0 if v is grad else 1
            ins.append(v)
            specs.append(ANY)
    if hid is not None:
        outs.append(shape)
    return pl.pallas_call(
        functools.partial(finish_kernel, k, rows, mine, C, n),
        out_shape=outs,
        in_specs=specs,
        out_specs=[ANY] * len(outs),
        scratch_shapes=[pltpu.VMEM((C, rows * n), bf16), pltpu.SemaphoreType.DMA((2 * rows,))],
        input_output_aliases=alias,
        compiler_params=pltpu.CompilerParams(vmem_limit_bytes=8 << 20),
        cost_estimate=pl.CostEstimate(flops=1, bytes_accessed=1, transcendentals=0),
        name="finish",
    )(*ins)


def in_two(v):
    high = v.astype(bf16)
    low = v - high.astype(f32)
    at = lax.broadcasted_iota(jnp.int32, (SEGS, v.shape[1]), 0)
    return jnp.where(at == 0, high.astype(f32), jnp.where(at == 1, low, 0.0)).astype(bf16)


def from_two(v):
    v = v[...].astype(f32)
    return v[0:1] + v[1:2]


def leaf_kernel(C, own, other, out, b_out):
    b = own[C : C + 1] + from_two(other[C:])
    out[0:C] = (own[0:C] + other[0:C].astype(f32)).astype(bf16)
    out[C:] = in_two(b)
    b_out[...] = jnp.broadcast_to(b, (SEGS, b.shape[1]))


def leaf(C, own, other):
    half = own.shape[1]
    return pl.pallas_call(
        functools.partial(leaf_kernel, C),
        out_shape=[jax.ShapeDtypeStruct((C + SEGS, half), bf16), jax.ShapeDtypeStruct((SEGS, half), f32)],
        in_specs=[VMEM] * 2,
        out_specs=[VMEM] * 2,
        compiler_params=pltpu.CompilerParams(vmem_limit_bytes=4 << 20),
        cost_estimate=pl.CostEstimate(flops=1, bytes_accessed=1, transcendentals=0),
        name="leaf",
    )(own, other)


def split_kernel(C, own, other, b, s3, s5, s2, k6, k1, k4, k0):
    two = in_two(b[0:1])
    for i, out in enumerate((s3, s5, s2, k6, k1, k4, k0)):
        at = slice(i * C, (i + 1) * C)
        v = own[at, :] + other[at, :].astype(f32)
        if i < 3:
            out[0:C] = v.astype(bf16)
            out[C:] = two
        else:
            out[0:C] = v
            out[C:] = b[...]


def split(C, own, other, b):
    half = own.shape[1]
    shape = (C + SEGS, half)
    return pl.pallas_call(
        functools.partial(split_kernel, C),
        out_shape=[jax.ShapeDtypeStruct(shape, bf16)] * 3 + [jax.ShapeDtypeStruct(shape, f32)] * 4,
        in_specs=[VMEM] * 3,
        out_specs=[VMEM] * 7,
        compiler_params=pltpu.CompilerParams(vmem_limit_bytes=16 << 20),
        cost_estimate=pl.CostEstimate(flops=1, bytes_accessed=1, transcendentals=0),
        name="split",
    )(own, other, b)


def pass_on_kernel(C, kept, *refs):
    out = refs[-1]
    v, b = kept[0:C], kept[C : C + 1]
    for r in refs[:-1]:
        v = v + r[0:C].astype(f32)
        b = b + from_two(r[C:])
    out[0:C] = v.astype(bf16)
    out[C:] = in_two(b)


def pass_on(C, kept, *received):
    return pl.pallas_call(
        functools.partial(pass_on_kernel, C),
        out_shape=jax.ShapeDtypeStruct(kept.shape, bf16),
        in_specs=[VMEM] * (1 + len(received)),
        out_specs=VMEM,
        compiler_params=pltpu.CompilerParams(vmem_limit_bytes=4 << 20),
        cost_estimate=pl.CostEstimate(flops=1, bytes_accessed=1, transcendentals=0),
        name="pass_on",
    )(kept, *received)


def total_kernel(C, k0, r2, r1, r4, grad, bias, buf, b_buf, sem):
    v = k0[0:C] + r2[0:C].astype(f32) + (r1[0:C].astype(f32) + r4[0:C].astype(f32))
    t = v.T
    tail = C - LANES
    b = k0[C : C + 1] + from_two(r2[C:]) + (from_two(r1[C:]) + from_two(r4[C:]))
    for g in range(3):
        buf[g, 0:LANES] = t[g * LANES : (g + 1) * LANES]
        buf[g, LANES:C] = t[3 * LANES + g * tail : 3 * LANES + (g + 1) * tail]
        b_buf[g : g + 1, 0:LANES] = b[:, g * LANES : (g + 1) * LANES]
        b_buf[g : g + 1, LANES:C] = b[:, 3 * LANES + g * tail : 3 * LANES + (g + 1) * tail]
    copies = [pltpu.make_async_copy(buf, grad, sem.at[0]), pltpu.make_async_copy(b_buf, bias, sem.at[1])]
    for copy in copies:
        copy.start()
    for copy in copies:
        copy.wait()


def total_sum(C, k0, r2, r1, r4):
    shapes = ((3, C, C), (3, C))
    return pl.pallas_call(
        functools.partial(total_kernel, C),
        out_shape=[jax.ShapeDtypeStruct(shape, f32) for shape in shapes],
        in_specs=[VMEM] * 4,
        out_specs=[HBM] * 2,
        scratch_shapes=[pltpu.VMEM(shape, f32) for shape in shapes] + [pltpu.SemaphoreType.DMA((2,))],
        compiler_params=pltpu.CompilerParams(vmem_limit_bytes=4 << 20),
        cost_estimate=pl.CostEstimate(flops=1, bytes_accessed=1, transcendentals=0),
        name="total",
    )(k0, r2, r1, r4)


def local(chan, parts, tokens, weights, bias, segment_ids, cotangent):
    C, total = tokens.shape
    n = LEN
    pairs = total // n // 2
    rows = pairs // CALLS
    me = lax.axis_index("chan")
    core = me & 1

    def chan_move(v, j):
        return lax.ppermute(v, "chan", [(i, i ^ j) for i in range(chan)])

    def dp_move(v, j):
        return lax.ppermute(v, "dp", [(i, i ^ j) for i in range(parts)])

    def after(v, *others):
        return lax.optimization_barrier((v,) + others)[0]

    ids = segment_ids.reshape(2 * pairs * SEGS, n // SEGS)
    def other_rows(k, tok):
        picks = [[(k * rows + r, mine) for r in range(rows)] for mine in (True, False)]
        return take_rows(picks, C, n, tok)

    to_near, to_far = other_rows(0, tokens)
    near, far = chan_move(to_near, 2), chan_move(to_far, 3)
    xs = [(near, far)]
    shard, b_own = pack(C, after(weights, to_near), bias)
    sib = chan_move(tokens, 1)
    scot = chan_move(cotangent, 1)
    g = {0: shard, 4: dp_move(shard, 4), 1: dp_move(shard, 1)}
    def to_sibling(group):
        return chan_move(jnp.concatenate([g[j] for j in group], 0), 1)

    g4, own = lax.optimization_barrier((g[4], shard, sib))[:2]
    g[6] = dp_move(g4, 2)
    g[5] = dp_move(g4, 1)
    w_sib = [to_sibling(GROUPS[0])]
    biases = [b_own, chan_move(after(b_own, far), 1)]
    g[2] = dp_move(own, 2)
    g6, g1 = lax.optimization_barrier((g[6], g[1], near, scot))[:2]
    g[7] = dp_move(g6, 1)
    g[3] = dp_move(g1, 2)
    w_sib.append(to_sibling(GROUPS[1]))
    w_sib.append(to_sibling(GROUPS[2]))
    w = [g[j] for j in range(parts)] + w_sib
    for k in range(1, CALLS):
        to_near, to_far = other_rows(k, after(tokens, g[6]))
        xs.append((chan_move(to_near, 2), chan_move(to_far, 3)))

    acc = hid = grad = None
    moved = []
    for k in range(CALLS):
        out = layer(k, CALLS, rows, parts, C, n, tokens, sib, cotangent, scot, ids, biases, xs[k], w, acc, hid)
        if k == 0:
            w = out[-1]
        hid, to_sib, d_px, d_pd, own, acc = out[:6]
        if k == CALLS - 1:
            own_first, own_rest, sib_first, sib_rest = out[5:9]
            got = [v for m in moved for v in m[1:]]
            to_sib, d_px, d_pd, sib_first, sib_rest = lax.optimization_barrier(
                (to_sib, d_px, d_pd, sib_first, sib_rest, *got)
            )[:5]
            sib_first, sib_rest = chan_move(sib_first, 1), chan_move(sib_rest, 1)
        else:
            to_sib, d_px, d_pd = lax.optimization_barrier((to_sib, d_px, d_pd, *xs[k + 1]))[:3]
        moved.append((own, chan_move(d_px, 2), chan_move(to_sib, 1), chan_move(d_pd, 3)))

    def end(k, mine, *others):
        nonlocal grad, hid
        own, from_px, from_sib, from_pd = moved[k]
        if mine:
            (grad,) = finish(k, rows, True, C, n, total, after(own, *others), from_px, grad)
        else:
            grad, hid = finish(k, rows, False, C, n, total, after(from_sib, *others), from_pd, grad, hid)

    s7, b = leaf(C, own_first, sib_first)
    r7 = dp_move(s7, 1)
    for k in range(CALLS - 1):
        end(k, True, s7)
    s3, s5, s2, k6, k1, k4, k0 = split(C, own_rest, after(sib_rest, moved[-1][2], grad), b)
    r3, r5 = dp_move(s3, 2), dp_move(s5, 1)
    s6 = pass_on(C, k6, r7)
    r6 = dp_move(s6, 2)
    for k in range(CALLS - 1):
        end(k, False, s6, r5)
    r1, r2 = dp_move(pass_on(C, k1, after(r3, grad)), 1), dp_move(after(s2, r3), 2)
    s4 = pass_on(C, k4, r5, after(r6, grad))
    r4 = dp_move(s4, 4)
    end(CALLS - 1, True, s4, r1)
    end(CALLS - 1, False, s4)
    weight_grad, bias_grad = total_sum(C, k0, r2, r1, after(r4, grad))
    return (hid, grad, weight_grad, bias_grad)


def combine(earlier, later):
    return (earlier[0] * later[0], later[0] * earlier[1] + later[1])


def local_any(tokens, weights, bias, segment_ids, cotangent):
    width_part, total_rows = tokens.shape
    batch_rows = total_rows // MICRO
    grad_shard = jnp.zeros(weights.shape, jnp.float32)
    bias_total = jnp.zeros(bias.shape, jnp.float32)
    position = jnp.arange(batch_rows) % LEN
    hidden_parts = []
    input_parts = []
    for micro in range(MICRO):
        lower = micro * batch_rows
        upper = lower + batch_rows
        part_in = tokens[:, lower:upper]
        ids = segment_ids[lower:upper]
        cot = cotangent[:, lower:upper].astype(jnp.float32)
        before = jnp.concatenate([ids[:1], ids[:-1]], 0)
        carry_flag = (position > 0) & (ids == before)
        carry_on = jnp.where(carry_flag, 1.0, 0.0).astype(jnp.float32)
        gathered = lax.all_gather(part_in, "chan", axis=0, tiled=True)
        width = gathered.shape[0]
        shifted = jnp.concatenate([jnp.zeros((width, 1), jnp.bfloat16), gathered[:, :-1]], 1)
        previous = jnp.where(carry_flag[None, :], shifted, jnp.zeros((), jnp.bfloat16))
        joined_inputs = jnp.concatenate([gathered, previous], 0)
        preactivation = jnp.einsum(
            "gcr,rl->gcl",
            lax.all_gather(weights, "dp", axis=2, tiled=True),
            joined_inputs,
            preferred_element_type=jnp.float32,
        )
        preactivation = preactivation + bias[:, :, None]
        gate_z = jnp.tanh(preactivation[0])
        forget = jax.nn.sigmoid(preactivation[1])
        output_gate = jax.nn.sigmoid(preactivation[2])
        decay = forget * carry_on[None, :]
        source = (1.0 - forget) * gate_z
        cell = lax.associative_scan(combine, (decay, source), axis=1)[1]
        hidden_parts.append((output_gate * cell).astype(jnp.bfloat16))
        decay_next = jnp.concatenate([decay[:, 1:], jnp.zeros((width_part, 1), jnp.float32)], 1)
        dcell = lax.associative_scan(combine, (decay_next, cot * output_gate), reverse=True, axis=1)[1]
        cell_before = (
            jnp.concatenate([jnp.zeros((width_part, 1), jnp.float32), cell[:, :-1]], 1)
            * carry_on[None, :]
        )
        grad_z = dcell * (1.0 - forget) * (1.0 - gate_z * gate_z)
        grad_f = dcell * (cell_before - gate_z) * forget * (1.0 - forget)
        grad_o = cot * cell * output_gate * (1.0 - output_gate)
        dpre_low = jnp.stack([grad_z, grad_f, grad_o], 0).astype(jnp.bfloat16)
        bias_total = bias_total + jnp.sum(dpre_low.astype(jnp.float32), axis=2)
        weight_term = jnp.einsum(
            "gcl,rl->gcr", dpre_low, joined_inputs, preferred_element_type=jnp.float32
        )
        djoined = jnp.einsum(
            "gcl,gcr->rl",
            dpre_low,
            lax.all_gather(weights, "dp", axis=2, tiled=True),
            preferred_element_type=jnp.float32,
        )
        later = djoined[width:] * carry_on[None, :]
        later = jnp.concatenate([later[:, 1:], jnp.zeros((width, 1), jnp.float32)], 1)
        term = djoined[:width] + later
        input_parts.append(
            lax.psum_scatter(term, "chan", scatter_dimension=0, tiled=True).astype(jnp.bfloat16)
        )
        grad_shard = grad_shard + lax.psum_scatter(weight_term, "dp", scatter_dimension=2, tiled=True)
    bias_grad = lax.psum(bias_total, "dp")
    hidden = jnp.concatenate(hidden_parts, 1)
    input_grad = jnp.concatenate(input_parts, 1)
    return (hidden, input_grad, grad_shard, bias_grad)


def solution(mesh):
    chan, parts = mesh.shape["chan"], mesh.shape["dp"]
    in_specs = (P("chan", "dp"), P(None, "chan", "dp"), P(None, "chan"), P("dp"), P("chan", "dp"))
    out_specs = (P("chan", "dp"), P("chan", "dp"), P(None, "chan", "dp"), P(None, "chan"))

    def run(tokens, weights, bias, segment_ids, cotangent):
        C = tokens.shape[0] // chan
        row_part = weights.shape[2] // parts
        pairs = tokens.shape[1] // parts % (2 * LEN * CALLS) == 0
        tail = C - LANES
        fits = chan == 4 and parts == 8 and row_part == C and pairs and 0 < 3 * tail < LANES and tail % 32 == 0
        body = functools.partial(local, chan, parts) if fits else local_any
        return jax.shard_map(body, mesh=mesh, in_specs=in_specs, out_specs=out_specs, check_vma=False)(
            tokens, weights, bias, segment_ids, cotangent
        )

    return run
```

```python
import functools

import jax
import jax.numpy as jnp
from jax import lax
from jax.experimental import pallas as pl
from jax.experimental.pallas import tpu as pltpu
from jax.sharding import PartitionSpec as P

LEN = 1024
MICRO = 4
LANES = 128
SEGS = 8
PAD = 8
TILE = 512
UNROLL = 16
FTILE = 1024
TILES = LEN // TILE
CALLS = 2
REST = (3, 5, 2, 6, 1, 4, 0)
GROUPS = ((0, 1, 4), (2, 5, 6), (3, 7))
f32 = jnp.float32
bf16 = jnp.bfloat16
ANY = pl.BlockSpec(memory_space=pl.ANY)
VMEM = pl.BlockSpec(memory_space=pltpu.VMEM)
HBM = pl.BlockSpec(memory_space=pltpu.HBM)
SMEM = pl.BlockSpec(memory_space=pltpu.SMEM)


def dot(a, b, ca, cb):
    return lax.dot_general(a, b, (((ca,), (cb,)), ((), ())), preferred_element_type=f32)


def sigmoid(v):
    return 0.5 * jnp.tanh(0.5 * v) + 0.5


def layer_kernel(k, calls, rows, parts, C, n, *refs):
    first, last = k == 0, k == calls - 1
    refs = list(refs)
    tok, sib, cot, scot, ids, bias, bias_sib, x_near, x_far = refs[:9]
    refs = refs[9:]
    if first:
        w_in, refs = refs[: parts + len(GROUPS)], refs[parts + len(GROUPS) :]
    else:
        w_in, acc_in, refs = refs[0], refs[1], refs[3:]
    hid, to_sib, dx_px, dx_pd, dx_own = refs[:5]
    refs = refs[5:]
    if last:
        own_first, own_rest, sib_first, sib_rest, refs = *refs[:4], refs[4:]
    else:
        acc_out, refs = refs[0], refs[1:]
    if first:
        w_out, refs = refs[0], refs[1:]
    (xb, wb, cb, pre, gp, zs, fs, os_, cbs, ct, hs, hb, dp, dxb, accb, ab, nxt, sums, cl, ca_t, id_b, bb, sem, rsem, osem) = refs
    D = 4 * C
    tl = C - LANES
    steps = n // SEGS
    sp = steps + PAD
    half = 4 * LANES
    me, place = lax.axis_index("chan"), lax.axis_index("dp")
    core = me & 1

    def go(src, dst, i):
        copy = pltpu.make_async_copy(src, dst, sem.at[i])
        copy.start()
        return copy

    def here(r):
        return pl.ds(pl.multiple_of((2 * (k * rows + r) + core) * n, n), n)

    def span(r):
        return pl.ds(pl.multiple_of(r * n, n), n)

    def block(j):
        return pl.ds(pl.multiple_of((me ^ j) * C, 32), C)

    def seg(h):
        return pl.ds(pl.multiple_of(h * sp, 8), steps)

    def id_rows(r):
        return pl.ds(pl.multiple_of((2 * (k * rows + r) + core) * SEGS, SEGS), SEGS)

    def x_copies(r):
        from_row = span(r)
        pairs = (
            (tok.at[:, here(r)], xb.at[block(0), span(r)]),
            (sib.at[:, here(r)], xb.at[block(1), span(r)]),
            (x_near.at[:, from_row], xb.at[block(2), span(r)]),
            (x_far.at[:, from_row], xb.at[block(3), span(r)]),
            (ids.at[id_rows(r)], id_b.at[r]),
        )
        return [pltpu.make_async_copy(a, b, rsem.at[r, i]) for i, (a, b) in enumerate(pairs)]

    def c_copies(r):
        pairs = (
            (cot.at[0:LANES, here(r)], cb.at[0:LANES, span(r)]),
            (scot.at[0:LANES, here(r)], cb.at[LANES : 2 * LANES, span(r)]),
            (cot.at[LANES:C, here(r)], cb.at[2 * LANES : 2 * LANES + tl, span(r)]),
            (scot.at[LANES:C, here(r)], cb.at[2 * LANES + tl : 2 * LANES + 2 * tl, span(r)]),
        )
        return [pltpu.make_async_copy(a, b, rsem.at[r, 5 + i]) for i, (a, b) in enumerate(pairs)]

    def hidden_copies(r):
        pairs = (
            (hb.at[0:LANES, span(r)], hid.at[0:LANES, here(r)]),
            (hb.at[LANES : 2 * LANES, span(r)], to_sib.at[C : C + LANES, span(r)]),
            (hb.at[2 * LANES : 2 * LANES + tl, span(r)], hid.at[LANES:C, here(r)]),
            (hb.at[2 * LANES + tl : 2 * LANES + 2 * tl, span(r)], to_sib.at[C + LANES : 2 * C, span(r)]),
        )
        return [pltpu.make_async_copy(a, b, rsem.at[r, 10 + i]) for i, (a, b) in enumerate(pairs)]

    def grad_copies(r):
        outs = (dx_own, to_sib.at[0:C], dx_px, dx_pd)
        return [
            pltpu.make_async_copy(dxb.at[block(j), span(r)], out.at[:, span(r)], rsem.at[r, 14 + j])
            for j, out in enumerate(outs)
        ]

    for copy in x_copies(0):
        copy.start()
    if first:
        w_copies = []
        for j in range(parts):
            at = pl.ds(pl.multiple_of((place ^ j) * C, 32), C)
            w_copies.append(go(w_in[j], wb.at[at, 0:half], 8 + j))
            which = [j in group for group in GROUPS].index(True)
            spot = GROUPS[which].index(j)
            other = w_in[parts + which].at[spot * C : (spot + 1) * C]
            w_copies.append(go(other, wb.at[at, half : 2 * half], 8 + parts + j))
    else:
        w_copies = [go(w_in, wb, 0)]
    b_copies = [go(bias, bb.at[:, 0:half], 1), go(bias_sib, bb.at[:, half : 2 * half], 3)]
    for r in range(rows):
        for copy in (x_copies(r) if r else []) + c_copies(r):
            copy.start()
    sums[...] = jnp.zeros_like(sums)
    lane = lax.broadcasted_iota(jnp.int32, (SEGS, LANES), 1)
    edge = lax.broadcasted_iota(jnp.int32, (D, LANES), 1) == LANES - 1
    cols = [slice(q * LANES, (q + 1) * LANES) for q in range(3)]
    one = jnp.ones((SEGS, LANES), f32)
    zero = jnp.zeros((SEGS, LANES), f32)

    def strided(ref, t, q):
        return ref[q, pl.ds(t, SEGS, stride=sp), :]

    def now(t):
        return pl.ds(pl.multiple_of(t * SEGS, SEGS), SEGS)

    def arrive(r):
        for copy in x_copies(r):
            copy.wait()
        seg_ids = id_b[r]
        before = pltpu.roll(seg_ids, 1, 1)
        before = jnp.where(lane == 0, pltpu.roll(before, 1, 0), before)
        sub = lax.broadcasted_iota(jnp.int32, (SEGS, steps), 0)
        carry = jnp.where((seg_ids == before) & ((lane > 0) | (sub > 0)), 1.0, 0.0).astype(f32)
        for s in range(SEGS):
            cl[r, :, s * steps : (s + 1) * steps] = jnp.broadcast_to(carry[s : s + 1, :], (SEGS, steps))
        for t in range(steps):
            ca_t[r, t * SEGS : (t + 1) * SEGS, :] = jnp.broadcast_to(carry[:, t : t + 1], (SEGS, LANES))

    rb = 32

    def previous(r, i):
        o = pl.multiple_of(i * rb, rb)
        v = xb[pl.ds(o, rb), span(r)].astype(f32)
        xb[pl.ds(D + o, rb), span(r)] = (pltpu.roll(v, 1, 1) * cl[r, 0:1, :]).astype(bf16)

    def forward(r, i):
        o = pl.multiple_of(r * n + i * FTILE, FTILE)
        v = dot(xb[:, pl.ds(o, FTILE)], wb[...], 0, 0)
        for h in range(FTILE // steps):
            at = seg(i * (FTILE // steps) + h)
            for q in range(8):
                pre[q, at, :] = v[h * steps : (h + 1) * steps, q * LANES : (q + 1) * LANES]
            c = cb[:, pl.ds(pl.multiple_of(o + h * steps, LANES), steps)].astype(f32).T
            for q in range(3):
                ct[q, at, :] = c[:, q * LANES : (q + 1) * LANES]

    def round_tile(r, i):
        into = pl.ds(pl.multiple_of(r * n + i * steps, LANES), steps)
        for q in range(8):
            v = gp[q, seg(i), :].astype(bf16)
            dp[into, q * LANES : (q + 1) * LANES] = v
            v = v.astype(f32)
            a = v[0:SEGS]
            for s in range(SEGS, steps, SEGS):
                a = a + v[s : s + SEGS]
            sums[:, q * LANES : (q + 1) * LANES] += a
        for q in range(3):
            e = LANES if q < 2 else 2 * tl
            hb[q * LANES : q * LANES + e, into] = hs[q, seg(i), :].T.astype(bf16)[0:e]

    def input_tile(r, i):
        i = n // TILE - 1 - i
        o = pl.multiple_of(i * TILE, TILE)
        dj = dot(wb[...], dp[pl.ds(pl.multiple_of(r * n + o, TILE), TILE), :], 1, 1)
        after = nxt[...]
        for h in range(TILE // LANES - 1, -1, -1):
            at = slice(h * LANES, (h + 1) * LANES)
            into = pl.ds(pl.multiple_of(r * n + o + h * LANES, LANES), LANES)
            rolled = pltpu.roll(
                dj[D:, at] * cl[r, 0:1, pl.ds(pl.multiple_of(o + h * LANES, LANES), LANES)], LANES - 1, 1
            )
            dxb[:, into] = (dj[:D, at] + jnp.where(edge, after, rolled)).astype(bf16)
            after = rolled
        nxt[...] = after

    def weight_tile(r, i, add):
        at = pl.ds(pl.multiple_of(i * TILE, TILE), TILE)
        v = dot(xb[:, span(r)], dp[span(r), at], 1, 0)
        return (v + accb[0 : 2 * D, at] if add else v), at

    def weight_step(r, i):
        v, at = weight_tile(r, i, not (first and r == 0))
        accb[0 : 2 * D, at] = v

    def gates_step(r, b, t, state):
        gain, total = state
        v = [strided(pre, t, q) + b[q] for q in range(8)]
        u, w = v[3], v[7]
        tz = jnp.where(lane < tl, u, pltpu.roll(w, tl, 1))
        tf = jnp.where(lane < tl, pltpu.roll(u, LANES - tl, 1), w)
        to = jnp.where(lane < tl, pltpu.roll(u, LANES - 2 * tl, 1), pltpu.roll(w, LANES - tl, 1))
        z = [jnp.tanh(g) for g in (v[0], v[4], tz)]
        f = [sigmoid(g) for g in (v[1], v[5], tf)]
        o = [sigmoid(g) for g in (v[2], v[6], to)]
        at = now(t)
        ca = ca_t[r, at, :]
        gains, totals = [], []
        for q in range(3):
            zs[at, cols[q]] = z[q]
            fs[at, cols[q]] = f[q]
            os_[at, cols[q]] = o[q]
            gains.append(gain[q] * (f[q] * ca))
            totals.append(z[q] + f[q] * (ca * total[q] - z[q]))
        return tuple(gains), tuple(totals)

    def cell_step(r, t, state):
        cell, back, gain = state
        at = now(t)
        ca = ca_t[r, at, :]
        cells, backs, gains = [], [], []
        for q in range(3):
            z, f, o = zs[at, cols[q]], fs[at, cols[q]], os_[at, cols[q]]
            prev = ca * cell[q]
            cbs[at, cols[q]] = prev
            new = z + f * (prev - z)
            hs[q, pl.ds(t, SEGS, stride=sp), :] = o * new
            g = jnp.where(t == 0, one, gain[q] * (f * ca))
            cells.append(new)
            gains.append(g)
            backs.append(back[q] + g * (strided(ct, t, q) * o))
        return tuple(cells), tuple(backs), tuple(gains)

    def grad_step(r, i, later):
        t = steps - 1 - i
        at = now(t)
        ca = ca_t[r, at, :]
        gz, gf, go_, laters = [], [], [], []
        for q in range(3):
            z, f, o, prev = zs[at, cols[q]], fs[at, cols[q]], os_[at, cols[q]], cbs[at, cols[q]]
            c = strided(ct, t, q)
            dc = c * o + later[q]
            laters.append((f * ca) * dc)
            d = prev - z
            u = dc * (1.0 - f)
            gz.append(u * (1.0 - z * z))
            gf.append(u * (f * d))
            go_.append(c * (z + f * d) * (o * (1.0 - o)))
        z, f, o = gz[2], gf[2], go_[2]
        u = jnp.where(
            lane < tl,
            z,
            jnp.where(
                lane < 2 * tl,
                pltpu.roll(f, tl, 1),
                jnp.where(lane < 3 * tl, pltpu.roll(o, 2 * tl, 1), 0.0),
            ),
        )
        w = jnp.where(
            lane < tl,
            pltpu.roll(z, LANES - tl, 1),
            jnp.where(lane < 2 * tl, f, jnp.where(lane < 3 * tl, pltpu.roll(o, tl, 1), 0.0)),
        )
        for q, v in enumerate((gz[0], gf[0], go_[0], u, gz[1], gf[1], go_[1], w)):
            gp[q, pl.ds(t, SEGS, stride=sp), :] = v
        return tuple(laters)

    def scan(step, state, beside=None):
        if beside is None:
            return lax.fori_loop(0, steps, step, state, unroll=UNROLL)
        count = steps // TILES

        def body(i, state):
            beside(i)
            for u in range(count):
                state = step(i * count + u, state)
            return state

        return lax.fori_loop(0, TILES, body, state)

    def combine_segments(gain, total, backward):
        sub = lax.broadcasted_iota(jnp.int32, (SEGS, LANES), 0)
        d = 1
        while d < SEGS:
            there = sub < SEGS - d if backward else sub >= d
            by = SEGS - d if backward else d
            total = total + gain * jnp.where(there, pltpu.roll(total, by, 0), 0.0)
            gain = gain * jnp.where(there, pltpu.roll(gain, by, 0), 1.0)
            d *= 2
        there = sub < SEGS - 1 if backward else sub >= 1
        return jnp.where(there, pltpu.roll(total, SEGS - 1 if backward else 1, 0), 0.0)

    def row(r):
        b = [jnp.broadcast_to(bb[0:1, q * LANES : (q + 1) * LANES], (SEGS, LANES)) for q in range(8)]
        inputs = weights = None
        if r > 0:
            nxt[...] = jnp.zeros_like(nxt)
            inputs, weights = functools.partial(input_tile, r - 1), functools.partial(weight_step, r - 1)
        gain, total = scan(functools.partial(gates_step, r, b), ((one,) * 3, (zero,) * 3), inputs)
        if r > 0:
            for copy in grad_copies(r - 1):
                copy.start()
            if r == 1 and not first:
                pltpu.make_async_copy(acc_in, accb, sem.at[2]).wait()
        cell = tuple(combine_segments(gain[q], total[q], False) for q in range(3))
        cell, back, gain = scan(functools.partial(cell_step, r), (cell, (zero,) * 3, (one,) * 3), weights)
        enter = [fs[0:SEGS, cols[q]] * ca_t[r, 0:SEGS, :] for q in range(3)]
        later = tuple(combine_segments(enter[q] * gain[q], enter[q] * back[q], True) for q in range(3))
        scan(functools.partial(grad_step, r), later)

    arrive(0)
    lax.fori_loop(0, D // rb, lambda i, _: (previous(0, i), 0)[1], 0)
    for r in range(1, rows):
        arrive(r)
    for copy in w_copies + b_copies:
        copy.wait()
    if first:
        go(wb, w_out, 0)
    else:
        go(acc_in, accb, 2)
    for r in range(rows):
        for copy in c_copies(r):
            copy.wait()

        def forward_step(i, _):
            forward(r, i)
            if r + 1 < rows:
                for j in range(D // rb * FTILE // n):
                    previous(r + 1, i * (D // rb * FTILE // n) + j)
            if r > 0:
                for j in range(FTILE // steps):
                    round_tile(r - 1, i * (FTILE // steps) + j)
            return 0

        lax.fori_loop(0, n // FTILE, forward_step, 0)
        if r > 0:
            for copy in hidden_copies(r - 1):
                copy.start()
        row(r)
    end = rows - 1
    nxt[...] = jnp.zeros_like(nxt)
    if end == 0 and not first:
        pltpu.make_async_copy(acc_in, accb, sem.at[2]).wait()

    def input_step(i, _):
        for j in range(TILE // steps):
            round_tile(end, (TILES - 1 - i) * (TILE // steps) + j)
        input_tile(end, i)
        return 0

    lax.fori_loop(0, TILES, input_step, 0)
    for copy in hidden_copies(end) + grad_copies(end):
        copy.start()
    for q in range(8):
        at = slice(q * LANES, (q + 1) * LANES)
        s = sums[:, at]
        if not first:
            s = s + accb[2 * D :, at]
        if last:
            s = jnp.sum(s, 0, keepdims=True)
            if q >= 4:
                ab[2 * D :, (q - 4) * LANES : (q - 3) * LANES] = in_two(s)
        accb[2 * D :, at] = jnp.broadcast_to(s, (SEGS, LANES))

    def blocks_out(source, first_out, rest_out, which, i):
        at = pl.ds(pl.multiple_of(i * TILE, TILE), TILE)
        copies = []
        for place_in, j in enumerate((7,) + REST):
            rows_in = pl.ds(pl.multiple_of((place ^ j) * C, 32), C)
            out = first_out.at[0:C, at] if j == 7 else rest_out.at[(place_in - 1) * C : place_in * C, at]
            copies.append(pltpu.make_async_copy(source.at[rows_in, at], out, osem.at[which, i, place_in]))
        return copies

    def own_copies(i):
        if last:
            return blocks_out(accb, own_first, own_rest, 0, i)
        at = pl.ds(pl.multiple_of(i * TILE, TILE), TILE)
        return [pltpu.make_async_copy(accb.at[:, at], acc_out.at[:, at], sem.at[4 + i])]

    def own_step(i, _):
        v, at = weight_tile(end, i, not (first and rows == 1))
        accb[0 : 2 * D, at] = v
        for copy in own_copies(i):
            copy.start()
        return 0

    def sib_step(i, _):
        v, _ = weight_tile(end, half // TILE + i, not (first and rows == 1))
        ab[0 : 2 * D, pl.ds(pl.multiple_of(i * TILE, TILE), TILE)] = v.astype(bf16)
        for copy in blocks_out(ab, sib_first, sib_rest, 1, i):
            copy.start()
        return 0

    own_tiles = (half if last else 2 * half) // TILE
    tails = []
    if last:
        tails = [
            go(accb.at[2 * D :, 0:half], own_first.at[C:], 4),
            go(ab.at[2 * D :], sib_first.at[C:], 5),
        ]
        lax.fori_loop(0, half // TILE, sib_step, 0)
    lax.fori_loop(0, own_tiles, own_step, 0)
    for i in range(own_tiles):
        tails += own_copies(i)
    if last:
        for i in range(half // TILE):
            tails += blocks_out(ab, sib_first, sib_rest, 1, i)
    for copy in tails:
        copy.wait()
    if first:
        pltpu.make_async_copy(wb, w_out, sem.at[0]).wait()
    for r in range(rows):
        for copy in hidden_copies(r) + grad_copies(r):
            copy.wait()


def layer(k, calls, rows, parts, C, n, tok, sib, cot, scot, ids, biases, x, w, acc, hid):
    first, last = k == 0, k == calls - 1
    D = 4 * C
    N = 8 * LANES
    T = rows * n
    shape = jax.ShapeDtypeStruct
    ins = [tok, sib, cot, scot, ids] + list(biases) + list(x)
    alias = {}
    outs = [shape(tok.shape, bf16), shape((2 * C, T), bf16)] + [shape((C, T), bf16)] * 3
    if first:
        ins += list(w)
    else:
        ins += [w, acc, hid]
        alias = {len(ins) - 1: 0}
        if not last:
            alias[len(ins) - 2] = 5
    if last:
        for kind in (f32, bf16):
            outs += [shape((C + SEGS, N // 2), kind), shape((len(REST) * C, N // 2), kind)]
    else:
        outs += [shape((2 * D + SEGS, N), f32)]
    if first:
        outs += [shape((2 * D, N), bf16)]
    w3 = 3 * LANES
    tall = n + SEGS * PAD
    scratch = (
        [
            pltpu.VMEM((2 * D, T), bf16),
            pltpu.VMEM((2 * D, N), bf16),
            pltpu.VMEM((w3, T), bf16),
            pltpu.VMEM((8, tall, LANES), f32),
            pltpu.VMEM((8, tall, LANES), f32),
        ]
        + [pltpu.VMEM((n, w3), f32)] * 4
        + [pltpu.VMEM((3, tall, LANES), f32)] * 2
        + [
            pltpu.VMEM((2 * C, T), bf16),
            pltpu.VMEM((T, N), bf16),
            pltpu.VMEM((D, T), bf16),
            pltpu.VMEM((2 * D + SEGS, N), f32),
            pltpu.VMEM((2 * D + SEGS, N // 2), bf16),
            pltpu.VMEM((D, LANES), f32),
            pltpu.VMEM((SEGS, N), f32),
            pltpu.VMEM((rows, SEGS, n), f32),
            pltpu.VMEM((rows, n, LANES), f32),
            pltpu.VMEM((rows, SEGS, LANES), jnp.int32),
            pltpu.VMEM((SEGS, N), f32),
            pltpu.SemaphoreType.DMA((8 + 2 * parts,)),
            pltpu.SemaphoreType.DMA((rows, 18)),
            pltpu.SemaphoreType.DMA((2, N // 2 // TILE, 1 + len(REST))),
        ]
    )
    return pl.pallas_call(
        functools.partial(layer_kernel, k, calls, rows, parts, C, n),
        out_shape=outs,
        in_specs=[ANY] * len(ins),
        out_specs=[ANY] * len(outs),
        scratch_shapes=scratch,
        input_output_aliases=alias,
        compiler_params=pltpu.CompilerParams(vmem_limit_bytes=60 << 20),
        cost_estimate=pl.CostEstimate(flops=1, bytes_accessed=1, transcendentals=0),
        name="layer",
    )(*ins)


def take_kernel(picks, n, tok, *refs):
    outs, (bufs, sem) = refs[:-2], refs[-2:]
    core = lax.axis_index("chan") & 1
    copies, sends = [], []
    for i, pick in enumerate(picks):
        for j, (pair, mine) in enumerate(pick):
            at = pl.ds(pl.multiple_of((2 * pair + (core if mine else 1 - core)) * n, n), n)
            copies.append(pltpu.make_async_copy(tok.at[:, at], bufs.at[i, :, j * n : (j + 1) * n], sem.at[i, j]))
            copies[-1].start()
    for i, pick in enumerate(picks):
        for copy in copies[i * len(pick) : (i + 1) * len(pick)]:
            copy.wait()
        sends.append(pltpu.make_async_copy(bufs.at[i], outs[i], sem.at[i, 0]))
        sends[-1].start()
    for send in sends:
        send.wait()


def take_rows(picks, C, n, tok):
    width = len(picks[0]) * n
    return pl.pallas_call(
        functools.partial(take_kernel, picks, n),
        out_shape=[jax.ShapeDtypeStruct((C, width), bf16)] * len(picks),
        in_specs=[ANY],
        out_specs=[ANY] * len(picks),
        scratch_shapes=[
            pltpu.VMEM((len(picks), C, width), bf16),
            pltpu.SemaphoreType.DMA((len(picks), len(picks[0]))),
        ],
        compiler_params=pltpu.CompilerParams(vmem_limit_bytes=8 << 20),
        cost_estimate=pl.CostEstimate(flops=1, bytes_accessed=1, transcendentals=0),
        name="take",
    )(tok)


def pack_kernel(C, w, b, out, b_out):
    tail = C - LANES
    parts = [w[g, 0:LANES].astype(f32) for g in range(3)] + [w[g, LANES:C].astype(f32) for g in range(3)]
    parts.append(jnp.zeros((LANES - 3 * tail, w.shape[2]), f32))
    out[...] = jnp.concatenate(parts, 0).T.astype(bf16)
    b_out[...] = jnp.zeros_like(b_out)
    for g in range(3):
        b_out[0:1, g * LANES : (g + 1) * LANES] = b[g : g + 1, 0:LANES]
        b_out[0:1, 3 * LANES + g * tail : 3 * LANES + (g + 1) * tail] = b[g : g + 1, LANES:C]


def pack(C, w, b):
    return pl.pallas_call(
        functools.partial(pack_kernel, C),
        out_shape=[
            jax.ShapeDtypeStruct((w.shape[2], 4 * LANES), bf16),
            jax.ShapeDtypeStruct((SEGS, 4 * LANES), f32),
        ],
        in_specs=[VMEM] * 2,
        out_specs=[VMEM] * 2,
        compiler_params=pltpu.CompilerParams(vmem_limit_bytes=4 << 20),
        cost_estimate=pl.CostEstimate(flops=1, bytes_accessed=1, transcendentals=0),
        name="pack",
    )(w, b)


def finish_kernel(k, rows, mine, C, n, near, far, *refs):
    total, sem = refs[-2:]
    if mine:
        grad = refs[-3]
    else:
        grad, hid = refs[-4:-2]
    core = lax.axis_index("chan") & 1
    which = core if mine else 1 - core
    copies = []

    def go(src, out, r):
        at = pl.ds(pl.multiple_of((2 * (k * rows + r) + which) * n, n), n)
        copies.append(pltpu.make_async_copy(src, out.at[:, at], sem.at[len(copies)]))
        copies[-1].start()

    for r in range(rows):
        at = slice(r * n, (r + 1) * n)
        if not mine:
            go(near.at[C : 2 * C, at], hid, r)
        total[:, at] = (near[0:C, at].astype(f32) + far[:, at].astype(f32)).astype(bf16)
        go(total.at[:, at], grad, r)
    for copy in copies:
        copy.wait()


def finish(k, rows, mine, C, n, total, near, far, grad, hid=None):
    ins = [near, far]
    specs = [VMEM] * 2
    shape = jax.ShapeDtypeStruct((C, total), bf16)
    outs = [shape]
    alias = {}
    for v in (grad, hid):
        if v is not None:
            alias[len(ins)] = 0 if v is grad else 1
            ins.append(v)
            specs.append(ANY)
    if hid is not None:
        outs.append(shape)
    return pl.pallas_call(
        functools.partial(finish_kernel, k, rows, mine, C, n),
        out_shape=outs,
        in_specs=specs,
        out_specs=[ANY] * len(outs),
        scratch_shapes=[pltpu.VMEM((C, rows * n), bf16), pltpu.SemaphoreType.DMA((2 * rows,))],
        input_output_aliases=alias,
        compiler_params=pltpu.CompilerParams(vmem_limit_bytes=8 << 20),
        cost_estimate=pl.CostEstimate(flops=1, bytes_accessed=1, transcendentals=0),
        name="finish",
    )(*ins)


def in_two(v):
    high = v.astype(bf16)
    low = v - high.astype(f32)
    at = lax.broadcasted_iota(jnp.int32, (SEGS, v.shape[1]), 0)
    return jnp.where(at == 0, high.astype(f32), jnp.where(at == 1, low, 0.0)).astype(bf16)


def from_two(v):
    v = v[...].astype(f32)
    return v[0:1] + v[1:2]


def leaf_kernel(C, own, other, out, b_out):
    b = own[C : C + 1] + from_two(other[C:])
    out[0:C] = (own[0:C] + other[0:C].astype(f32)).astype(bf16)
    out[C:] = in_two(b)
    b_out[...] = jnp.broadcast_to(b, (SEGS, b.shape[1]))


def leaf(C, own, other):
    half = own.shape[1]
    return pl.pallas_call(
        functools.partial(leaf_kernel, C),
        out_shape=[jax.ShapeDtypeStruct((C + SEGS, half), bf16), jax.ShapeDtypeStruct((SEGS, half), f32)],
        in_specs=[VMEM] * 2,
        out_specs=[VMEM] * 2,
        compiler_params=pltpu.CompilerParams(vmem_limit_bytes=4 << 20),
        cost_estimate=pl.CostEstimate(flops=1, bytes_accessed=1, transcendentals=0),
        name="leaf",
    )(own, other)


def split_kernel(C, own, other, b, s3, s5, s2, k6, k1, k4, k0):
    two = in_two(b[0:1])
    for i, out in enumerate((s3, s5, s2, k6, k1, k4, k0)):
        at = slice(i * C, (i + 1) * C)
        v = own[at, :] + other[at, :].astype(f32)
        if i < 3:
            out[0:C] = v.astype(bf16)
            out[C:] = two
        else:
            out[0:C] = v
            out[C:] = b[...]


def split(C, own, other, b):
    half = own.shape[1]
    shape = (C + SEGS, half)
    return pl.pallas_call(
        functools.partial(split_kernel, C),
        out_shape=[jax.ShapeDtypeStruct(shape, bf16)] * 3 + [jax.ShapeDtypeStruct(shape, f32)] * 4,
        in_specs=[VMEM] * 3,
        out_specs=[VMEM] * 7,
        compiler_params=pltpu.CompilerParams(vmem_limit_bytes=16 << 20),
        cost_estimate=pl.CostEstimate(flops=1, bytes_accessed=1, transcendentals=0),
        name="split",
    )(own, other, b)


def pass_on_kernel(C, kept, *refs):
    out = refs[-1]
    v, b = kept[0:C], kept[C : C + 1]
    for r in refs[:-1]:
        v = v + r[0:C].astype(f32)
        b = b + from_two(r[C:])
    out[0:C] = v.astype(bf16)
    out[C:] = in_two(b)


def pass_on(C, kept, *received):
    return pl.pallas_call(
        functools.partial(pass_on_kernel, C),
        out_shape=jax.ShapeDtypeStruct(kept.shape, bf16),
        in_specs=[VMEM] * (1 + len(received)),
        out_specs=VMEM,
        compiler_params=pltpu.CompilerParams(vmem_limit_bytes=4 << 20),
        cost_estimate=pl.CostEstimate(flops=1, bytes_accessed=1, transcendentals=0),
        name="pass_on",
    )(kept, *received)


def total_kernel(C, k0, r2, r1, r4, grad, bias, buf, b_buf, sem):
    v = k0[0:C] + r2[0:C].astype(f32) + (r1[0:C].astype(f32) + r4[0:C].astype(f32))
    t = v.T
    tail = C - LANES
    b = k0[C : C + 1] + from_two(r2[C:]) + (from_two(r1[C:]) + from_two(r4[C:]))
    for g in range(3):
        buf[g, 0:LANES] = t[g * LANES : (g + 1) * LANES]
        buf[g, LANES:C] = t[3 * LANES + g * tail : 3 * LANES + (g + 1) * tail]
        b_buf[g : g + 1, 0:LANES] = b[:, g * LANES : (g + 1) * LANES]
        b_buf[g : g + 1, LANES:C] = b[:, 3 * LANES + g * tail : 3 * LANES + (g + 1) * tail]
    copies = [pltpu.make_async_copy(buf, grad, sem.at[0]), pltpu.make_async_copy(b_buf, bias, sem.at[1])]
    for copy in copies:
        copy.start()
    for copy in copies:
        copy.wait()


def total_sum(C, k0, r2, r1, r4):
    shapes = ((3, C, C), (3, C))
    return pl.pallas_call(
        functools.partial(total_kernel, C),
        out_shape=[jax.ShapeDtypeStruct(shape, f32) for shape in shapes],
        in_specs=[VMEM] * 4,
        out_specs=[HBM] * 2,
        scratch_shapes=[pltpu.VMEM(shape, f32) for shape in shapes] + [pltpu.SemaphoreType.DMA((2,))],
        compiler_params=pltpu.CompilerParams(vmem_limit_bytes=4 << 20),
        cost_estimate=pl.CostEstimate(flops=1, bytes_accessed=1, transcendentals=0),
        name="total",
    )(k0, r2, r1, r4)


def local(chan, parts, tokens, weights, bias, segment_ids, cotangent):
    C, total = tokens.shape
    n = LEN
    pairs = total // n // 2
    rows = pairs // CALLS
    me = lax.axis_index("chan")
    core = me & 1

    def chan_move(v, j):
        return lax.ppermute(v, "chan", [(i, i ^ j) for i in range(chan)])

    def dp_move(v, j):
        return lax.ppermute(v, "dp", [(i, i ^ j) for i in range(parts)])

    def after(v, *others):
        return lax.optimization_barrier((v,) + others)[0]

    ids = segment_ids.reshape(2 * pairs * SEGS, n // SEGS)
    def other_rows(k, tok):
        picks = [[(k * rows + r, mine) for r in range(rows)] for mine in (True, False)]
        return take_rows(picks, C, n, tok)

    to_near, to_far = other_rows(0, tokens)
    near, far = chan_move(to_near, 2), chan_move(to_far, 3)
    xs = [(near, far)]
    shard, b_own = pack(C, after(weights, to_near), bias)
    sib = chan_move(tokens, 1)
    scot = chan_move(cotangent, 1)
    g = {0: shard, 4: dp_move(shard, 4), 1: dp_move(shard, 1)}
    def to_sibling(group):
        return chan_move(jnp.concatenate([g[j] for j in group], 0), 1)

    g4, own = lax.optimization_barrier((g[4], shard, sib))[:2]
    g[6] = dp_move(g4, 2)
    g[5] = dp_move(g4, 1)
    w_sib = [to_sibling(GROUPS[0])]
    biases = [b_own, chan_move(after(b_own, far), 1)]
    g[2] = dp_move(own, 2)
    g6, g1 = lax.optimization_barrier((g[6], g[1], near, scot))[:2]
    g[7] = dp_move(g6, 1)
    g[3] = dp_move(g1, 2)
    w_sib.append(to_sibling(GROUPS[1]))
    w_sib.append(to_sibling(GROUPS[2]))
    w = [g[j] for j in range(parts)] + w_sib
    for k in range(1, CALLS):
        to_near, to_far = other_rows(k, after(tokens, g[6]))
        xs.append((chan_move(to_near, 2), chan_move(to_far, 3)))

    acc = hid = grad = None
    moved = []
    for k in range(CALLS):
        out = layer(k, CALLS, rows, parts, C, n, tokens, sib, cotangent, scot, ids, biases, xs[k], w, acc, hid)
        if k == 0:
            w = out[-1]
        hid, to_sib, d_px, d_pd, own, acc = out[:6]
        if k == CALLS - 1:
            own_first, own_rest, sib_first, sib_rest = out[5:9]
            got = [v for m in moved for v in m[1:]]
            to_sib, d_px, d_pd, sib_first, sib_rest = lax.optimization_barrier(
                (to_sib, d_px, d_pd, sib_first, sib_rest, *got)
            )[:5]
            sib_first, sib_rest = chan_move(sib_first, 1), chan_move(sib_rest, 1)
        else:
            to_sib, d_px, d_pd = lax.optimization_barrier((to_sib, d_px, d_pd, *xs[k + 1]))[:3]
        moved.append((own, chan_move(d_px, 2), chan_move(to_sib, 1), chan_move(d_pd, 3)))

    def end(k, mine, *others):
        nonlocal grad, hid
        own, from_px, from_sib, from_pd = moved[k]
        if mine:
            (grad,) = finish(k, rows, True, C, n, total, after(own, *others), from_px, grad)
        else:
            grad, hid = finish(k, rows, False, C, n, total, after(from_sib, *others), from_pd, grad, hid)

    s7, b = leaf(C, own_first, sib_first)
    r7 = dp_move(s7, 1)
    for k in range(CALLS - 1):
        end(k, True, s7)
    s3, s5, s2, k6, k1, k4, k0 = split(C, own_rest, after(sib_rest, moved[-1][2], grad), b)
    r3, r5 = dp_move(s3, 2), dp_move(s5, 1)
    s6 = pass_on(C, k6, r7)
    r6 = dp_move(s6, 2)
    for k in range(CALLS - 1):
        end(k, False, s6, r5)
    r1, r2 = dp_move(pass_on(C, k1, after(r3, grad)), 1), dp_move(after(s2, r3), 2)
    s4 = pass_on(C, k4, r5, after(r6, grad))
    r4 = dp_move(s4, 4)
    end(CALLS - 1, True, s4, r1)
    weight_grad, bias_grad = total_sum(C, k0, r2, r1, after(r4, grad))
    end(CALLS - 1, False, weight_grad)
    return (hid, grad, weight_grad, bias_grad)


def combine(earlier, later):
    return (earlier[0] * later[0], later[0] * earlier[1] + later[1])


def local_any(tokens, weights, bias, segment_ids, cotangent):
    width_part, total_rows = tokens.shape
    batch_rows = total_rows // MICRO
    grad_shard = jnp.zeros(weights.shape, jnp.float32)
    bias_total = jnp.zeros(bias.shape, jnp.float32)
    position = jnp.arange(batch_rows) % LEN
    hidden_parts = []
    input_parts = []
    for micro in range(MICRO):
        lower = micro * batch_rows
        upper = lower + batch_rows
        part_in = tokens[:, lower:upper]
        ids = segment_ids[lower:upper]
        cot = cotangent[:, lower:upper].astype(jnp.float32)
        before = jnp.concatenate([ids[:1], ids[:-1]], 0)
        carry_flag = (position > 0) & (ids == before)
        carry_on = jnp.where(carry_flag, 1.0, 0.0).astype(jnp.float32)
        gathered = lax.all_gather(part_in, "chan", axis=0, tiled=True)
        width = gathered.shape[0]
        shifted = jnp.concatenate([jnp.zeros((width, 1), jnp.bfloat16), gathered[:, :-1]], 1)
        previous = jnp.where(carry_flag[None, :], shifted, jnp.zeros((), jnp.bfloat16))
        joined_inputs = jnp.concatenate([gathered, previous], 0)
        preactivation = jnp.einsum(
            "gcr,rl->gcl",
            lax.all_gather(weights, "dp", axis=2, tiled=True),
            joined_inputs,
            preferred_element_type=jnp.float32,
        )
        preactivation = preactivation + bias[:, :, None]
        gate_z = jnp.tanh(preactivation[0])
        forget = jax.nn.sigmoid(preactivation[1])
        output_gate = jax.nn.sigmoid(preactivation[2])
        decay = forget * carry_on[None, :]
        source = (1.0 - forget) * gate_z
        cell = lax.associative_scan(combine, (decay, source), axis=1)[1]
        hidden_parts.append((output_gate * cell).astype(jnp.bfloat16))
        decay_next = jnp.concatenate([decay[:, 1:], jnp.zeros((width_part, 1), jnp.float32)], 1)
        dcell = lax.associative_scan(combine, (decay_next, cot * output_gate), reverse=True, axis=1)[1]
        cell_before = (
            jnp.concatenate([jnp.zeros((width_part, 1), jnp.float32), cell[:, :-1]], 1)
            * carry_on[None, :]
        )
        grad_z = dcell * (1.0 - forget) * (1.0 - gate_z * gate_z)
        grad_f = dcell * (cell_before - gate_z) * forget * (1.0 - forget)
        grad_o = cot * cell * output_gate * (1.0 - output_gate)
        dpre_low = jnp.stack([grad_z, grad_f, grad_o], 0).astype(jnp.bfloat16)
        bias_total = bias_total + jnp.sum(dpre_low.astype(jnp.float32), axis=2)
        weight_term = jnp.einsum(
            "gcl,rl->gcr", dpre_low, joined_inputs, preferred_element_type=jnp.float32
        )
        djoined = jnp.einsum(
            "gcl,gcr->rl",
            dpre_low,
            lax.all_gather(weights, "dp", axis=2, tiled=True),
            preferred_element_type=jnp.float32,
        )
        later = djoined[width:] * carry_on[None, :]
        later = jnp.concatenate([later[:, 1:], jnp.zeros((width, 1), jnp.float32)], 1)
        term = djoined[:width] + later
        input_parts.append(
            lax.psum_scatter(term, "chan", scatter_dimension=0, tiled=True).astype(jnp.bfloat16)
        )
        grad_shard = grad_shard + lax.psum_scatter(weight_term, "dp", scatter_dimension=2, tiled=True)
    bias_grad = lax.psum(bias_total, "dp")
    hidden = jnp.concatenate(hidden_parts, 1)
    input_grad = jnp.concatenate(input_parts, 1)
    return (hidden, input_grad, grad_shard, bias_grad)


def solution(mesh):
    chan, parts = mesh.shape["chan"], mesh.shape["dp"]
    in_specs = (P("chan", "dp"), P(None, "chan", "dp"), P(None, "chan"), P("dp"), P("chan", "dp"))
    out_specs = (P("chan", "dp"), P("chan", "dp"), P(None, "chan", "dp"), P(None, "chan"))

    def run(tokens, weights, bias, segment_ids, cotangent):
        C = tokens.shape[0] // chan
        row_part = weights.shape[2] // parts
        pairs = tokens.shape[1] // parts % (2 * LEN * CALLS) == 0
        tail = C - LANES
        fits = chan == 4 and parts == 8 and row_part == C and pairs and 0 < 3 * tail < LANES and tail % 32 == 0
        body = functools.partial(local, chan, parts) if fits else local_any
        return jax.shard_map(body, mesh=mesh, in_specs=in_specs, out_specs=out_specs, check_vma=False)(
            tokens, weights, bias, segment_ids, cotangent
        )

    return run
```

```python
import functools

import jax
import jax.numpy as jnp
from jax import lax
from jax.experimental import pallas as pl
from jax.experimental.pallas import tpu as pltpu
from jax.sharding import PartitionSpec as P

LEN = 1024
MICRO = 4
LANES = 128
SEGS = 8
PAD = 8
TILE = 512
UNROLL = 16
FTILE = 1024
TILES = LEN // TILE
CALLS = 2
REST = (3, 5, 2, 6, 1, 4, 0)
GROUPS = ((0, 1, 4), (5, 6), (2, 3, 7))
f32 = jnp.float32
bf16 = jnp.bfloat16
ANY = pl.BlockSpec(memory_space=pl.ANY)
VMEM = pl.BlockSpec(memory_space=pltpu.VMEM)
HBM = pl.BlockSpec(memory_space=pltpu.HBM)
SMEM = pl.BlockSpec(memory_space=pltpu.SMEM)


def dot(a, b, ca, cb):
    return lax.dot_general(a, b, (((ca,), (cb,)), ((), ())), preferred_element_type=f32)


def sigmoid(v):
    return 0.5 * jnp.tanh(0.5 * v) + 0.5


def layer_kernel(k, calls, rows, parts, C, n, *refs):
    first, last = k == 0, k == calls - 1
    refs = list(refs)
    tok, sib, cot, scot, ids, bias, bias_sib, x_near, x_far = refs[:9]
    refs = refs[9:]
    if first:
        w_in, refs = refs[: parts + len(GROUPS)], refs[parts + len(GROUPS) :]
    else:
        w_in, acc_in, refs = refs[0], refs[1], refs[3:]
    hid, to_sib, dx_px, dx_pd, dx_own = refs[:5]
    refs = refs[5:]
    if last:
        own_first, own_rest, sib_first, sib_rest, refs = *refs[:4], refs[4:]
    else:
        acc_out, refs = refs[0], refs[1:]
    if first:
        w_out, refs = refs[0], refs[1:]
    (xb, wb, cb, pre, gp, zs, fs, os_, cbs, ct, hs, hb, dp, dxb, accb, ab, nxt, sums, cl, ca_t, id_b, bb, sem, rsem, osem) = refs
    D = 4 * C
    tl = C - LANES
    steps = n // SEGS
    sp = steps + PAD
    half = 4 * LANES
    me, place = lax.axis_index("chan"), lax.axis_index("dp")
    core = me & 1

    def go(src, dst, i):
        copy = pltpu.make_async_copy(src, dst, sem.at[i])
        copy.start()
        return copy

    def here(r):
        return pl.ds(pl.multiple_of((2 * (k * rows + r) + core) * n, n), n)

    def span(r):
        return pl.ds(pl.multiple_of(r * n, n), n)

    def block(j):
        return pl.ds(pl.multiple_of((me ^ j) * C, 32), C)

    def seg(h):
        return pl.ds(pl.multiple_of(h * sp, 8), steps)

    def id_rows(r):
        return pl.ds(pl.multiple_of((2 * (k * rows + r) + core) * SEGS, SEGS), SEGS)

    def x_copies(r):
        from_row = span(r)
        pairs = (
            (tok.at[:, here(r)], xb.at[block(0), span(r)]),
            (sib.at[:, here(r)], xb.at[block(1), span(r)]),
            (x_near.at[:, from_row], xb.at[block(2), span(r)]),
            (x_far.at[:, from_row], xb.at[block(3), span(r)]),
            (ids.at[id_rows(r)], id_b.at[r]),
        )
        return [pltpu.make_async_copy(a, b, rsem.at[r, i]) for i, (a, b) in enumerate(pairs)]

    def c_copies(r):
        pairs = (
            (cot.at[0:LANES, here(r)], cb.at[0:LANES, span(r)]),
            (scot.at[0:LANES, here(r)], cb.at[LANES : 2 * LANES, span(r)]),
            (cot.at[LANES:C, here(r)], cb.at[2 * LANES : 2 * LANES + tl, span(r)]),
            (scot.at[LANES:C, here(r)], cb.at[2 * LANES + tl : 2 * LANES + 2 * tl, span(r)]),
        )
        return [pltpu.make_async_copy(a, b, rsem.at[r, 5 + i]) for i, (a, b) in enumerate(pairs)]

    def hidden_copies(r):
        pairs = (
            (hb.at[0:LANES, span(r)], hid.at[0:LANES, here(r)]),
            (hb.at[LANES : 2 * LANES, span(r)], to_sib.at[C : C + LANES, span(r)]),
            (hb.at[2 * LANES : 2 * LANES + tl, span(r)], hid.at[LANES:C, here(r)]),
            (hb.at[2 * LANES + tl : 2 * LANES + 2 * tl, span(r)], to_sib.at[C + LANES : 2 * C, span(r)]),
        )
        return [pltpu.make_async_copy(a, b, rsem.at[r, 10 + i]) for i, (a, b) in enumerate(pairs)]

    def grad_copies(r):
        outs = (dx_own, to_sib.at[0:C], dx_px, dx_pd)
        return [
            pltpu.make_async_copy(dxb.at[block(j), span(r)], out.at[:, span(r)], rsem.at[r, 14 + j])
            for j, out in enumerate(outs)
        ]

    for copy in x_copies(0):
        copy.start()
    if first:
        w_copies = []
        for j in range(parts):
            at = pl.ds(pl.multiple_of((place ^ j) * C, 32), C)
            w_copies.append(go(w_in[j], wb.at[at, 0:half], 8 + j))
            which = [j in group for group in GROUPS].index(True)
            spot = GROUPS[which].index(j)
            other = w_in[parts + which].at[spot * C : (spot + 1) * C]
            w_copies.append(go(other, wb.at[at, half : 2 * half], 8 + parts + j))
    else:
        w_copies = [go(w_in, wb, 0)]
    b_copies = [go(bias, bb.at[:, 0:half], 1), go(bias_sib, bb.at[:, half : 2 * half], 3)]
    for r in range(rows):
        for copy in (x_copies(r) if r else []) + c_copies(r):
            copy.start()
    sums[...] = jnp.zeros_like(sums)
    lane = lax.broadcasted_iota(jnp.int32, (SEGS, LANES), 1)
    edge = lax.broadcasted_iota(jnp.int32, (D, LANES), 1) == LANES - 1
    cols = [slice(q * LANES, (q + 1) * LANES) for q in range(3)]
    one = jnp.ones((SEGS, LANES), f32)
    zero = jnp.zeros((SEGS, LANES), f32)

    def strided(ref, t, q):
        return ref[q, pl.ds(t, SEGS, stride=sp), :]

    def now(t):
        return pl.ds(pl.multiple_of(t * SEGS, SEGS), SEGS)

    def arrive(r):
        for copy in x_copies(r):
            copy.wait()
        seg_ids = id_b[r]
        before = pltpu.roll(seg_ids, 1, 1)
        before = jnp.where(lane == 0, pltpu.roll(before, 1, 0), before)
        sub = lax.broadcasted_iota(jnp.int32, (SEGS, steps), 0)
        carry = jnp.where((seg_ids == before) & ((lane > 0) | (sub > 0)), 1.0, 0.0).astype(f32)
        for s in range(SEGS):
            cl[r, :, s * steps : (s + 1) * steps] = jnp.broadcast_to(carry[s : s + 1, :], (SEGS, steps))
        for t in range(steps):
            ca_t[r, t * SEGS : (t + 1) * SEGS, :] = jnp.broadcast_to(carry[:, t : t + 1], (SEGS, LANES))

    rb = 32

    def previous(r, i):
        o = pl.multiple_of(i * rb, rb)
        v = xb[pl.ds(o, rb), span(r)].astype(f32)
        xb[pl.ds(D + o, rb), span(r)] = (pltpu.roll(v, 1, 1) * cl[r, 0:1, :]).astype(bf16)

    def forward(r, i):
        o = pl.multiple_of(r * n + i * FTILE, FTILE)
        v = dot(xb[:, pl.ds(o, FTILE)], wb[...], 0, 0)
        for h in range(FTILE // steps):
            at = seg(i * (FTILE // steps) + h)
            for q in range(8):
                pre[q, at, :] = v[h * steps : (h + 1) * steps, q * LANES : (q + 1) * LANES]
            c = cb[:, pl.ds(pl.multiple_of(o + h * steps, LANES), steps)].astype(f32).T
            for q in range(3):
                ct[q, at, :] = c[:, q * LANES : (q + 1) * LANES]

    def round_tile(r, i):
        into = pl.ds(pl.multiple_of(r * n + i * steps, LANES), steps)
        for q in range(8):
            v = gp[q, seg(i), :].astype(bf16)
            dp[into, q * LANES : (q + 1) * LANES] = v
            v = v.astype(f32)
            a = v[0:SEGS]
            for s in range(SEGS, steps, SEGS):
                a = a + v[s : s + SEGS]
            sums[:, q * LANES : (q + 1) * LANES] += a
        for q in range(3):
            e = LANES if q < 2 else 2 * tl
            hb[q * LANES : q * LANES + e, into] = hs[q, seg(i), :].T.astype(bf16)[0:e]

    def input_tile(r, i):
        i = n // TILE - 1 - i
        o = pl.multiple_of(i * TILE, TILE)
        dj = dot(wb[...], dp[pl.ds(pl.multiple_of(r * n + o, TILE), TILE), :], 1, 1)
        after = nxt[...]
        for h in range(TILE // LANES - 1, -1, -1):
            at = slice(h * LANES, (h + 1) * LANES)
            into = pl.ds(pl.multiple_of(r * n + o + h * LANES, LANES), LANES)
            rolled = pltpu.roll(
                dj[D:, at] * cl[r, 0:1, pl.ds(pl.multiple_of(o + h * LANES, LANES), LANES)], LANES - 1, 1
            )
            dxb[:, into] = (dj[:D, at] + jnp.where(edge, after, rolled)).astype(bf16)
            after = rolled
        nxt[...] = after

    def weight_tile(r, i, add):
        at = pl.ds(pl.multiple_of(i * TILE, TILE), TILE)
        v = dot(xb[:, span(r)], dp[span(r), at], 1, 0)
        return (v + accb[0 : 2 * D, at] if add else v), at

    def weight_step(r, i):
        v, at = weight_tile(r, i, not (first and r == 0))
        accb[0 : 2 * D, at] = v

    def gates_step(r, b, t, state):
        gain, total = state
        v = [strided(pre, t, q) + b[q] for q in range(8)]
        u, w = v[3], v[7]
        tz = jnp.where(lane < tl, u, pltpu.roll(w, tl, 1))
        tf = jnp.where(lane < tl, pltpu.roll(u, LANES - tl, 1), w)
        to = jnp.where(lane < tl, pltpu.roll(u, LANES - 2 * tl, 1), pltpu.roll(w, LANES - tl, 1))
        z = [jnp.tanh(g) for g in (v[0], v[4], tz)]
        f = [sigmoid(g) for g in (v[1], v[5], tf)]
        o = [sigmoid(g) for g in (v[2], v[6], to)]
        at = now(t)
        ca = ca_t[r, at, :]
        gains, totals = [], []
        for q in range(3):
            zs[at, cols[q]] = z[q]
            fs[at, cols[q]] = f[q]
            os_[at, cols[q]] = o[q]
            gains.append(gain[q] * (f[q] * ca))
            totals.append(z[q] + f[q] * (ca * total[q] - z[q]))
        return tuple(gains), tuple(totals)

    def cell_step(r, t, state):
        cell, back, gain = state
        at = now(t)
        ca = ca_t[r, at, :]
        cells, backs, gains = [], [], []
        for q in range(3):
            z, f, o = zs[at, cols[q]], fs[at, cols[q]], os_[at, cols[q]]
            prev = ca * cell[q]
            cbs[at, cols[q]] = prev
            new = z + f * (prev - z)
            hs[q, pl.ds(t, SEGS, stride=sp), :] = o * new
            g = jnp.where(t == 0, one, gain[q] * (f * ca))
            cells.append(new)
            gains.append(g)
            backs.append(back[q] + g * (strided(ct, t, q) * o))
        return tuple(cells), tuple(backs), tuple(gains)

    def grad_step(r, i, later):
        t = steps - 1 - i
        at = now(t)
        ca = ca_t[r, at, :]
        gz, gf, go_, laters = [], [], [], []
        for q in range(3):
            z, f, o, prev = zs[at, cols[q]], fs[at, cols[q]], os_[at, cols[q]], cbs[at, cols[q]]
            c = strided(ct, t, q)
            dc = c * o + later[q]
            laters.append((f * ca) * dc)
            d = prev - z
            u = dc * (1.0 - f)
            gz.append(u * (1.0 - z * z))
            gf.append(u * (f * d))
            go_.append(c * (z + f * d) * (o * (1.0 - o)))
        z, f, o = gz[2], gf[2], go_[2]
        u = jnp.where(
            lane < tl,
            z,
            jnp.where(
                lane < 2 * tl,
                pltpu.roll(f, tl, 1),
                jnp.where(lane < 3 * tl, pltpu.roll(o, 2 * tl, 1), 0.0),
            ),
        )
        w = jnp.where(
            lane < tl,
            pltpu.roll(z, LANES - tl, 1),
            jnp.where(lane < 2 * tl, f, jnp.where(lane < 3 * tl, pltpu.roll(o, tl, 1), 0.0)),
        )
        for q, v in enumerate((gz[0], gf[0], go_[0], u, gz[1], gf[1], go_[1], w)):
            gp[q, pl.ds(t, SEGS, stride=sp), :] = v
        return tuple(laters)

    def scan(step, state, beside=None):
        if beside is None:
            return lax.fori_loop(0, steps, step, state, unroll=UNROLL)
        count = steps // TILES

        def body(i, state):
            beside(i)
            for u in range(count):
                state = step(i * count + u, state)
            return state

        return lax.fori_loop(0, TILES, body, state)

    def combine_segments(gain, total, backward):
        sub = lax.broadcasted_iota(jnp.int32, (SEGS, LANES), 0)
        d = 1
        while d < SEGS:
            there = sub < SEGS - d if backward else sub >= d
            by = SEGS - d if backward else d
            total = total + gain * jnp.where(there, pltpu.roll(total, by, 0), 0.0)
            gain = gain * jnp.where(there, pltpu.roll(gain, by, 0), 1.0)
            d *= 2
        there = sub < SEGS - 1 if backward else sub >= 1
        return jnp.where(there, pltpu.roll(total, SEGS - 1 if backward else 1, 0), 0.0)

    def row(r):
        b = [jnp.broadcast_to(bb[0:1, q * LANES : (q + 1) * LANES], (SEGS, LANES)) for q in range(8)]
        inputs = weights = None
        if r > 0:
            nxt[...] = jnp.zeros_like(nxt)
            inputs, weights = functools.partial(input_tile, r - 1), functools.partial(weight_step, r - 1)
        gain, total = scan(functools.partial(gates_step, r, b), ((one,) * 3, (zero,) * 3), inputs)
        if r > 0:
            for copy in grad_copies(r - 1):
                copy.start()
            if r == 1 and not first:
                pltpu.make_async_copy(acc_in, accb, sem.at[2]).wait()
        cell = tuple(combine_segments(gain[q], total[q], False) for q in range(3))
        cell, back, gain = scan(functools.partial(cell_step, r), (cell, (zero,) * 3, (one,) * 3), weights)
        enter = [fs[0:SEGS, cols[q]] * ca_t[r, 0:SEGS, :] for q in range(3)]
        later = tuple(combine_segments(enter[q] * gain[q], enter[q] * back[q], True) for q in range(3))
        scan(functools.partial(grad_step, r), later)

    arrive(0)
    lax.fori_loop(0, D // rb, lambda i, _: (previous(0, i), 0)[1], 0)
    for r in range(1, rows):
        arrive(r)
    for copy in w_copies + b_copies:
        copy.wait()
    if first:
        go(wb, w_out, 0)
    else:
        go(acc_in, accb, 2)
    for r in range(rows):
        for copy in c_copies(r):
            copy.wait()

        def forward_step(i, _):
            forward(r, i)
            if r + 1 < rows:
                for j in range(D // rb * FTILE // n):
                    previous(r + 1, i * (D // rb * FTILE // n) + j)
            if r > 0:
                for j in range(FTILE // steps):
                    round_tile(r - 1, i * (FTILE // steps) + j)
            return 0

        lax.fori_loop(0, n // FTILE, forward_step, 0)
        if r > 0:
            for copy in hidden_copies(r - 1):
                copy.start()
        row(r)
    end = rows - 1
    nxt[...] = jnp.zeros_like(nxt)
    if end == 0 and not first:
        pltpu.make_async_copy(acc_in, accb, sem.at[2]).wait()

    def input_step(i, _):
        for j in range(TILE // steps):
            round_tile(end, (TILES - 1 - i) * (TILE // steps) + j)
        input_tile(end, i)
        return 0

    lax.fori_loop(0, TILES, input_step, 0)
    for copy in hidden_copies(end) + grad_copies(end):
        copy.start()
    for q in range(8):
        at = slice(q * LANES, (q + 1) * LANES)
        s = sums[:, at]
        if not first:
            s = s + accb[2 * D :, at]
        if last:
            s = jnp.sum(s, 0, keepdims=True)
            if q >= 4:
                ab[2 * D :, (q - 4) * LANES : (q - 3) * LANES] = in_two(s)
        accb[2 * D :, at] = jnp.broadcast_to(s, (SEGS, LANES))

    def blocks_out(source, first_out, rest_out, which, i):
        at = pl.ds(pl.multiple_of(i * TILE, TILE), TILE)
        copies = []
        for place_in, j in enumerate((7,) + REST):
            rows_in = pl.ds(pl.multiple_of((place ^ j) * C, 32), C)
            out = first_out.at[0:C, at] if j == 7 else rest_out.at[(place_in - 1) * C : place_in * C, at]
            copies.append(pltpu.make_async_copy(source.at[rows_in, at], out, osem.at[which, i, place_in]))
        return copies

    def own_copies(i):
        if last:
            return blocks_out(accb, own_first, own_rest, 0, i)
        at = pl.ds(pl.multiple_of(i * TILE, TILE), TILE)
        return [pltpu.make_async_copy(accb.at[:, at], acc_out.at[:, at], sem.at[4 + i])]

    def own_step(i, _):
        v, at = weight_tile(end, i, not (first and rows == 1))
        accb[0 : 2 * D, at] = v
        for copy in own_copies(i):
            copy.start()
        return 0

    def sib_step(i, _):
        v, _ = weight_tile(end, half // TILE + i, not (first and rows == 1))
        ab[0 : 2 * D, pl.ds(pl.multiple_of(i * TILE, TILE), TILE)] = v.astype(bf16)
        for copy in blocks_out(ab, sib_first, sib_rest, 1, i):
            copy.start()
        return 0

    own_tiles = (half if last else 2 * half) // TILE
    tails = []
    if last:
        tails = [
            go(accb.at[2 * D :, 0:half], own_first.at[C:], 4),
            go(ab.at[2 * D :], sib_first.at[C:], 5),
        ]
        lax.fori_loop(0, half // TILE, sib_step, 0)
    lax.fori_loop(0, own_tiles, own_step, 0)
    for i in range(own_tiles):
        tails += own_copies(i)
    if last:
        for i in range(half // TILE):
            tails += blocks_out(ab, sib_first, sib_rest, 1, i)
    for copy in tails:
        copy.wait()
    if first:
        pltpu.make_async_copy(wb, w_out, sem.at[0]).wait()
    for r in range(rows):
        for copy in hidden_copies(r) + grad_copies(r):
            copy.wait()


def layer(k, calls, rows, parts, C, n, tok, sib, cot, scot, ids, biases, x, w, acc, hid):
    first, last = k == 0, k == calls - 1
    D = 4 * C
    N = 8 * LANES
    T = rows * n
    shape = jax.ShapeDtypeStruct
    ins = [tok, sib, cot, scot, ids] + list(biases) + list(x)
    alias = {}
    outs = [shape(tok.shape, bf16), shape((2 * C, T), bf16)] + [shape((C, T), bf16)] * 3
    if first:
        ins += list(w)
    else:
        ins += [w, acc, hid]
        alias = {len(ins) - 1: 0}
        if not last:
            alias[len(ins) - 2] = 5
    if last:
        for kind in (f32, bf16):
            outs += [shape((C + SEGS, N // 2), kind), shape((len(REST) * C, N // 2), kind)]
    else:
        outs += [shape((2 * D + SEGS, N), f32)]
    if first:
        outs += [shape((2 * D, N), bf16)]
    w3 = 3 * LANES
    tall = n + SEGS * PAD
    scratch = (
        [
            pltpu.VMEM((2 * D, T), bf16),
            pltpu.VMEM((2 * D, N), bf16),
            pltpu.VMEM((w3, T), bf16),
            pltpu.VMEM((8, tall, LANES), f32),
            pltpu.VMEM((8, tall, LANES), f32),
        ]
        + [pltpu.VMEM((n, w3), f32)] * 4
        + [pltpu.VMEM((3, tall, LANES), f32)] * 2
        + [
            pltpu.VMEM((2 * C, T), bf16),
            pltpu.VMEM((T, N), bf16),
            pltpu.VMEM((D, T), bf16),
            pltpu.VMEM((2 * D + SEGS, N), f32),
            pltpu.VMEM((2 * D + SEGS, N // 2), bf16),
            pltpu.VMEM((D, LANES), f32),
            pltpu.VMEM((SEGS, N), f32),
            pltpu.VMEM((rows, SEGS, n), f32),
            pltpu.VMEM((rows, n, LANES), f32),
            pltpu.VMEM((rows, SEGS, LANES), jnp.int32),
            pltpu.VMEM((SEGS, N), f32),
            pltpu.SemaphoreType.DMA((8 + 2 * parts,)),
            pltpu.SemaphoreType.DMA((rows, 18)),
            pltpu.SemaphoreType.DMA((2, N // 2 // TILE, 1 + len(REST))),
        ]
    )
    return pl.pallas_call(
        functools.partial(layer_kernel, k, calls, rows, parts, C, n),
        out_shape=outs,
        in_specs=[ANY] * len(ins),
        out_specs=[ANY] * len(outs),
        scratch_shapes=scratch,
        input_output_aliases=alias,
        compiler_params=pltpu.CompilerParams(vmem_limit_bytes=54 << 20),
        cost_estimate=pl.CostEstimate(flops=1, bytes_accessed=1, transcendentals=0),
        name="layer",
    )(*ins)


def take_kernel(picks, n, tok, *refs):
    outs, (bufs, sem) = refs[:-2], refs[-2:]
    core = lax.axis_index("chan") & 1
    copies, sends = [], []
    for i, pick in enumerate(picks):
        for j, (pair, mine) in enumerate(pick):
            at = pl.ds(pl.multiple_of((2 * pair + (core if mine else 1 - core)) * n, n), n)
            copies.append(pltpu.make_async_copy(tok.at[:, at], bufs.at[i, :, j * n : (j + 1) * n], sem.at[i, j]))
            copies[-1].start()
    for i, pick in enumerate(picks):
        for copy in copies[i * len(pick) : (i + 1) * len(pick)]:
            copy.wait()
        sends.append(pltpu.make_async_copy(bufs.at[i], outs[i], sem.at[i, 0]))
        sends[-1].start()
    for send in sends:
        send.wait()


def take_rows(picks, C, n, tok):
    width = len(picks[0]) * n
    return pl.pallas_call(
        functools.partial(take_kernel, picks, n),
        out_shape=[jax.ShapeDtypeStruct((C, width), bf16)] * len(picks),
        in_specs=[ANY],
        out_specs=[ANY] * len(picks),
        scratch_shapes=[
            pltpu.VMEM((len(picks), C, width), bf16),
            pltpu.SemaphoreType.DMA((len(picks), len(picks[0]))),
        ],
        compiler_params=pltpu.CompilerParams(vmem_limit_bytes=8 << 20),
        cost_estimate=pl.CostEstimate(flops=1, bytes_accessed=1, transcendentals=0),
        name="take",
    )(tok)


def pack_kernel(C, w, b, out, b_out):
    tail = C - LANES
    parts = [w[g, 0:LANES].astype(f32) for g in range(3)] + [w[g, LANES:C].astype(f32) for g in range(3)]
    parts.append(jnp.zeros((LANES - 3 * tail, w.shape[2]), f32))
    out[...] = jnp.concatenate(parts, 0).T.astype(bf16)
    b_out[...] = jnp.zeros_like(b_out)
    for g in range(3):
        b_out[0:1, g * LANES : (g + 1) * LANES] = b[g : g + 1, 0:LANES]
        b_out[0:1, 3 * LANES + g * tail : 3 * LANES + (g + 1) * tail] = b[g : g + 1, LANES:C]


def pack(C, w, b):
    return pl.pallas_call(
        functools.partial(pack_kernel, C),
        out_shape=[
            jax.ShapeDtypeStruct((w.shape[2], 4 * LANES), bf16),
            jax.ShapeDtypeStruct((SEGS, 4 * LANES), f32),
        ],
        in_specs=[VMEM] * 2,
        out_specs=[VMEM] * 2,
        compiler_params=pltpu.CompilerParams(vmem_limit_bytes=4 << 20),
        cost_estimate=pl.CostEstimate(flops=1, bytes_accessed=1, transcendentals=0),
        name="pack",
    )(w, b)


def finish_kernel(k, rows, mine, C, n, near, far, *refs):
    total, sem = refs[-2:]
    if mine:
        grad = refs[-3]
    else:
        grad, hid = refs[-4:-2]
    core = lax.axis_index("chan") & 1
    which = core if mine else 1 - core
    copies = []

    def go(src, out, r):
        at = pl.ds(pl.multiple_of((2 * (k * rows + r) + which) * n, n), n)
        copies.append(pltpu.make_async_copy(src, out.at[:, at], sem.at[len(copies)]))
        copies[-1].start()

    for r in range(rows):
        at = slice(r * n, (r + 1) * n)
        if not mine:
            go(near.at[C : 2 * C, at], hid, r)
        total[:, at] = (near[0:C, at].astype(f32) + far[:, at].astype(f32)).astype(bf16)
        go(total.at[:, at], grad, r)
    for copy in copies:
        copy.wait()


def finish(k, rows, mine, C, n, total, near, far, grad, hid=None):
    ins = [near, far]
    specs = [VMEM] * 2
    shape = jax.ShapeDtypeStruct((C, total), bf16)
    outs = [shape]
    alias = {}
    for v in (grad, hid):
        if v is not None:
            alias[len(ins)] = 0 if v is grad else 1
            ins.append(v)
            specs.append(ANY)
    if hid is not None:
        outs.append(shape)
    return pl.pallas_call(
        functools.partial(finish_kernel, k, rows, mine, C, n),
        out_shape=outs,
        in_specs=specs,
        out_specs=[ANY] * len(outs),
        scratch_shapes=[pltpu.VMEM((C, rows * n), bf16), pltpu.SemaphoreType.DMA((2 * rows,))],
        input_output_aliases=alias,
        compiler_params=pltpu.CompilerParams(vmem_limit_bytes=8 << 20),
        cost_estimate=pl.CostEstimate(flops=1, bytes_accessed=1, transcendentals=0),
        name="finish",
    )(*ins)


def in_two(v):
    high = v.astype(bf16)
    low = v - high.astype(f32)
    at = lax.broadcasted_iota(jnp.int32, (SEGS, v.shape[1]), 0)
    return jnp.where(at == 0, high.astype(f32), jnp.where(at == 1, low, 0.0)).astype(bf16)


def from_two(v):
    v = v[...].astype(f32)
    return v[0:1] + v[1:2]


def leaf_kernel(C, own, other, out, b_out):
    b = own[C : C + 1] + from_two(other[C:])
    out[0:C] = (own[0:C] + other[0:C].astype(f32)).astype(bf16)
    out[C:] = in_two(b)
    b_out[...] = jnp.broadcast_to(b, (SEGS, b.shape[1]))


def leaf(C, own, other):
    half = own.shape[1]
    return pl.pallas_call(
        functools.partial(leaf_kernel, C),
        out_shape=[jax.ShapeDtypeStruct((C + SEGS, half), bf16), jax.ShapeDtypeStruct((SEGS, half), f32)],
        in_specs=[VMEM] * 2,
        out_specs=[VMEM] * 2,
        compiler_params=pltpu.CompilerParams(vmem_limit_bytes=4 << 20),
        cost_estimate=pl.CostEstimate(flops=1, bytes_accessed=1, transcendentals=0),
        name="leaf",
    )(own, other)


def split_kernel(C, own, other, b, s3, s5, s2, k6, k1, k4, k0):
    two = in_two(b[0:1])
    for i, out in enumerate((s3, s5, s2, k6, k1, k4, k0)):
        at = slice(i * C, (i + 1) * C)
        v = own[at, :] + other[at, :].astype(f32)
        if i < 3:
            out[0:C] = v.astype(bf16)
            out[C:] = two
        else:
            out[0:C] = v
            out[C:] = b[...]


def split(C, own, other, b):
    half = own.shape[1]
    shape = (C + SEGS, half)
    return pl.pallas_call(
        functools.partial(split_kernel, C),
        out_shape=[jax.ShapeDtypeStruct(shape, bf16)] * 3 + [jax.ShapeDtypeStruct(shape, f32)] * 4,
        in_specs=[VMEM] * 3,
        out_specs=[VMEM] * 7,
        compiler_params=pltpu.CompilerParams(vmem_limit_bytes=16 << 20),
        cost_estimate=pl.CostEstimate(flops=1, bytes_accessed=1, transcendentals=0),
        name="split",
    )(own, other, b)


def pass_on_kernel(C, kept, *refs):
    out = refs[-1]
    v, b = kept[0:C], kept[C : C + 1]
    for r in refs[:-1]:
        v = v + r[0:C].astype(f32)
        b = b + from_two(r[C:])
    out[0:C] = v.astype(bf16)
    out[C:] = in_two(b)


def pass_on(C, kept, *received):
    return pl.pallas_call(
        functools.partial(pass_on_kernel, C),
        out_shape=jax.ShapeDtypeStruct(kept.shape, bf16),
        in_specs=[VMEM] * (1 + len(received)),
        out_specs=VMEM,
        compiler_params=pltpu.CompilerParams(vmem_limit_bytes=4 << 20),
        cost_estimate=pl.CostEstimate(flops=1, bytes_accessed=1, transcendentals=0),
        name="pass_on",
    )(kept, *received)


def total_kernel(C, k0, r2, r1, r4, grad, bias, buf, b_buf, sem):
    v = k0[0:C] + r2[0:C].astype(f32) + (r1[0:C].astype(f32) + r4[0:C].astype(f32))
    t = v.T
    tail = C - LANES
    b = k0[C : C + 1] + from_two(r2[C:]) + (from_two(r1[C:]) + from_two(r4[C:]))
    for g in range(3):
        buf[g, 0:LANES] = t[g * LANES : (g + 1) * LANES]
        buf[g, LANES:C] = t[3 * LANES + g * tail : 3 * LANES + (g + 1) * tail]
        b_buf[g : g + 1, 0:LANES] = b[:, g * LANES : (g + 1) * LANES]
        b_buf[g : g + 1, LANES:C] = b[:, 3 * LANES + g * tail : 3 * LANES + (g + 1) * tail]
    copies = [pltpu.make_async_copy(buf, grad, sem.at[0]), pltpu.make_async_copy(b_buf, bias, sem.at[1])]
    for copy in copies:
        copy.start()
    for copy in copies:
        copy.wait()


def total_sum(C, k0, r2, r1, r4):
    shapes = ((3, C, C), (3, C))
    return pl.pallas_call(
        functools.partial(total_kernel, C),
        out_shape=[jax.ShapeDtypeStruct(shape, f32) for shape in shapes],
        in_specs=[VMEM] * 4,
        out_specs=[HBM] * 2,
        scratch_shapes=[pltpu.VMEM(shape, f32) for shape in shapes] + [pltpu.SemaphoreType.DMA((2,))],
        compiler_params=pltpu.CompilerParams(vmem_limit_bytes=4 << 20),
        cost_estimate=pl.CostEstimate(flops=1, bytes_accessed=1, transcendentals=0),
        name="total",
    )(k0, r2, r1, r4)


def local(chan, parts, tokens, weights, bias, segment_ids, cotangent):
    C, total = tokens.shape
    n = LEN
    pairs = total // n // 2
    rows = pairs // CALLS
    me = lax.axis_index("chan")
    core = me & 1

    def chan_move(v, j):
        return lax.ppermute(v, "chan", [(i, i ^ j) for i in range(chan)])

    def dp_move(v, j):
        return lax.ppermute(v, "dp", [(i, i ^ j) for i in range(parts)])

    def after(v, *others):
        return lax.optimization_barrier((v,) + others)[0]

    ids = segment_ids.reshape(2 * pairs * SEGS, n // SEGS)
    def other_rows(k, tok):
        picks = [[(k * rows + r, mine) for r in range(rows)] for mine in (True, False)]
        return take_rows(picks, C, n, tok)

    to_near, to_far = other_rows(0, tokens)
    near, far = chan_move(to_near, 2), chan_move(to_far, 3)
    xs = [(near, far)]
    shard, b_own = pack(C, after(weights, to_near), bias)
    sib = chan_move(tokens, 1)
    scot = chan_move(cotangent, 1)
    g = {0: shard, 4: dp_move(shard, 4), 1: dp_move(shard, 1)}
    def to_sibling(group):
        return chan_move(jnp.concatenate([g[j] for j in group], 0), 1)

    g4, own = lax.optimization_barrier((g[4], shard, sib))[:2]
    g[6] = dp_move(g4, 2)
    g[5] = dp_move(g4, 1)
    w_sib = [to_sibling(GROUPS[0])]
    biases = [b_own, chan_move(after(b_own, far), 1)]
    g[2] = dp_move(own, 2)
    g6, g1 = lax.optimization_barrier((g[6], g[1], near, scot))[:2]
    g[7] = dp_move(g6, 1)
    g[3] = dp_move(g1, 2)
    w_sib.append(to_sibling(GROUPS[1]))
    w_sib.append(to_sibling(GROUPS[2]))
    w = [g[j] for j in range(parts)] + w_sib
    for k in range(1, CALLS):
        to_near, to_far = other_rows(k, after(tokens, g[6]))
        xs.append((chan_move(to_near, 2), chan_move(to_far, 3)))

    acc = hid = grad = None
    moved = []
    for k in range(CALLS):
        out = layer(k, CALLS, rows, parts, C, n, tokens, sib, cotangent, scot, ids, biases, xs[k], w, acc, hid)
        if k == 0:
            w = out[-1]
        hid, to_sib, d_px, d_pd, own, acc = out[:6]
        if k == CALLS - 1:
            own_first, own_rest, sib_first, sib_rest = out[5:9]
            got = [v for m in moved for v in m[1:]]
            to_sib, d_px, d_pd, sib_first, sib_rest = lax.optimization_barrier(
                (to_sib, d_px, d_pd, sib_first, sib_rest, *got)
            )[:5]
            sib_first, sib_rest = chan_move(sib_first, 1), chan_move(sib_rest, 1)
        else:
            to_sib, d_px, d_pd = lax.optimization_barrier((to_sib, d_px, d_pd, *xs[k + 1]))[:3]
        moved.append((own, chan_move(d_px, 2), chan_move(to_sib, 1), chan_move(d_pd, 3)))

    def end(k, mine, *others):
        nonlocal grad, hid
        own, from_px, from_sib, from_pd = moved[k]
        if mine:
            (grad,) = finish(k, rows, True, C, n, total, after(own, *others), from_px, grad)
        else:
            grad, hid = finish(k, rows, False, C, n, total, after(from_sib, *others), from_pd, grad, hid)

    s7, b = leaf(C, own_first, sib_first)
    r7 = dp_move(s7, 1)
    for k in range(CALLS - 1):
        end(k, True, s7)
    s3, s5, s2, k6, k1, k4, k0 = split(C, own_rest, after(sib_rest, moved[-1][2], grad), b)
    r3, r5 = dp_move(s3, 2), dp_move(s5, 1)
    s6 = pass_on(C, k6, r7)
    r6 = dp_move(s6, 2)
    for k in range(CALLS - 1):
        end(k, False, s6, r5)
    r1, r2 = dp_move(pass_on(C, k1, after(r3, grad)), 1), dp_move(after(s2, r3), 2)
    s4 = pass_on(C, k4, r5, after(r6, grad))
    r4 = dp_move(s4, 4)
    end(CALLS - 1, True, s4, r1)
    weight_grad, bias_grad = total_sum(C, k0, r2, r1, after(r4, grad))
    end(CALLS - 1, False, weight_grad)
    return (hid, grad, weight_grad, bias_grad)


def combine(earlier, later):
    return (earlier[0] * later[0], later[0] * earlier[1] + later[1])


def local_any(tokens, weights, bias, segment_ids, cotangent):
    width_part, total_rows = tokens.shape
    batch_rows = total_rows // MICRO
    grad_shard = jnp.zeros(weights.shape, jnp.float32)
    bias_total = jnp.zeros(bias.shape, jnp.float32)
    position = jnp.arange(batch_rows) % LEN
    hidden_parts = []
    input_parts = []
    for micro in range(MICRO):
        lower = micro * batch_rows
        upper = lower + batch_rows
        part_in = tokens[:, lower:upper]
        ids = segment_ids[lower:upper]
        cot = cotangent[:, lower:upper].astype(jnp.float32)
        before = jnp.concatenate([ids[:1], ids[:-1]], 0)
        carry_flag = (position > 0) & (ids == before)
        carry_on = jnp.where(carry_flag, 1.0, 0.0).astype(jnp.float32)
        gathered = lax.all_gather(part_in, "chan", axis=0, tiled=True)
        width = gathered.shape[0]
        shifted = jnp.concatenate([jnp.zeros((width, 1), jnp.bfloat16), gathered[:, :-1]], 1)
        previous = jnp.where(carry_flag[None, :], shifted, jnp.zeros((), jnp.bfloat16))
        joined_inputs = jnp.concatenate([gathered, previous], 0)
        preactivation = jnp.einsum(
            "gcr,rl->gcl",
            lax.all_gather(weights, "dp", axis=2, tiled=True),
            joined_inputs,
            preferred_element_type=jnp.float32,
        )
        preactivation = preactivation + bias[:, :, None]
        gate_z = jnp.tanh(preactivation[0])
        forget = jax.nn.sigmoid(preactivation[1])
        output_gate = jax.nn.sigmoid(preactivation[2])
        decay = forget * carry_on[None, :]
        source = (1.0 - forget) * gate_z
        cell = lax.associative_scan(combine, (decay, source), axis=1)[1]
        hidden_parts.append((output_gate * cell).astype(jnp.bfloat16))
        decay_next = jnp.concatenate([decay[:, 1:], jnp.zeros((width_part, 1), jnp.float32)], 1)
        dcell = lax.associative_scan(combine, (decay_next, cot * output_gate), reverse=True, axis=1)[1]
        cell_before = (
            jnp.concatenate([jnp.zeros((width_part, 1), jnp.float32), cell[:, :-1]], 1)
            * carry_on[None, :]
        )
        grad_z = dcell * (1.0 - forget) * (1.0 - gate_z * gate_z)
        grad_f = dcell * (cell_before - gate_z) * forget * (1.0 - forget)
        grad_o = cot * cell * output_gate * (1.0 - output_gate)
        dpre_low = jnp.stack([grad_z, grad_f, grad_o], 0).astype(jnp.bfloat16)
        bias_total = bias_total + jnp.sum(dpre_low.astype(jnp.float32), axis=2)
        weight_term = jnp.einsum(
            "gcl,rl->gcr", dpre_low, joined_inputs, preferred_element_type=jnp.float32
        )
        djoined = jnp.einsum(
            "gcl,gcr->rl",
            dpre_low,
            lax.all_gather(weights, "dp", axis=2, tiled=True),
            preferred_element_type=jnp.float32,
        )
        later = djoined[width:] * carry_on[None, :]
        later = jnp.concatenate([later[:, 1:], jnp.zeros((width, 1), jnp.float32)], 1)
        term = djoined[:width] + later
        input_parts.append(
            lax.psum_scatter(term, "chan", scatter_dimension=0, tiled=True).astype(jnp.bfloat16)
        )
        grad_shard = grad_shard + lax.psum_scatter(weight_term, "dp", scatter_dimension=2, tiled=True)
    bias_grad = lax.psum(bias_total, "dp")
    hidden = jnp.concatenate(hidden_parts, 1)
    input_grad = jnp.concatenate(input_parts, 1)
    return (hidden, input_grad, grad_shard, bias_grad)


def solution(mesh):
    chan, parts = mesh.shape["chan"], mesh.shape["dp"]
    in_specs = (P("chan", "dp"), P(None, "chan", "dp"), P(None, "chan"), P("dp"), P("chan", "dp"))
    out_specs = (P("chan", "dp"), P("chan", "dp"), P(None, "chan", "dp"), P(None, "chan"))

    def run(tokens, weights, bias, segment_ids, cotangent):
        C = tokens.shape[0] // chan
        row_part = weights.shape[2] // parts
        pairs = tokens.shape[1] // parts % (2 * LEN * CALLS) == 0
        tail = C - LANES
        fits = chan == 4 and parts == 8 and row_part == C and pairs and 0 < 3 * tail < LANES and tail % 32 == 0
        body = functools.partial(local, chan, parts) if fits else local_any
        return jax.shard_map(body, mesh=mesh, in_specs=in_specs, out_specs=out_specs, check_vma=False)(
            tokens, weights, bias, segment_ids, cotangent
        )

    return run
```
